512 devices in a mesh: dp: 16 (over y, core), space: 32 (over z, x).
Axes of the slice: x: 4, y: 8, z: 8, core: 2. Of those that a mesh axis runs over, the one named last changes fastest.
Arguments:
- latent: bfloat16 [16, 256, 64, 320], P('dp', 'space'), may hold values from -6 to 6
- first_weight: bfloat16 [320, 3, 3, 320], replicated, may hold values from -0.109375 to 0.109375
- second_weight: bfloat16 [320, 3, 3, 320], replicated, may hold values from -0.109375 to 0.109375
- cotangent: bfloat16 [16, 256, 64, 320], P('dp', 'space'), may hold values from -6 to 6
Outputs:
- output_map: bfloat16 [16, 256, 64, 320], P('dp', 'space')
- latent_grad: bfloat16 [16, 256, 64, 320], P('dp', 'space')
- first_grad: float32 [921600], P(('dp', 'space'))
- second_grad: float32 [921600], P(('dp', 'space'))
The draws below stay inside these ranges and needn't reach their ends.
All inputs are finite; a program needn't handle non-finite values.
Results may differ from the reference program's by a relative error of at most 0.017.
Values may be sent and summed in bfloat16 or wider, within the bound.
A program may use at most 128 MiB of HBM per device.

```python
import jax
import jax.numpy as jnp
from jax import lax

CIN = 320
CMID = 320
W = 64
BATCH = 16
H = 256


def with_spikes(entries, stream_key, source, target, shards_of, factor):
    def block_of(dim):
        return (jnp.arange(entries.shape[dim]) // (entries.shape[dim] // shards_of)).reshape((-1,) + (1,) * (entries.ndim - 1 - dim))

    one_side = jax.random.permutation(stream_key, shards_of)[block_of(target)]
    far = (block_of(target) + shards_of // 2) % shards_of
    return jnp.where((block_of(source) == one_side) | (block_of(source) == far), factor * entries, entries)


def shard_levels(own_key, shape, shards, low, high):
    loudness = 1.0
    for axis_at, shards_of in shards:
        heights = jax.random.uniform(jax.random.fold_in(jax.random.fold_in(own_key, 6), axis_at), (shards_of,), jnp.float32, low / len(shards), high / len(shards))
        loudness = loudness * jnp.repeat(jnp.exp(heights), shape[axis_at] // shards_of).reshape((-1,) + (1,) * (len(shape) - 1 - axis_at))
    return loudness


def scatter_about(key, extent, deviation, reach, shards=(), dtype=jnp.bfloat16):
    gain = shard_levels(key, extent, shards, -0.22, 0.18) if shards else 1.0
    result = jax.random.normal(key, extent, jnp.float32) * deviation * gain
    return jnp.minimum(jnp.maximum(result, -reach), reach).astype(dtype)


def gaussian_with(key, extent, width, limit, cuts, heavy, held_as=jnp.bfloat16):
    drawn = width * jax.random.normal(key, extent, jnp.float32)
    if cuts:
        drawn = drawn * shard_levels(key, extent, cuts, -0.22, 0.18)
    return jnp.clip(with_spikes(drawn, jax.random.fold_in(key, 3), *heavy), -limit, limit).astype(held_as)


def setup_inputs(seed: int = 0) -> dict:
    streams_of = jax.random.split(jax.random.key(seed), 5)
    return {
        "latent": gaussian_with(streams_of[0], (BATCH, H, W, CIN), 1.0, 6.0, ((0, 16), (1, 32)), (0, 3, 16, 2.0)),
        "first_weight": scatter_about(streams_of[1], (CIN, 3, 3, CMID), (9 * CIN) ** -0.5, 0.109375),
        "second_weight": scatter_about(streams_of[2], (CIN, 3, 3, CMID), (9 * CMID) ** -0.5, 0.109375),
        "cotangent": gaussian_with(streams_of[3], (BATCH, H, W, CIN), 1.0, 6.0, ((0, 16), (1, 32)), (0, 3, 16, 2.0)),
    }


def silu_value(value):
    return value * jax.nn.sigmoid(value)


def silu_slope(value):
    sig = jax.nn.sigmoid(value)
    return sig * (1.0 + value * (1.0 - sig))


def pad_both(field):
    return jnp.pad(field, ((1, 1), (1, 1), (0, 0)))


def conv_sum(padded, weight, row_count, col_count, flip, weight_dim):
    total = None
    for i in range(3):
        for j in range(3):
            start_row = 2 - i if flip else i
            start_col = 2 - j if flip else j
            piece = padded[start_row:start_row + row_count, start_col:start_col + col_count]
            piece = piece.reshape(row_count * col_count, padded.shape[2])
            term = lax.dot_general(piece, weight[:, i, j, :], (((1,), (weight_dim,)), ((), ())), preferred_element_type=jnp.float32)
            total = term if total is None else total + term
    return total


def weight_terms(padded, other, row_count, col_count, first):
    pieces = []
    for i in range(3):
        for j in range(3):
            piece = padded[i:i + row_count, j:j + col_count].reshape(row_count * col_count, padded.shape[2])
            if first:
                term = lax.dot_general(piece, other, (((0,), (0,)), ((), ())), preferred_element_type=jnp.float32)
            else:
                term = lax.dot_general(other, piece, (((0,), (0,)), ((), ())), preferred_element_type=jnp.float32)
            pieces.append(term)
    return jnp.concatenate(pieces, axis=1).reshape(-1)


def one_sample(sample, grad_out, first_weight, second_weight):
    row_count, col_count, chans = sample.shape
    mids = first_weight.shape[3]
    active = silu_value(sample.astype(jnp.float32)).astype(jnp.bfloat16)
    active_pad = pad_both(active)
    hidden = conv_sum(active_pad, first_weight, row_count, col_count, False, 0).astype(jnp.bfloat16)
    hidden_act = silu_value(hidden.astype(jnp.float32)).astype(jnp.bfloat16)
    hidden_pad = pad_both(hidden_act.reshape(row_count, col_count, mids))
    output_map = conv_sum(hidden_pad, second_weight, row_count, col_count, False, 1).astype(jnp.bfloat16)
    grad_flat = grad_out.reshape(row_count * col_count, chans)
    second_term = weight_terms(hidden_pad, grad_flat, row_count, col_count, False)
    hidden_back = conv_sum(pad_both(grad_out), second_weight, row_count, col_count, True, 0)
    hidden_grad = (hidden_back * silu_slope(hidden.astype(jnp.float32))).astype(jnp.bfloat16)
    first_term = weight_terms(active_pad, hidden_grad, row_count, col_count, True)
    active_back = conv_sum(pad_both(hidden_grad.reshape(row_count, col_count, mids)), first_weight, row_count, col_count, True, 1)
    latent_grad = (active_back * silu_slope(sample.reshape(row_count * col_count, chans).astype(jnp.float32))).astype(jnp.bfloat16)
    return output_map.reshape(row_count, col_count, chans), latent_grad.reshape(row_count, col_count, chans), first_term, second_term


def reference(latent, first_weight, second_weight, cotangent):
    def advance(carry, pair):
        made = one_sample(pair[0], pair[1], first_weight, second_weight)
        return (carry[0] + made[2], carry[1] + made[3]), (made[0], made[1])

    length = first_weight.shape[0] * 9 * first_weight.shape[3]
    start = (jnp.zeros((length,), jnp.float32), jnp.zeros((length,), jnp.float32))
    grads, maps = lax.scan(advance, start, (latent, cotangent))
    return maps[0], maps[1], grads[0], grads[1]
```

```python
import jax
import jax.numpy as jnp
from jax import lax
from jax.experimental import pallas as pl
from jax.experimental.pallas import tpu as pltpu
from jax.sharding import PartitionSpec as P

BF = jnp.bfloat16
F32 = jnp.float32
MESH = pl.DeviceIdType.MESH
COLS = 64
CH = 320
ROWS = 8
OWN = ROWS * COLS
EXT = (ROWS + 4) * COLS
MID = (ROWS + 2) * COLS
NT = (((1,), (1,)), ((), ()))
UNIT = 360
LANES = 384
UNITS = 40


def dot(a, b):
    return jnp.dot(a, b, preferred_element_type=F32)


def dot_nt(a, b):
    return lax.dot_general(a, b, NT, preferred_element_type=F32)


def column_shifts(value):
    count = value.shape[0]
    col = lax.broadcasted_iota(jnp.int32, value.shape, 0) % COLS
    before = jnp.where(col == 0, 0.0, pltpu.roll(value, 1, 0))
    after = jnp.where(col == COLS - 1, 0.0, pltpu.roll(value, count - 1, 0))
    return before.astype(BF), value.astype(BF), after.astype(BF)


def unit_pieces(u):
    pieces = []
    start, left, lane = UNIT * u, UNIT, 0
    while left:
        tap, col = divmod(start, 3 * CH)
        size = min(left, 3 * CH - col)
        pieces.append((tap, col, size, lane))
        start, left, lane = start + size, left - size, lane + size
    return pieces


def kernel(
    lat_hbm, w1_hbm, w2_hbm, cot_hbm, out_hbm, lg_hbm, g1_ref, g2_ref,
    latx, cotx, act, a3, c3, w1, w2, w1t, w2t, acc, slope, h3, hg3, terms, perm, lhs_t,
    grid, core_recv, zsum, zrecv, xs, xf, xr, sc, ys, yr, outv, lgv,
    load_sem, halo_send, halo_recv, core_send, core_rsem, zsend, zrsem, xsend, xrsem, ysend, yrsem, store_sem,
):
    dp, space = lax.axis_index("dp"), lax.axis_index("space")
    yy, core = dp // 2, dp % 2
    zz, xx = space // 4, space % 4
    up, down = (space + 31) % 32, (space + 1) % 32

    loads = [
        pltpu.make_async_copy(lat_hbm, latx.at[pl.ds(2 * COLS, OWN)], load_sem.at[0]),
        pltpu.make_async_copy(cot_hbm, cotx.at[pl.ds(2 * COLS, OWN)], load_sem.at[1]),
        pltpu.make_async_copy(w1_hbm, w1, load_sem.at[2]),
        pltpu.make_async_copy(w2_hbm, w2, load_sem.at[3]),
    ]
    for load in loads:
        load.start()

    peers = [(dp, up), (dp, down), (yy * 2 + 1 - core, space)]
    peers += [(dp, (zz + k) % 8 * 4 + xx) for k in (1, 7)]
    peers += [(dp, zz * 4 + (xx + k) % 4) for k in (1, 2, 3)]
    peers += [((yy + k) % 8 * 2 + core, space) for k in range(1, 8)]
    barrier = pltpu.get_barrier_semaphore()
    for peer in peers:
        pl.semaphore_signal(barrier, inc=1, device_id=peer, device_id_type=MESH)

    def widen(src, dst, first, last, flip, activate):
        def group(k, _):
            at = pl.ds(pl.multiple_of(k * COLS, COLS), COLS)
            value = src[at, :].astype(F32)
            if activate:
                value = value * jax.nn.sigmoid(value)
                act[at, :] = value.astype(BF)
            one, two, three = column_shifts(value)
            dst[at, :] = jnp.concatenate([three, two, one] if flip else [one, two, three], axis=1)
            return 0
        lax.fori_loop(first, last, group, 0)

    loads[0].wait()
    widen(latx, a3, 2, 10, False, True)
    loads[1].wait()
    widen(cotx, c3, 2, 10, True, False)

    pl.semaphore_wait(barrier, len(peers))
    halos = []
    for n, (src, dst) in enumerate(((lat_hbm, latx), (cot_hbm, cotx))):
        to_up = pltpu.make_async_remote_copy(
            src_ref=src.at[pl.ds(0, 2 * COLS)], dst_ref=dst.at[pl.ds(10 * COLS, 2 * COLS)],
            send_sem=halo_send.at[2 * n], recv_sem=halo_recv.at[2 * n],
            device_id=(dp, up), device_id_type=MESH)
        to_down = pltpu.make_async_remote_copy(
            src_ref=src.at[pl.ds(6 * COLS, 2 * COLS)], dst_ref=dst.at[pl.ds(0, 2 * COLS)],
            send_sem=halo_send.at[2 * n + 1], recv_sem=halo_recv.at[2 * n + 1],
            device_id=(dp, down), device_id_type=MESH)
        halos.append((to_up, to_down))

    @pl.when(space > 0)
    def _():
        for to_up, _d in halos:
            to_up.start()

    @pl.when(space < 31)
    def _():
        for _u, to_down in halos:
            to_down.start()

    shape = (CH, CH)
    row = lax.broadcasted_iota(jnp.int32, shape, 0)
    chan = lax.broadcasted_iota(jnp.int32, shape, 1)
    group = ((row % 8) * 2 + row // 32 % 2) * 4 + row // 8 % 4
    perm[...] = jnp.where(chan == 5 * group + row // 64, 1.0, 0.0).astype(BF)
    lhs_t[...] = dot_nt(perm[...], cotx[2 * COLS : 10 * COLS, :]).astype(BF)

    loads[2].wait()

    def conv_one(first, count):
        size = count * COLS
        total = dot(a3[first * COLS : first * COLS + size, :], w1[0])
        total += dot(a3[(first + 1) * COLS : (first + 1) * COLS + size, :], w1[1])
        total += dot(a3[(first + 2) * COLS : (first + 2) * COLS + size, :], w1[2])
        acc[first * COLS : first * COLS + size, :] = total

        def finish(k, _):
            at = pl.ds(pl.multiple_of(k * COLS, COLS), COLS)
            hidden = acc[at, :].astype(BF).astype(F32)
            sig = jax.nn.sigmoid(hidden)
            slope[at, :] = sig * (1.0 + hidden * (1.0 - sig))
            h3[at, :] = jnp.concatenate(column_shifts(hidden * sig), axis=1)
            return 0

        lax.fori_loop(first, first + count, finish, 0)

    conv_one(2, 6)

    @pl.when(space == 0)
    def _():
        latx[0 : 2 * COLS, :] = jnp.zeros((2 * COLS, CH), BF)
        cotx[0 : 2 * COLS, :] = jnp.zeros((2 * COLS, CH), BF)

    @pl.when(space == 31)
    def _():
        latx[10 * COLS :, :] = jnp.zeros((2 * COLS, CH), BF)
        cotx[10 * COLS :, :] = jnp.zeros((2 * COLS, CH), BF)

    @pl.when(space < 31)
    def _():
        for to_up, _d in halos:
            to_up.wait_recv()

    @pl.when(space > 0)
    def _():
        for _u, to_down in halos:
            to_down.wait_recv()

    for first in (0, 10):
        widen(latx, a3, first, first + 2, False, True)
        widen(cotx, c3, first, first + 2, True, False)
    conv_one(0, 2)
    conv_one(8, 2)

    def clear_outside(ref):
        @pl.when(space == 0)
        def _():
            ref[0:COLS, :] = jnp.zeros((COLS, 3 * CH), BF)

        @pl.when(space == 31)
        def _():
            ref[9 * COLS :, :] = jnp.zeros((COLS, 3 * CH), BF)

    clear_outside(h3)

    other = (yy * 2 + 1 - core, space)

    def core_copy(n, r):
        return pltpu.make_async_remote_copy(
            src_ref=grid.at[n, pl.ds(8 * r, 8), pl.ds(4 * (1 - core), 4)],
            dst_ref=core_recv.at[n, pl.ds(8 * r, 8)],
            send_sem=core_send.at[n, r], recv_sem=core_rsem.at[n, r],
            device_id=other, device_id_type=MESH)

    def pack_terms(n):
        lane = lax.broadcasted_iota(jnp.int32, (64, LANES), 1)
        for r in range(5):
            for u in range(8):
                value = None
                for tap, col, size, put in unit_pieces(u):
                    base = min(col // 128 * 128, 1024 - LANES)
                    width = -(-max(col - base + size, LANES) // 128) * 128
                    shift = (put - (col - base)) % width
                    piece = terms[tap, 64 * r : 64 * r + 64, base : base + width]
                    if shift:
                        piece = pltpu.roll(piece, shift, 1)
                    piece = piece[:, :LANES]
                    value = piece if value is None else jnp.where(lane < put, value, piece)
                grid[n, 8 * r + u] = value.reshape(8, 8, LANES).astype(BF)
            core_copy(n, r).start()

    def core_sum(n):
        for r in range(5):
            core_copy(n, r).wait_recv()
            for k in range(4):
                zsum[n, k, 8 * r : 8 * r + 8] = (
                    grid[n, 8 * r : 8 * r + 8, 4 * core + k].astype(F32)
                    + core_recv[n, 8 * r : 8 * r + 8, k].astype(F32)
                ).astype(BF)

    def block(n, target, lo, size):
        return zsum.at[n, target // 2, pl.ds(20 * (target % 2) + lo, size)]

    def zcopy(n, s, way):
        step = 1 if way == 0 else 7
        target = (zz + step * (5 - s)) % 8
        lo, size = (10 * way, 10) if s == 1 else (0, 20)
        return pltpu.make_async_remote_copy(
            src_ref=block(n, target, lo, size),
            dst_ref=zrecv.at[n, way, s - 1, pl.ds(lo, size)],
            send_sem=zsend.at[n, way, s - 1], recv_sem=zrsem.at[n, way, s - 1],
            device_id=(dp, (zz + step) % 8 * 4 + xx), device_id_type=MESH)

    def zstep(n, s):
        for way in range(2):
            if s >= 2:
                zcopy(n, s - 1, way).wait_recv()
                step = 1 if way == 0 else 7
                target = (zz + step * (5 - s)) % 8
                lo, size = (10 * way, 10) if s == 2 else (0, 20)
                ref = block(n, target, lo, size)
                got = zrecv[n, way, s - 2, lo : lo + size]
                ref[...] = (ref[...].astype(F32) + got.astype(F32)).astype(BF)
            zcopy(n, s, way).start()

    def xcopy(n, d):
        to = (xx + d) % 4
        return pltpu.make_async_remote_copy(
            src_ref=xs.at[n, pl.ds(5 * to, 5)], dst_ref=xr.at[n, d - 1],
            send_sem=xsend.at[n, d - 1], recv_sem=xrsem.at[n, d - 1],
            device_id=(dp, zz * 4 + to), device_id_type=MESH)

    def zfinal(n):
        for way in range(2):
            zcopy(n, 4, way).wait_recv()
        total = block(n, zz, 0, 20)[...].astype(F32) + zrecv[n, 0, 3].astype(F32) + zrecv[n, 1, 3].astype(F32)
        xf[n] = total
        xs[n] = total.astype(BF)
        for d in (1, 2, 3):
            xcopy(n, d).start()

    def ycopy(n, d):
        to = (yy + d) % 8
        return pltpu.make_async_remote_copy(
            src_ref=ys.at[n, to], dst_ref=yr.at[n, d - 1],
            send_sem=ysend.at[n, d - 1], recv_sem=yrsem.at[n, d - 1],
            device_id=(to * 2 + core, space), device_id_type=MESH)

    def xfinal(n):
        total = xf[n, pl.ds(5 * xx, 5)]
        for d in (1, 2, 3):
            xcopy(n, d).wait_recv()
            total += xr[n, d - 1].astype(F32)
        flat = total.reshape(5 * 8, LANES)
        for k in range(3):
            sc[n, k] = flat[:, 128 * k : 128 * k + 128]
        for to in range(8):
            for k in range(3):
                ys[n, to, 0:5, 128 * k : 128 * k + 128] = sc[n, k, pl.ds(to, 5, stride=8), :].astype(BF)
        for d in range(1, 8):
            ycopy(n, d).start()

    def yfinal(n, ref):
        total = ys[n, yy].astype(F32)
        for d in range(1, 8):
            ycopy(n, d).wait_recv()
            total += yr[n, d - 1].astype(F32)
        ref[...] = total

    ys[...] = jnp.zeros(ys.shape, BF)
    for i in range(3):
        terms[i, :, 3 * CH :] = jnp.zeros((CH, 64), F32)

    for i in range(3):
        terms[i, :, : 3 * CH] = dot(lhs_t[...], h3[i * COLS : i * COLS + OWN, :])
    pack_terms(1)

    loads[3].wait()
    total = dot(c3[2 * COLS : 2 * COLS + MID, :], w2[0])
    total += dot(c3[COLS : COLS + MID, :], w2[1])
    total += dot(c3[0:MID, :], w2[2])
    acc[...] = total

    def finish_back(k, _):
        at = pl.ds(pl.multiple_of(k * COLS, COLS), COLS)
        before, here, after = column_shifts(acc[at, :] * slope[at, :])
        hg3[at, :] = jnp.concatenate([after, here, before], axis=1)
        return 0

    lax.fori_loop(0, 10, finish_back, 0)
    clear_outside(hg3)

    core_sum(1)
    zstep(1, 1)

    for i in range(3):
        left = dot_nt(perm[...], act[(i + 1) * COLS : (i + 1) * COLS + OWN, :]).astype(BF)
        terms[i, :, : 3 * CH] = dot(left, hg3[COLS : COLS + OWN, :])
    zstep(1, 2)
    pack_terms(0)
    zstep(1, 3)

    for i in range(3):
        w2t[i] = jnp.concatenate([w2[i, CH * j : CH * j + CH, :] for j in range(3)], axis=1)
        w1t[i] = jnp.concatenate([w1[i, CH * j : CH * j + CH, :] for j in range(3)], axis=1)
    core_sum(0)
    zstep(0, 1)
    zstep(1, 4)

    total = dot_nt(h3[0:OWN, :], w2t[0])
    total += dot_nt(h3[COLS : COLS + OWN, :], w2t[1])
    total += dot_nt(h3[2 * COLS : 2 * COLS + OWN, :], w2t[2])
    outv[...] = total.astype(BF)
    store_out = pltpu.make_async_copy(outv, out_hbm, store_sem.at[0])
    store_out.start()
    zstep(0, 2)
    zfinal(1)

    total = dot_nt(hg3[2 * COLS : 2 * COLS + OWN, :], w1t[0])
    total += dot_nt(hg3[COLS : COLS + OWN, :], w1t[1])
    total += dot_nt(hg3[0:OWN, :], w1t[2])
    acc[0:OWN, :] = total
    zstep(0, 3)

    def finish_latent(k, _):
        at = pl.ds(pl.multiple_of(k * COLS, COLS), COLS)
        value = latx[pl.ds(pl.multiple_of((k + 2) * COLS, COLS), COLS), :].astype(F32)
        sig = jax.nn.sigmoid(value)
        lgv[at, :] = (acc[at, :] * (sig * (1.0 + value * (1.0 - sig)))).astype(BF)
        return 0

    lax.fori_loop(0, 8, finish_latent, 0)
    store_lg = pltpu.make_async_copy(lgv, lg_hbm, store_sem.at[1])
    store_lg.start()
    xfinal(1)
    zstep(0, 4)
    yfinal(1, g2_ref)
    zfinal(0)
    xfinal(0)
    yfinal(0, g1_ref)

    @pl.when(space > 0)
    def _():
        for to_up, _d in halos:
            to_up.wait_send()

    @pl.when(space < 31)
    def _():
        for _u, to_down in halos:
            to_down.wait_send()

    for n in range(2):
        for r in range(5):
            core_copy(n, r).wait_send()
        for s in range(1, 5):
            for way in range(2):
                zcopy(n, s, way).wait_send()
        for d in (1, 2, 3):
            xcopy(n, d).wait_send()
        for d in range(1, 8):
            ycopy(n, d).wait_send()
    store_out.wait()
    store_lg.wait()


def local(latent, first_weight, second_weight, cotangent):
    def taps(weight):
        return jnp.transpose(weight, (1, 2, 0, 3)).reshape(3, 3 * CH, CH)

    any_spec = pl.BlockSpec(memory_space=pl.ANY)
    vmem_spec = pl.BlockSpec(memory_space=pltpu.VMEM)
    dma = pltpu.SemaphoreType.DMA
    out, latent_grad, first, second = pl.pallas_call(
        kernel,
        out_shape=(
            jax.ShapeDtypeStruct((OWN, CH), BF),
            jax.ShapeDtypeStruct((OWN, CH), BF),
            jax.ShapeDtypeStruct((8, LANES), F32),
            jax.ShapeDtypeStruct((8, LANES), F32),
        ),
        in_specs=[any_spec] * 4,
        out_specs=(any_spec, any_spec, vmem_spec, vmem_spec),
        scratch_shapes=[
            pltpu.VMEM((EXT, CH), BF),
            pltpu.VMEM((EXT, CH), BF),
            pltpu.VMEM((EXT, CH), BF),
            pltpu.VMEM((EXT, 3 * CH), BF),
            pltpu.VMEM((EXT, 3 * CH), BF),
            pltpu.VMEM((3, 3 * CH, CH), BF),
            pltpu.VMEM((3, 3 * CH, CH), BF),
            pltpu.VMEM((3, CH, 3 * CH), BF),
            pltpu.VMEM((3, CH, 3 * CH), BF),
            pltpu.VMEM((MID, CH), F32),
            pltpu.VMEM((MID, CH), F32),
            pltpu.VMEM((MID, 3 * CH), BF),
            pltpu.VMEM((MID, 3 * CH), BF),
            pltpu.VMEM((3, CH, 1024), F32),
            pltpu.VMEM((CH, CH), BF),
            pltpu.VMEM((CH, OWN), BF),
            pltpu.VMEM((2, UNITS, 8, 8, LANES), BF),
            pltpu.VMEM((2, UNITS, 4, 8, LANES), BF),
            pltpu.VMEM((2, 4, UNITS, 8, LANES), BF),
            pltpu.VMEM((2, 2, 4, 20, 8, LANES), BF),
            pltpu.VMEM((2, 20, 8, LANES), BF),
            pltpu.VMEM((2, 20, 8, LANES), F32),
            pltpu.VMEM((2, 3, 5, 8, LANES), BF),
            pltpu.VMEM((2, 3, 40, 128), F32),
            pltpu.VMEM((2, 8, 8, LANES), BF),
            pltpu.VMEM((2, 7, 8, LANES), BF),
            pltpu.VMEM((OWN, CH), BF),
            pltpu.VMEM((OWN, CH), BF),
            dma((4,)),
            dma((4,)),
            dma((4,)),
            dma((2, 5)),
            dma((2, 5)),
            dma((2, 2, 4)),
            dma((2, 2, 4)),
            dma((2, 3)),
            dma((2, 3)),
            dma((2, 7)),
            dma((2, 7)),
            dma((2,)),
        ],
        compiler_params=pltpu.CompilerParams(
            collective_id=0, has_side_effects=True, vmem_limit_bytes=60 * 1024 * 1024
        ),
        name="conv_pair",
    )(
        latent.reshape(OWN, CH), taps(first_weight), taps(second_weight), cotangent.reshape(OWN, CH)
    )
    return (
        out.reshape(1, ROWS, COLS, CH),
        latent_grad.reshape(1, ROWS, COLS, CH),
        first[:5, :UNIT].reshape(-1),
        second[:5, :UNIT].reshape(-1),
    )


def solution(mesh):
    placed = (P("dp", "space", None, None), P(), P(), P("dp", "space", None, None))
    return jax.shard_map(
        local,
        mesh=mesh,
        in_specs=placed,
        out_specs=(
            P("dp", "space", None, None),
            P("dp", "space", None, None),
            P(("dp", "space")),
            P(("dp", "space")),
        ),
        check_vma=False,
    )
```

```python
import jax
import jax.numpy as jnp
from jax import lax
from jax.experimental import pallas as pl
from jax.experimental.pallas import tpu as pltpu
from jax.sharding import PartitionSpec as P

BF = jnp.bfloat16
F32 = jnp.float32
MESH = pl.DeviceIdType.MESH
COLS = 64
CH = 320
ROWS = 8
OWN = ROWS * COLS
EXT = (ROWS + 4) * COLS
MID = (ROWS + 2) * COLS
NT = (((1,), (1,)), ((), ()))
UNIT = 360
LANES = 384
UNITS = 40


def dot(a, b):
    return jnp.dot(a, b, preferred_element_type=F32)


def dot_nt(a, b):
    return lax.dot_general(a, b, NT, preferred_element_type=F32)


def column_shifts(value):
    count = value.shape[0]
    col = lax.broadcasted_iota(jnp.int32, value.shape, 0) % COLS
    before = jnp.where(col == 0, 0.0, pltpu.roll(value, 1, 0))
    after = jnp.where(col == COLS - 1, 0.0, pltpu.roll(value, count - 1, 0))
    return before.astype(BF), value.astype(BF), after.astype(BF)


def unit_pieces(u):
    pieces = []
    start, left, lane = UNIT * u, UNIT, 0
    while left:
        tap, col = divmod(start, 3 * CH)
        size = min(left, 3 * CH - col)
        pieces.append((tap, col, size, lane))
        start, left, lane = start + size, left - size, lane + size
    return pieces


def kernel(
    lat_hbm, w1_hbm, w2_hbm, cot_hbm, out_hbm, lg_hbm, g1_ref, g2_ref,
    latx, cotx, act, a3, c3, w1, w2, w1t, w2t, acc, slope, h3, hg3, terms, perm, lhs_t,
    grid, core_recv, sums, zrecv, xrecv, late, mids, midr, sc, ys, yr, outv, lgv,
    load_sem, halo_send, halo_recv, core_send, core_rsem, zsend, zrsem, lsend, lrsem, ysend, yrsem, store_sem,
):
    dp, space = lax.axis_index("dp"), lax.axis_index("space")
    yy, core = dp // 2, dp % 2
    zz, xx = space // 4, space % 4
    up, down = (space + 31) % 32, (space + 1) % 32

    loads = [
        pltpu.make_async_copy(lat_hbm, latx.at[pl.ds(2 * COLS, OWN)], load_sem.at[0]),
        pltpu.make_async_copy(cot_hbm, cotx.at[pl.ds(2 * COLS, OWN)], load_sem.at[1]),
        pltpu.make_async_copy(w1_hbm, w1, load_sem.at[2]),
        pltpu.make_async_copy(w2_hbm, w2, load_sem.at[3]),
    ]
    for load in loads:
        load.start()

    peers = [(dp, up), (dp, down), (yy * 2 + 1 - core, space)]
    peers += [(dp, (zz + k) % 8 * 4 + xx) for k in range(1, 8)]
    peers += [(dp, zz * 4 + (xx + k) % 4) for k in (1, 2, 3)]
    peers += [((yy + k) % 8 * 2 + core, space) for k in range(1, 8)]
    barrier = pltpu.get_barrier_semaphore()
    for peer in peers:
        pl.semaphore_signal(barrier, inc=1, device_id=peer, device_id_type=MESH)

    def widen(src, dst, first, last, flip, activate):
        def group(k, _):
            at = pl.ds(pl.multiple_of(k * COLS, COLS), COLS)
            value = src[at, :].astype(F32)
            if activate:
                value = value * jax.nn.sigmoid(value)
                act[at, :] = value.astype(BF)
            one, two, three = column_shifts(value)
            dst[at, :] = jnp.concatenate([three, two, one] if flip else [one, two, three], axis=1)
            return 0
        lax.fori_loop(first, last, group, 0)

    loads[0].wait()
    widen(latx, a3, 2, 10, False, True)
    loads[1].wait()
    widen(cotx, c3, 2, 10, True, False)

    pl.semaphore_wait(barrier, len(peers))
    halos = []
    for n, (src, dst) in enumerate(((lat_hbm, latx), (cot_hbm, cotx))):
        to_up = pltpu.make_async_remote_copy(
            src_ref=src.at[pl.ds(0, 2 * COLS)], dst_ref=dst.at[pl.ds(10 * COLS, 2 * COLS)],
            send_sem=halo_send.at[2 * n], recv_sem=halo_recv.at[2 * n],
            device_id=(dp, up), device_id_type=MESH)
        to_down = pltpu.make_async_remote_copy(
            src_ref=src.at[pl.ds(6 * COLS, 2 * COLS)], dst_ref=dst.at[pl.ds(0, 2 * COLS)],
            send_sem=halo_send.at[2 * n + 1], recv_sem=halo_recv.at[2 * n + 1],
            device_id=(dp, down), device_id_type=MESH)
        halos.append((to_up, to_down))

    @pl.when(space > 0)
    def _():
        for to_up, _d in halos:
            to_up.start()

    @pl.when(space < 31)
    def _():
        for _u, to_down in halos:
            to_down.start()

    shape = (CH, CH)
    row = lax.broadcasted_iota(jnp.int32, shape, 0)
    chan = lax.broadcasted_iota(jnp.int32, shape, 1)
    group = ((row % 8) * 2 + row // 32 % 2) * 4 + row // 8 % 4
    perm[...] = jnp.where(chan == 5 * group + row // 64, 1.0, 0.0).astype(BF)
    lhs_t[...] = dot_nt(perm[...], cotx[2 * COLS : 10 * COLS, :]).astype(BF)

    loads[2].wait()

    def conv_one(first, count):
        size = count * COLS
        total = dot(a3[first * COLS : first * COLS + size, :], w1[0])
        total += dot(a3[(first + 1) * COLS : (first + 1) * COLS + size, :], w1[1])
        total += dot(a3[(first + 2) * COLS : (first + 2) * COLS + size, :], w1[2])
        acc[first * COLS : first * COLS + size, :] = total

        def finish(k, _):
            at = pl.ds(pl.multiple_of(k * COLS, COLS), COLS)
            hidden = acc[at, :].astype(BF).astype(F32)
            sig = jax.nn.sigmoid(hidden)
            slope[at, :] = sig * (1.0 + hidden * (1.0 - sig))
            h3[at, :] = jnp.concatenate(column_shifts(hidden * sig), axis=1)
            return 0

        lax.fori_loop(first, first + count, finish, 0)

    conv_one(2, 6)

    @pl.when(space == 0)
    def _():
        latx[0 : 2 * COLS, :] = jnp.zeros((2 * COLS, CH), BF)
        cotx[0 : 2 * COLS, :] = jnp.zeros((2 * COLS, CH), BF)

    @pl.when(space == 31)
    def _():
        latx[10 * COLS :, :] = jnp.zeros((2 * COLS, CH), BF)
        cotx[10 * COLS :, :] = jnp.zeros((2 * COLS, CH), BF)

    @pl.when(space < 31)
    def _():
        for to_up, _d in halos:
            to_up.wait_recv()

    @pl.when(space > 0)
    def _():
        for _u, to_down in halos:
            to_down.wait_recv()

    for first in (0, 10):
        widen(latx, a3, first, first + 2, False, True)
        widen(cotx, c3, first, first + 2, True, False)
    conv_one(0, 2)
    conv_one(8, 2)

    def clear_outside(ref):
        @pl.when(space == 0)
        def _():
            ref[0:COLS, :] = jnp.zeros((COLS, 3 * CH), BF)

        @pl.when(space == 31)
        def _():
            ref[9 * COLS :, :] = jnp.zeros((COLS, 3 * CH), BF)

    clear_outside(h3)

    other = (yy * 2 + 1 - core, space)

    def core_copy(n, r):
        return pltpu.make_async_remote_copy(
            src_ref=grid.at[n, pl.ds(8 * r, 8), pl.ds(4 * (1 - core), 4)],
            dst_ref=core_recv.at[n, pl.ds(8 * r, 8)],
            send_sem=core_send.at[n, r], recv_sem=core_rsem.at[n, r],
            device_id=other, device_id_type=MESH)

    def pack_terms(n):
        lane = lax.broadcasted_iota(jnp.int32, (64, LANES), 1)
        for r in range(5):
            for u in range(8):
                value = None
                for tap, col, size, put in unit_pieces(u):
                    base = min(col // 128 * 128, 1024 - LANES)
                    width = -(-max(col - base + size, LANES) // 128) * 128
                    shift = (put - (col - base)) % width
                    piece = terms[tap, 64 * r : 64 * r + 64, base : base + width]
                    if shift:
                        piece = pltpu.roll(piece, shift, 1)
                    piece = piece[:, :LANES]
                    value = piece if value is None else jnp.where(lane < put, value, piece)
                grid[n, 8 * r + u] = value.reshape(8, 8, LANES).astype(BF)
            core_copy(n, r).start()

    def core_sum(n):
        for r in range(5):
            core_copy(n, r).wait_recv()
        for k in range(4):
            part = grid[n, :, 4 * core + k].astype(F32) + core_recv[n, :, k].astype(F32)
            sums[n, k] = part.reshape(2, 4, 5, 8, LANES).astype(BF)

    steps = (1, 7)

    def zblock(ref, n, target, way, half):
        lo, size = (2 * way, 2) if half else (0, 4)
        return ref.at[n, target // 2, target % 2, pl.ds(lo, size)]

    def zcopy(n, s, way):
        target = (zz + steps[way] * (5 - s)) % 8
        lo, size = (2 * way, 2) if s == 1 else (0, 4)
        return pltpu.make_async_remote_copy(
            src_ref=zblock(sums, n, target, way, s == 1),
            dst_ref=zrecv.at[n, way, s - 1, pl.ds(lo, size)],
            send_sem=zsend.at[n, way, s - 1], recv_sem=zrsem.at[n, way, s - 1],
            device_id=(dp, (zz + steps[way]) % 8 * 4 + xx), device_id_type=MESH)

    def zstep(n, s):
        for way in range(2):
            if s >= 2:
                zcopy(n, s - 1, way).wait_recv()
                ref = zblock(sums, n, (zz + steps[way] * (5 - s)) % 8, way, s == 2)
                lo, size = (2 * way, 2) if s == 2 else (0, 4)
                ref[...] = (ref[...].astype(F32) + zrecv[n, way, s - 2, lo : lo + size].astype(F32)).astype(BF)
            zcopy(n, s, way).start()

    def xcopy(n, s, way):
        target = (xx + (1 if way == 0 else 3) * (3 - s)) % 4
        lo, size = (2 * way, 2) if s == 1 else (0, 4)
        return pltpu.make_async_remote_copy(
            src_ref=sums.at[n, pl.ds(lo, size), :, target],
            dst_ref=xrecv.at[n, way, s - 1, pl.ds(lo, size)],
            send_sem=zsend.at[n, way, s - 1], recv_sem=zrsem.at[n, way, s - 1],
            device_id=(dp, zz * 4 + (xx + (1 if way == 0 else 3)) % 4), device_id_type=MESH)

    def xstep(n, s):
        for way in range(2):
            if s == 2:
                xcopy(n, 1, way).wait_recv()
                lo = 2 * way
                ref = sums.at[n, pl.ds(lo, 2), :, (xx + (1 if way == 0 else 3)) % 4]
                ref[...] = (ref[...].astype(F32) + xrecv[n, way, 0, lo : lo + 2].astype(F32)).astype(BF)
            xcopy(n, s, way).start()

    def x_direct(n, d):
        to = (xx + d) % 4
        return pltpu.make_async_remote_copy(
            src_ref=sums.at[n, zz // 2, zz % 2, to], dst_ref=late.at[n, d - 1],
            send_sem=lsend.at[n, d - 1], recv_sem=lrsem.at[n, d - 1],
            device_id=(dp, zz * 4 + to), device_id_type=MESH)

    def y_direct(n, d):
        to = (yy + d) % 8
        return pltpu.make_async_remote_copy(
            src_ref=mids.at[n, to], dst_ref=midr.at[n, d - 1],
            send_sem=lsend.at[n, d - 1], recv_sem=lrsem.at[n, d - 1],
            device_id=(to * 2 + core, space), device_id_type=MESH)

    def zfinal(n):
        for way in range(2):
            zcopy(n, 4, way).wait_recv()
        ref = sums.at[n, zz // 2, zz % 2]
        ref[...] = (ref[...].astype(F32) + zrecv[n, 0, 3].astype(F32) + zrecv[n, 1, 3].astype(F32)).astype(BF)
        for d in range(1, 4):
            x_direct(n, d).start()

    def xfinal(n):
        for way in range(2):
            xcopy(n, 2, way).wait_recv()
        total = sums[n, :, :, xx].astype(F32) + xrecv[n, 0, 1].astype(F32) + xrecv[n, 1, 1].astype(F32)
        flat = total.reshape(40 * 8, LANES)
        for k in range(3):
            sc[k] = flat[:, 128 * k : 128 * k + 128]
        for to in range(8):
            for k in range(3):
                mids[n, to, :, 128 * k : 128 * k + 128] = sc[k, pl.ds(to, 40, stride=8), :].astype(BF)
        for d in range(1, 8):
            y_direct(n, d).start()

    def last_copy(n, d, over_y):
        if over_y:
            to = (yy + d) % 8
            device = (to * 2 + core, space)
        else:
            to = (zz + d) % 8
            device = (dp, to * 4 + xx)
        return pltpu.make_async_remote_copy(
            src_ref=ys.at[n, to], dst_ref=yr.at[n, d - 1],
            send_sem=ysend.at[n, d - 1], recv_sem=yrsem.at[n, d - 1],
            device_id=device, device_id_type=MESH)

    def x_finish(n):
        total = sums[n, zz // 2, zz % 2, xx].astype(F32)
        for d in range(1, 4):
            x_direct(n, d).wait_recv()
            total += late[n, d - 1].astype(F32)
        flat = total.reshape(5 * 8, LANES)
        for k in range(3):
            sc[k, 0:40] = flat[:, 128 * k : 128 * k + 128]
        for to in range(8):
            for k in range(3):
                ys[n, to, 0:5, 128 * k : 128 * k + 128] = sc[k, pl.ds(to, 5, stride=8), :].astype(BF)
        for d in range(1, 8):
            last_copy(n, d, True).start()

    def y_finish(n):
        total = mids[n, yy].astype(F32)
        for d in range(1, 8):
            y_direct(n, d).wait_recv()
            total += midr[n, d - 1].astype(F32)
        for k in range(3):
            sc[k, 0:40] = total[:, 128 * k : 128 * k + 128]
        for to in range(8):
            for k in range(3):
                ys[n, to, 0:5, 128 * k : 128 * k + 128] = sc[k, 5 * to : 5 * to + 5, :].astype(BF)
        for d in range(1, 8):
            last_copy(n, d, False).start()

    def last(n, ref):
        def total_over(over_y):
            total = ys[n, yy if over_y else zz].astype(F32)
            for d in range(1, 8):
                last_copy(n, d, over_y).wait_recv()
                total += yr[n, d - 1].astype(F32)
            ref[...] = total

        @pl.when(core == 0)
        def _():
            total_over(True)

        @pl.when(core == 1)
        def _():
            total_over(False)

    def advance(n, step):
        @pl.when(core == 0)
        def _():
            if step <= 4:
                zstep(n, step)
            elif step == 5:
                zfinal(n)
            else:
                x_finish(n)

        if step in (1, 2, 3, 5):
            @pl.when(core == 1)
            def _():
                if step <= 2:
                    xstep(n, step)
                elif step == 3:
                    xfinal(n)
                else:
                    y_finish(n)

    ys[...] = jnp.zeros(ys.shape, BF)
    for i in range(3):
        terms[i, :, 3 * CH :] = jnp.zeros((CH, 64), F32)

    for i in range(3):
        terms[i, :, : 3 * CH] = dot(lhs_t[...], h3[i * COLS : i * COLS + OWN, :])
    pack_terms(1)

    loads[3].wait()
    total = dot(c3[2 * COLS : 2 * COLS + MID, :], w2[0])
    total += dot(c3[COLS : COLS + MID, :], w2[1])
    total += dot(c3[0:MID, :], w2[2])
    acc[...] = total

    def finish_back(k, _):
        at = pl.ds(pl.multiple_of(k * COLS, COLS), COLS)
        before, here, after = column_shifts(acc[at, :] * slope[at, :])
        hg3[at, :] = jnp.concatenate([after, here, before], axis=1)
        return 0

    lax.fori_loop(0, 10, finish_back, 0)
    clear_outside(hg3)

    core_sum(1)
    advance(1, 1)

    for i in range(3):
        left = dot_nt(perm[...], act[(i + 1) * COLS : (i + 1) * COLS + OWN, :]).astype(BF)
        terms[i, :, : 3 * CH] = dot(left, hg3[COLS : COLS + OWN, :])
    pack_terms(0)
    advance(1, 2)

    for i in range(3):
        w2t[i] = jnp.concatenate([w2[i, CH * j : CH * j + CH, :] for j in range(3)], axis=1)
        w1t[i] = jnp.concatenate([w1[i, CH * j : CH * j + CH, :] for j in range(3)], axis=1)
    core_sum(0)
    advance(0, 1)
    advance(1, 3)

    total = dot_nt(h3[0:OWN, :], w2t[0])
    total += dot_nt(h3[COLS : COLS + OWN, :], w2t[1])
    total += dot_nt(h3[2 * COLS : 2 * COLS + OWN, :], w2t[2])
    outv[...] = total.astype(BF)
    store_out = pltpu.make_async_copy(outv, out_hbm, store_sem.at[0])
    store_out.start()
    advance(0, 2)
    advance(1, 4)

    total = dot_nt(hg3[2 * COLS : 2 * COLS + OWN, :], w1t[0])
    total += dot_nt(hg3[COLS : COLS + OWN, :], w1t[1])
    total += dot_nt(hg3[0:OWN, :], w1t[2])
    acc[0:OWN, :] = total
    advance(0, 3)
    advance(1, 5)

    def finish_latent(k, _):
        at = pl.ds(pl.multiple_of(k * COLS, COLS), COLS)
        value = latx[pl.ds(pl.multiple_of((k + 2) * COLS, COLS), COLS), :].astype(F32)
        sig = jax.nn.sigmoid(value)
        lgv[at, :] = (acc[at, :] * (sig * (1.0 + value * (1.0 - sig)))).astype(BF)
        return 0

    lax.fori_loop(0, 8, finish_latent, 0)
    store_lg = pltpu.make_async_copy(lgv, lg_hbm, store_sem.at[1])
    store_lg.start()
    advance(0, 4)
    advance(1, 6)
    advance(0, 5)
    advance(0, 6)
    last(1, g2_ref)
    last(0, g1_ref)

    @pl.when(space > 0)
    def _():
        for to_up, _d in halos:
            to_up.wait_send()

    @pl.when(space < 31)
    def _():
        for _u, to_down in halos:
            to_down.wait_send()

    for n in range(2):
        for r in range(5):
            core_copy(n, r).wait_send()

    @pl.when(core == 0)
    def _():
        for n in range(2):
            for way in range(2):
                for s in range(1, 5):
                    zcopy(n, s, way).wait_send()
            for d in range(1, 4):
                x_direct(n, d).wait_send()
            for d in range(1, 8):
                last_copy(n, d, True).wait_send()

    @pl.when(core == 1)
    def _():
        for n in range(2):
            for way in range(2):
                for s in range(1, 3):
                    xcopy(n, s, way).wait_send()
            for d in range(1, 8):
                y_direct(n, d).wait_send()
                last_copy(n, d, False).wait_send()

    store_out.wait()
    store_lg.wait()


def finish_kernel(out_hbm, lg_hbm, g1_ref, g2_ref, out_res, lg_res, f1_ref, f2_ref, buf, sem_in, sem_out):
    takes, puts = [], []
    for n, (src, dst) in enumerate(((out_hbm, out_res), (lg_hbm, lg_res))):
        for k in range(2):
            at = pl.ds(k * OWN // 2, OWN // 2)
            takes.append(pltpu.make_async_copy(src.at[at], buf.at[n, at], sem_in.at[n, k]))
            puts.append(pltpu.make_async_copy(buf.at[n, at], dst.at[at], sem_out.at[n, k]))
    for take in takes:
        take.start()
    for take, put in zip(takes, puts):
        take.wait()
        put.start()
    lane = lax.broadcasted_iota(jnp.int32, (1, 128), 1)
    for src, dst in ((g1_ref, f1_ref), (g2_ref, f2_ref)):
        for k in range(15):
            start, end = 128 * k, min(128 * k + 128, 5 * UNIT)
            size, value, at = end - start, None, start
            while at < end:
                row, col = divmod(at, UNIT)
                base = min(col // 128 * 128, LANES - 256)
                piece = src[row : row + 1, base : base + 256]
                shift = (at - start - (col - base)) % 256
                if shift:
                    piece = pltpu.roll(piece, shift, 1)
                piece = piece[:, :128]
                value = piece if value is None else jnp.where(lane < at - start, value, piece)
                at += min(UNIT - col, end - at)
            dst[pl.ds(start, size)] = value[0, :size]
    for put in puts:
        put.wait()


def local(latent, first_weight, second_weight, cotangent):
    def taps(weight):
        return jnp.transpose(weight, (1, 2, 0, 3)).reshape(3, 3 * CH, CH)

    any_spec = pl.BlockSpec(memory_space=pl.ANY)
    vmem_spec = pl.BlockSpec(memory_space=pltpu.VMEM)
    dma = pltpu.SemaphoreType.DMA
    out, latent_grad, first, second = pl.pallas_call(
        kernel,
        out_shape=(
            jax.ShapeDtypeStruct((OWN, CH), BF),
            jax.ShapeDtypeStruct((OWN, CH), BF),
            jax.ShapeDtypeStruct((8, LANES), F32),
            jax.ShapeDtypeStruct((8, LANES), F32),
        ),
        in_specs=[any_spec] * 4,
        out_specs=(any_spec, any_spec, vmem_spec, vmem_spec),
        scratch_shapes=[
            pltpu.VMEM((EXT, CH), BF),
            pltpu.VMEM((EXT, CH), BF),
            pltpu.VMEM((EXT, CH), BF),
            pltpu.VMEM((EXT, 3 * CH), BF),
            pltpu.VMEM((EXT, 3 * CH), BF),
            pltpu.VMEM((3, 3 * CH, CH), BF),
            pltpu.VMEM((3, 3 * CH, CH), BF),
            pltpu.VMEM((3, CH, 3 * CH), BF),
            pltpu.VMEM((3, CH, 3 * CH), BF),
            pltpu.VMEM((MID, CH), F32),
            pltpu.VMEM((MID, CH), F32),
            pltpu.VMEM((MID, 3 * CH), BF),
            pltpu.VMEM((MID, 3 * CH), BF),
            pltpu.VMEM((3, CH, 1024), F32),
            pltpu.VMEM((CH, CH), BF),
            pltpu.VMEM((CH, OWN), BF),
            pltpu.VMEM((2, UNITS, 8, 8, LANES), BF),
            pltpu.VMEM((2, UNITS, 4, 8, LANES), BF),
            pltpu.VMEM((2, 4, 2, 4, 5, 8, LANES), BF),
            pltpu.VMEM((2, 2, 4, 4, 5, 8, LANES), BF),
            pltpu.VMEM((2, 2, 2, 4, 2, 5, 8, LANES), BF),
            pltpu.VMEM((2, 3, 5, 8, LANES), BF),
            pltpu.VMEM((2, 8, 40, LANES), BF),
            pltpu.VMEM((2, 7, 40, LANES), BF),
            pltpu.VMEM((3, 320, 128), F32),
            pltpu.VMEM((2, 8, 8, LANES), BF),
            pltpu.VMEM((2, 7, 8, LANES), BF),
            pltpu.VMEM((OWN, CH), BF),
            pltpu.VMEM((OWN, CH), BF),
            dma((4,)),
            dma((4,)),
            dma((4,)),
            dma((2, 5)),
            dma((2, 5)),
            dma((2, 2, 4)),
            dma((2, 2, 4)),
            dma((2, 7)),
            dma((2, 7)),
            dma((2, 7)),
            dma((2, 7)),
            dma((2,)),
        ],
        compiler_params=pltpu.CompilerParams(
            collective_id=0, has_side_effects=True, vmem_limit_bytes=60 * 1024 * 1024
        ),
        name="conv_pair",
    )(
        latent.reshape(OWN, CH), taps(first_weight), taps(second_weight), cotangent.reshape(OWN, CH)
    )
    out, latent_grad, first, second = pl.pallas_call(
        finish_kernel,
        out_shape=(
            jax.ShapeDtypeStruct((OWN, CH), BF),
            jax.ShapeDtypeStruct((OWN, CH), BF),
            jax.ShapeDtypeStruct((5 * UNIT,), F32),
            jax.ShapeDtypeStruct((5 * UNIT,), F32),
        ),
        in_specs=[any_spec, any_spec, vmem_spec, vmem_spec],
        out_specs=(any_spec, any_spec, vmem_spec, vmem_spec),
        scratch_shapes=[pltpu.VMEM((2, OWN, CH), BF), dma((2, 2)), dma((2, 2))],
        name="finish",
    )(out, latent_grad, first, second)
    return (
        out.reshape(1, ROWS, COLS, CH),
        latent_grad.reshape(1, ROWS, COLS, CH),
        first,
        second,
    )


def solution(mesh):
    placed = (P("dp", "space", None, None), P(), P(), P("dp", "space", None, None))
    return jax.shard_map(
        local,
        mesh=mesh,
        in_specs=placed,
        out_specs=(
            P("dp", "space", None, None),
            P("dp", "space", None, None),
            P(("dp", "space")),
            P(("dp", "space")),
        ),
        check_vma=False,
    )
```

```python
import jax
import jax.numpy as jnp
from jax import lax
from jax.experimental import pallas as pl
from jax.experimental.pallas import tpu as pltpu
from jax.sharding import PartitionSpec as P

BF = jnp.bfloat16
F32 = jnp.float32
MESH = pl.DeviceIdType.MESH
COLS = 64
CH = 320
ROWS = 8
OWN = ROWS * COLS
EXT = (ROWS + 4) * COLS
MID = (ROWS + 2) * COLS
NT = (((1,), (1,)), ((), ()))
UNIT = 360
LANES = 384
UNITS = 40


def dot(a, b):
    return jnp.dot(a, b, preferred_element_type=F32)


def dot_nt(a, b):
    return lax.dot_general(a, b, NT, preferred_element_type=F32)


def column_shifts(value):
    count = value.shape[0]
    col = lax.broadcasted_iota(jnp.int32, value.shape, 0) % COLS
    before = jnp.where(col == 0, 0.0, pltpu.roll(value, 1, 0))
    after = jnp.where(col == COLS - 1, 0.0, pltpu.roll(value, count - 1, 0))
    return before.astype(BF), value.astype(BF), after.astype(BF)


def unit_pieces(u):
    pieces = []
    start, left, lane = UNIT * u, UNIT, 0
    while left:
        tap, col = divmod(start, 3 * CH)
        size = min(left, 3 * CH - col)
        pieces.append((tap, col, size, lane))
        start, left, lane = start + size, left - size, lane + size
    return pieces


def kernel(
    lat_hbm, w1_hbm, w2_hbm, cot_hbm, out_hbm, lg_hbm, g1_ref, g2_ref,
    latx, cotx, act, a3, c3, w1, w2, w1t, w2t, acc, slope, h3, hg3, terms, perm, lhs_t,
    grid, core_recv, sums, xrecv, late, mids, midr, sc, ys, yr, outv, lgv,
    load_sem, halo_send, halo_recv, core_send, core_rsem, xsend, xrsem, lsend, lrsem, ysend, yrsem, store_sem,
):
    dp, space = lax.axis_index("dp"), lax.axis_index("space")
    yy, core = dp // 2, dp % 2
    zz, xx = space // 4, space % 4
    up, down = (space + 31) % 32, (space + 1) % 32

    loads = [
        pltpu.make_async_copy(lat_hbm, latx.at[pl.ds(2 * COLS, OWN)], load_sem.at[0]),
        pltpu.make_async_copy(cot_hbm, cotx.at[pl.ds(2 * COLS, OWN)], load_sem.at[1]),
        pltpu.make_async_copy(w1_hbm, w1, load_sem.at[2]),
        pltpu.make_async_copy(w2_hbm, w2, load_sem.at[3]),
    ]
    for load in loads:
        load.start()

    peers = [(dp, up), (dp, down), (yy * 2 + 1 - core, space)]
    peers += [(dp, (zz + k) % 8 * 4 + xx) for k in range(1, 8)]
    peers += [(dp, zz * 4 + (xx + k) % 4) for k in (1, 2, 3)]
    peers += [((yy + k) % 8 * 2 + core, space) for k in range(1, 8)]
    barrier = pltpu.get_barrier_semaphore()
    for peer in peers:
        pl.semaphore_signal(barrier, inc=1, device_id=peer, device_id_type=MESH)

    def widen(src, dst, first, last, flip, activate):
        def group(k, _):
            at = pl.ds(pl.multiple_of(k * COLS, COLS), COLS)
            value = src[at, :].astype(F32)
            if activate:
                value = value * jax.nn.sigmoid(value)
                act[at, :] = value.astype(BF)
            one, two, three = column_shifts(value)
            dst[at, :] = jnp.concatenate([three, two, one] if flip else [one, two, three], axis=1)
            return 0
        lax.fori_loop(first, last, group, 0)

    loads[0].wait()
    widen(latx, a3, 2, 10, False, True)
    loads[1].wait()
    widen(cotx, c3, 2, 10, True, False)

    pl.semaphore_wait(barrier, len(peers))
    halos = []
    for n, (src, dst) in enumerate(((lat_hbm, latx), (cot_hbm, cotx))):
        to_up = pltpu.make_async_remote_copy(
            src_ref=src.at[pl.ds(0, 2 * COLS)], dst_ref=dst.at[pl.ds(10 * COLS, 2 * COLS)],
            send_sem=halo_send.at[2 * n], recv_sem=halo_recv.at[2 * n],
            device_id=(dp, up), device_id_type=MESH)
        to_down = pltpu.make_async_remote_copy(
            src_ref=src.at[pl.ds(6 * COLS, 2 * COLS)], dst_ref=dst.at[pl.ds(0, 2 * COLS)],
            send_sem=halo_send.at[2 * n + 1], recv_sem=halo_recv.at[2 * n + 1],
            device_id=(dp, down), device_id_type=MESH)
        halos.append((to_up, to_down))

    @pl.when(space > 0)
    def _():
        for to_up, _d in halos:
            to_up.start()

    @pl.when(space < 31)
    def _():
        for _u, to_down in halos:
            to_down.start()

    shape = (CH, CH)
    row = lax.broadcasted_iota(jnp.int32, shape, 0)
    chan = lax.broadcasted_iota(jnp.int32, shape, 1)
    group = ((row % 8) * 2 + row // 32 % 2) * 4 + row // 8 % 4
    perm[...] = jnp.where(chan == 5 * group + row // 64, 1.0, 0.0).astype(BF)
    lhs_t[...] = dot_nt(perm[...], cotx[2 * COLS : 10 * COLS, :]).astype(BF)

    loads[2].wait()

    def conv_one(runs):
        def rows(i):
            parts = [a3[(first + i) * COLS : (first + count + i) * COLS, :] for first, count in runs]
            return parts[0] if len(parts) == 1 else jnp.concatenate(parts, axis=0)

        total = dot(rows(0), w1[0])
        total += dot(rows(1), w1[1])
        total += dot(rows(2), w1[2])
        at = 0
        for first, count in runs:
            acc[first * COLS : (first + count) * COLS, :] = total[at : at + count * COLS]
            at += count * COLS

        def finish(k, _):
            at = pl.ds(pl.multiple_of(k * COLS, COLS), COLS)
            hidden = acc[at, :].astype(BF).astype(F32)
            sig = jax.nn.sigmoid(hidden)
            slope[at, :] = sig * (1.0 + hidden * (1.0 - sig))
            h3[at, :] = jnp.concatenate(column_shifts(hidden * sig), axis=1)
            return 0

        for first, count in runs:
            lax.fori_loop(first, first + count, finish, 0)

    conv_one([(2, 6)])

    @pl.when(space == 0)
    def _():
        latx[0 : 2 * COLS, :] = jnp.zeros((2 * COLS, CH), BF)
        cotx[0 : 2 * COLS, :] = jnp.zeros((2 * COLS, CH), BF)

    @pl.when(space == 31)
    def _():
        latx[10 * COLS :, :] = jnp.zeros((2 * COLS, CH), BF)
        cotx[10 * COLS :, :] = jnp.zeros((2 * COLS, CH), BF)

    @pl.when(space < 31)
    def _():
        for to_up, _d in halos:
            to_up.wait_recv()

    @pl.when(space > 0)
    def _():
        for _u, to_down in halos:
            to_down.wait_recv()

    for first in (0, 10):
        widen(latx, a3, first, first + 2, False, True)
        widen(cotx, c3, first, first + 2, True, False)
    conv_one([(0, 2), (8, 2)])

    def clear_outside(ref):
        @pl.when(space == 0)
        def _():
            ref[0:COLS, :] = jnp.zeros((COLS, 3 * CH), BF)

        @pl.when(space == 31)
        def _():
            ref[9 * COLS :, :] = jnp.zeros((COLS, 3 * CH), BF)

    clear_outside(h3)

    other = (yy * 2 + 1 - core, space)

    def core_copy(n, r):
        return pltpu.make_async_remote_copy(
            src_ref=grid.at[n, pl.ds(8 * r, 8), pl.ds(4 * (1 - core), 4)],
            dst_ref=core_recv.at[n, pl.ds(8 * r, 8)],
            send_sem=core_send.at[n, r], recv_sem=core_rsem.at[n, r],
            device_id=other, device_id_type=MESH)

    def pack_terms(n):
        lane = lax.broadcasted_iota(jnp.int32, (64, LANES), 1)
        for r in range(5):
            for u in range(8):
                value = None
                for tap, col, size, put in unit_pieces(u):
                    base = min(col // 128 * 128, 1024 - LANES)
                    width = -(-max(col - base + size, LANES) // 128) * 128
                    shift = (put - (col - base)) % width
                    piece = terms[tap, 64 * r : 64 * r + 64, base : base + width]
                    if shift:
                        piece = pltpu.roll(piece, shift, 1)
                    piece = piece[:, :LANES]
                    value = piece if value is None else jnp.where(lane < put, value, piece)
                grid[n, 8 * r + u] = value.reshape(8, 8, LANES).astype(BF)
            core_copy(n, r).start()

    def core_sum(n):
        for r in range(5):
            core_copy(n, r).wait_recv()
        for k in range(4):
            part = grid[n, :, 4 * core + k].astype(F32) + core_recv[n, :, k].astype(F32)
            sums[n, k] = part.reshape(2, 4, 5, 8, LANES).astype(BF)

    def xcopy(n, part, way):
        step = 1 if way == 0 else 3
        target = (xx + (2 * step if part == 1 else step)) % 4
        lo = 2 * way if part < 3 else 2 - 2 * way
        return pltpu.make_async_remote_copy(
            src_ref=sums.at[n, pl.ds(lo, 2), :, target],
            dst_ref=xrecv.at[n, way, min(part, 2) - 1, pl.ds(lo, 2)],
            send_sem=xsend.at[n, way, part - 1], recv_sem=xrsem.at[n, way, part - 1],
            device_id=(dp, zz * 4 + (xx + step) % 4), device_id_type=MESH)

    def xstart(n):
        for part in (1, 3):
            for way in range(2):
                xcopy(n, part, way).start()

    def xstep(n):
        for way in range(2):
            xcopy(n, 1, way).wait_recv()
            lo = 2 * way
            ref = sums.at[n, pl.ds(lo, 2), :, (xx + (1 if way == 0 else 3)) % 4]
            ref[...] = (ref[...].astype(F32) + xrecv[n, way, 0, lo : lo + 2].astype(F32)).astype(BF)
            xcopy(n, 2, way).start()

    def z_direct(n, d):
        to = (zz + d) % 8
        return pltpu.make_async_remote_copy(
            src_ref=sums.at[n, to // 2, to % 2, xx], dst_ref=late.at[n, d - 1],
            send_sem=lsend.at[n, d - 1], recv_sem=lrsem.at[n, d - 1],
            device_id=(dp, to * 4 + xx), device_id_type=MESH)

    def y_direct(n, d):
        to = (yy + d) % 8
        return pltpu.make_async_remote_copy(
            src_ref=mids.at[n, to], dst_ref=midr.at[n, d - 1],
            send_sem=lsend.at[n, d - 1], recv_sem=lrsem.at[n, d - 1],
            device_id=(to * 2 + core, space), device_id_type=MESH)

    def xfinal(n):
        for way in range(2):
            for part in (2, 3):
                xcopy(n, part, way).wait_recv()

        @pl.when(core == 0)
        def _():
            ref = sums.at[n, :, :, xx]
            ref[...] = (ref[...].astype(F32) + xrecv[n, 0, 1].astype(F32) + xrecv[n, 1, 1].astype(F32)).astype(BF)
            for d in range(1, 8):
                z_direct(n, d).start()

        @pl.when(core == 1)
        def _():
            total = sums[n, :, :, xx].astype(F32) + xrecv[n, 0, 1].astype(F32) + xrecv[n, 1, 1].astype(F32)
            flat = total.reshape(40 * 8, LANES)
            for k in range(3):
                sc[k] = flat[:, 128 * k : 128 * k + 128]
            for to in range(8):
                for k in range(3):
                    mids[n, to, :, 128 * k : 128 * k + 128] = sc[k, pl.ds(to, 40, stride=8), :].astype(BF)
            for d in range(1, 8):
                y_direct(n, d).start()

    def last_copy(n, d, over_y):
        if over_y:
            to = (yy + d) % 8
            device = (to * 2 + core, space)
        else:
            to = (zz + d) % 8
            device = (dp, to * 4 + xx)
        return pltpu.make_async_remote_copy(
            src_ref=ys.at[n, to], dst_ref=yr.at[n, d - 1],
            send_sem=ysend.at[n, d - 1], recv_sem=yrsem.at[n, d - 1],
            device_id=device, device_id_type=MESH)

    def z_finish(n):
        total = sums[n, zz // 2, zz % 2, xx].astype(F32)
        for d in range(1, 8):
            z_direct(n, d).wait_recv()
            total += late[n, d - 1].astype(F32)
        flat = total.reshape(5 * 8, LANES)
        for k in range(3):
            sc[k, 0:40] = flat[:, 128 * k : 128 * k + 128]
        for to in range(8):
            for k in range(3):
                ys[n, to, 0:5, 128 * k : 128 * k + 128] = sc[k, pl.ds(to, 5, stride=8), :].astype(BF)
        for d in range(1, 8):
            last_copy(n, d, True).start()

    def y_finish(n):
        total = mids[n, yy].astype(F32)
        for d in range(1, 8):
            y_direct(n, d).wait_recv()
            total += midr[n, d - 1].astype(F32)
        for k in range(3):
            sc[k, 0:40] = total[:, 128 * k : 128 * k + 128]
        for to in range(8):
            for k in range(3):
                ys[n, to, 0:5, 128 * k : 128 * k + 128] = sc[k, 5 * to : 5 * to + 5, :].astype(BF)
        for d in range(1, 8):
            last_copy(n, d, False).start()

    def last(n, ref):
        def total_over(over_y):
            total = ys[n, yy if over_y else zz].astype(F32)
            for d in range(1, 8):
                last_copy(n, d, over_y).wait_recv()
                total += yr[n, d - 1].astype(F32)
            ref[...] = total

        @pl.when(core == 0)
        def _():
            total_over(True)

        @pl.when(core == 1)
        def _():
            total_over(False)

    def middle(n):
        @pl.when(core == 0)
        def _():
            z_finish(n)

        @pl.when(core == 1)
        def _():
            y_finish(n)

    ys[...] = jnp.zeros(ys.shape, BF)
    for i in range(3):
        terms[i, :, 3 * CH :] = jnp.zeros((CH, 64), F32)

    for i in range(3):
        terms[i, :, : 3 * CH] = dot(lhs_t[...], h3[i * COLS : i * COLS + OWN, :])
    pack_terms(1)

    loads[3].wait()
    total = dot(c3[2 * COLS : 2 * COLS + MID, :], w2[0])
    total += dot(c3[COLS : COLS + MID, :], w2[1])
    total += dot(c3[0:MID, :], w2[2])
    acc[...] = total

    def finish_back(k, _):
        at = pl.ds(pl.multiple_of(k * COLS, COLS), COLS)
        before, here, after = column_shifts(acc[at, :] * slope[at, :])
        hg3[at, :] = jnp.concatenate([after, here, before], axis=1)
        return 0

    lax.fori_loop(0, 10, finish_back, 0)
    clear_outside(hg3)

    core_sum(1)
    xstart(1)

    for i in range(3):
        left = dot_nt(perm[...], act[(i + 1) * COLS : (i + 1) * COLS + OWN, :]).astype(BF)
        terms[i, :, : 3 * CH] = dot(left, hg3[COLS : COLS + OWN, :])
    pack_terms(0)
    xstep(1)

    for i in range(3):
        w2t[i] = jnp.concatenate([w2[i, CH * j : CH * j + CH, :] for j in range(3)], axis=1)
        w1t[i] = jnp.concatenate([w1[i, CH * j : CH * j + CH, :] for j in range(3)], axis=1)
    core_sum(0)
    xstart(0)

    total = dot_nt(h3[0:OWN, :], w2t[0])
    total += dot_nt(h3[COLS : COLS + OWN, :], w2t[1])
    total += dot_nt(h3[2 * COLS : 2 * COLS + OWN, :], w2t[2])
    outv[...] = total.astype(BF)
    store_out = pltpu.make_async_copy(outv, out_hbm, store_sem.at[0])
    store_out.start()
    xfinal(1)
    xstep(0)

    total = dot_nt(hg3[2 * COLS : 2 * COLS + OWN, :], w1t[0])
    total += dot_nt(hg3[COLS : COLS + OWN, :], w1t[1])
    total += dot_nt(hg3[0:OWN, :], w1t[2])
    acc[0:OWN, :] = total

    def finish_latent(k, _):
        at = pl.ds(pl.multiple_of(k * COLS, COLS), COLS)
        value = latx[pl.ds(pl.multiple_of((k + 2) * COLS, COLS), COLS), :].astype(F32)
        sig = jax.nn.sigmoid(value)
        lgv[at, :] = (acc[at, :] * (sig * (1.0 + value * (1.0 - sig)))).astype(BF)
        return 0

    lax.fori_loop(0, 8, finish_latent, 0)
    store_lg = pltpu.make_async_copy(lgv, lg_hbm, store_sem.at[1])
    store_lg.start()
    middle(1)
    xfinal(0)

    @pl.when(space > 0)
    def _():
        for to_up, _d in halos:
            to_up.wait_send()

    @pl.when(space < 31)
    def _():
        for _u, to_down in halos:
            to_down.wait_send()

    for n in range(2):
        for r in range(5):
            core_copy(n, r).wait_send()
        for way in range(2):
            for part in (1, 2, 3):
                xcopy(n, part, way).wait_send()
    store_out.wait()
    store_lg.wait()
    middle(0)

    def sent(copy):
        for n in range(2):
            for d in range(1, 8):
                copy(n, d).wait_send()

    @pl.when(core == 0)
    def _():
        sent(z_direct)

    @pl.when(core == 1)
    def _():
        sent(y_direct)

    last(1, g2_ref)
    last(0, g1_ref)

    @pl.when(core == 0)
    def _():
        sent(lambda n, d: last_copy(n, d, True))

    @pl.when(core == 1)
    def _():
        sent(lambda n, d: last_copy(n, d, False))


def finish_kernel(out_hbm, lg_hbm, g1_ref, g2_ref, out_res, lg_res, f1_ref, f2_ref, buf, sem_in, sem_out):
    takes, puts = [], []
    for n, (src, dst) in enumerate(((out_hbm, out_res), (lg_hbm, lg_res))):
        for k in range(2):
            at = pl.ds(k * OWN // 2, OWN // 2)
            takes.append(pltpu.make_async_copy(src.at[at], buf.at[n, at], sem_in.at[n, k]))
            puts.append(pltpu.make_async_copy(buf.at[n, at], dst.at[at], sem_out.at[n, k]))
    for take in takes:
        take.start()
    for take, put in zip(takes, puts):
        take.wait()
        put.start()
    lane = lax.broadcasted_iota(jnp.int32, (1, 128), 1)
    for src, dst in ((g1_ref, f1_ref), (g2_ref, f2_ref)):
        for k in range(15):
            start, end = 128 * k, min(128 * k + 128, 5 * UNIT)
            size, value, at = end - start, None, start
            while at < end:
                row, col = divmod(at, UNIT)
                base = min(col // 128 * 128, LANES - 256)
                piece = src[row : row + 1, base : base + 256]
                shift = (at - start - (col - base)) % 256
                if shift:
                    piece = pltpu.roll(piece, shift, 1)
                piece = piece[:, :128]
                value = piece if value is None else jnp.where(lane < at - start, value, piece)
                at += min(UNIT - col, end - at)
            dst[pl.ds(start, size)] = value[0, :size]
    for put in puts:
        put.wait()


def local(latent, first_weight, second_weight, cotangent):
    def taps(weight):
        return jnp.transpose(weight, (1, 2, 0, 3)).reshape(3, 3 * CH, CH)

    any_spec = pl.BlockSpec(memory_space=pl.ANY)
    vmem_spec = pl.BlockSpec(memory_space=pltpu.VMEM)
    dma = pltpu.SemaphoreType.DMA
    out, latent_grad, first, second = pl.pallas_call(
        kernel,
        out_shape=(
            jax.ShapeDtypeStruct((OWN, CH), BF),
            jax.ShapeDtypeStruct((OWN, CH), BF),
            jax.ShapeDtypeStruct((8, LANES), F32),
            jax.ShapeDtypeStruct((8, LANES), F32),
        ),
        in_specs=[any_spec] * 4,
        out_specs=(any_spec, any_spec, vmem_spec, vmem_spec),
        scratch_shapes=[
            pltpu.VMEM((EXT, CH), BF),
            pltpu.VMEM((EXT, CH), BF),
            pltpu.VMEM((EXT, CH), BF),
            pltpu.VMEM((EXT, 3 * CH), BF),
            pltpu.VMEM((EXT, 3 * CH), BF),
            pltpu.VMEM((3, 3 * CH, CH), BF),
            pltpu.VMEM((3, 3 * CH, CH), BF),
            pltpu.VMEM((3, CH, 3 * CH), BF),
            pltpu.VMEM((3, CH, 3 * CH), BF),
            pltpu.VMEM((MID, CH), F32),
            pltpu.VMEM((MID, CH), F32),
            pltpu.VMEM((MID, 3 * CH), BF),
            pltpu.VMEM((MID, 3 * CH), BF),
            pltpu.VMEM((3, CH, 1024), F32),
            pltpu.VMEM((CH, CH), BF),
            pltpu.VMEM((CH, OWN), BF),
            pltpu.VMEM((2, UNITS, 8, 8, LANES), BF),
            pltpu.VMEM((2, UNITS, 4, 8, LANES), BF),
            pltpu.VMEM((2, 4, 2, 4, 5, 8, LANES), BF),
            pltpu.VMEM((2, 2, 2, 4, 2, 5, 8, LANES), BF),
            pltpu.VMEM((2, 7, 5, 8, LANES), BF),
            pltpu.VMEM((2, 8, 40, LANES), BF),
            pltpu.VMEM((2, 7, 40, LANES), BF),
            pltpu.VMEM((3, 320, 128), F32),
            pltpu.VMEM((2, 8, 8, LANES), BF),
            pltpu.VMEM((2, 7, 8, LANES), BF),
            pltpu.VMEM((OWN, CH), BF),
            pltpu.VMEM((OWN, CH), BF),
            dma((4,)),
            dma((4,)),
            dma((4,)),
            dma((2, 5)),
            dma((2, 5)),
            dma((2, 2, 3)),
            dma((2, 2, 3)),
            dma((2, 7)),
            dma((2, 7)),
            dma((2, 7)),
            dma((2, 7)),
            dma((2,)),
        ],
        compiler_params=pltpu.CompilerParams(
            collective_id=0, has_side_effects=True, vmem_limit_bytes=60 * 1024 * 1024
        ),
        name="conv_pair",
    )(
        latent.reshape(OWN, CH), taps(first_weight), taps(second_weight), cotangent.reshape(OWN, CH)
    )
    out, latent_grad, first, second = pl.pallas_call(
        finish_kernel,
        out_shape=(
            jax.ShapeDtypeStruct((OWN, CH), BF),
            jax.ShapeDtypeStruct((OWN, CH), BF),
            jax.ShapeDtypeStruct((5 * UNIT,), F32),
            jax.ShapeDtypeStruct((5 * UNIT,), F32),
        ),
        in_specs=[any_spec, any_spec, vmem_spec, vmem_spec],
        out_specs=(any_spec, any_spec, vmem_spec, vmem_spec),
        scratch_shapes=[pltpu.VMEM((2, OWN, CH), BF), dma((2, 2)), dma((2, 2))],
        name="finish",
    )(out, latent_grad, first, second)
    return (
        out.reshape(1, ROWS, COLS, CH),
        latent_grad.reshape(1, ROWS, COLS, CH),
        first,
        second,
    )


def solution(mesh):
    placed = (P("dp", "space", None, None), P(), P(), P("dp", "space", None, None))
    return jax.shard_map(
        local,
        mesh=mesh,
        in_specs=placed,
        out_specs=(
            P("dp", "space", None, None),
            P("dp", "space", None, None),
            P(("dp", "space")),
            P(("dp", "space")),
        ),
        check_vma=False,
    )
```

```python
import jax
import jax.numpy as jnp
from jax import lax
from jax.experimental import pallas as pl
from jax.experimental.pallas import tpu as pltpu
from jax.sharding import PartitionSpec as P

BF = jnp.bfloat16
F32 = jnp.float32
MESH = pl.DeviceIdType.MESH
COLS = 64
CH = 320
ROWS = 8
OWN = ROWS * COLS
EXT = (ROWS + 4) * COLS
MID = (ROWS + 2) * COLS
NT = (((1,), (1,)), ((), ()))
UNIT = 360
LANES = 384
UNITS = 40


def dot(a, b):
    return jnp.dot(a, b, preferred_element_type=F32)


def dot_nt(a, b):
    return lax.dot_general(a, b, NT, preferred_element_type=F32)


def column_shifts(value):
    count = value.shape[0]
    col = lax.broadcasted_iota(jnp.int32, value.shape, 0) % COLS
    before = jnp.where(col == 0, 0.0, pltpu.roll(value, 1, 0))
    after = jnp.where(col == COLS - 1, 0.0, pltpu.roll(value, count - 1, 0))
    return before.astype(BF), value.astype(BF), after.astype(BF)


def unit_pieces(u):
    pieces = []
    start, left, lane = UNIT * u, UNIT, 0
    while left:
        tap, col = divmod(start, 3 * CH)
        size = min(left, 3 * CH - col)
        pieces.append((tap, col, size, lane))
        start, left, lane = start + size, left - size, lane + size
    return pieces


def kernel(
    lat_hbm, w1_hbm, w2_hbm, cot_hbm, out_hbm, lg_hbm, g1_ref, g2_ref,
    latx, cotx, act, a3, c3, w1, w2, w1t, w2t, acc, slope, h3, hg3, terms, perm, lhs_t, mid_t,
    grid, core_recv, sums, xrecv, late, mids, midr, sc, ys, yr, outv, lgv,
    load_sem, halo_send, halo_recv, core_send, core_rsem, xsend, xrsem, lsend, lrsem, ysend, yrsem, store_sem,
):
    dp, space = lax.axis_index("dp"), lax.axis_index("space")
    yy, core = dp // 2, dp % 2
    zz, xx = space // 4, space % 4
    up, down = (space + 31) % 32, (space + 1) % 32

    loads = [
        pltpu.make_async_copy(lat_hbm, latx.at[pl.ds(2 * COLS, OWN)], load_sem.at[0]),
        pltpu.make_async_copy(cot_hbm, cotx.at[pl.ds(2 * COLS, OWN)], load_sem.at[1]),
        pltpu.make_async_copy(w1_hbm, w1, load_sem.at[2]),
        pltpu.make_async_copy(w2_hbm, w2, load_sem.at[3]),
    ]
    for load in loads:
        load.start()

    peers = [(dp, up), (dp, down), (yy * 2 + 1 - core, space)]
    peers += [(dp, (zz + k) % 8 * 4 + xx) for k in range(1, 8)]
    peers += [(dp, zz * 4 + (xx + k) % 4) for k in (1, 2, 3)]
    peers += [((yy + k) % 8 * 2 + core, space) for k in range(1, 8)]
    barrier = pltpu.get_barrier_semaphore()
    for peer in peers:
        pl.semaphore_signal(barrier, inc=1, device_id=peer, device_id_type=MESH)

    def widen(src, dst, first, last, flip, activate):
        def group(k, _):
            at = pl.ds(pl.multiple_of(k * COLS, COLS), COLS)
            value = src[at, :].astype(F32)
            if activate:
                value = value * jax.nn.sigmoid(value)
                act[at, :] = value.astype(BF)
            one, two, three = column_shifts(value)
            dst[at, :] = jnp.concatenate([three, two, one] if flip else [one, two, three], axis=1)
            return 0
        lax.fori_loop(first, last, group, 0)

    loads[0].wait()
    widen(latx, a3, 2, 10, False, True)
    loads[1].wait()
    widen(cotx, c3, 2, 10, True, False)

    pl.semaphore_wait(barrier, len(peers))
    halos = []
    for n, (src, dst) in enumerate(((lat_hbm, latx), (cot_hbm, cotx))):
        to_up = pltpu.make_async_remote_copy(
            src_ref=src.at[pl.ds(0, 2 * COLS)], dst_ref=dst.at[pl.ds(10 * COLS, 2 * COLS)],
            send_sem=halo_send.at[2 * n], recv_sem=halo_recv.at[2 * n],
            device_id=(dp, up), device_id_type=MESH)
        to_down = pltpu.make_async_remote_copy(
            src_ref=src.at[pl.ds(6 * COLS, 2 * COLS)], dst_ref=dst.at[pl.ds(0, 2 * COLS)],
            send_sem=halo_send.at[2 * n + 1], recv_sem=halo_recv.at[2 * n + 1],
            device_id=(dp, down), device_id_type=MESH)
        halos.append((to_up, to_down))

    @pl.when(space > 0)
    def _():
        for to_up, _d in halos:
            to_up.start()

    @pl.when(space < 31)
    def _():
        for _u, to_down in halos:
            to_down.start()

    shape = (CH, CH)
    row = lax.broadcasted_iota(jnp.int32, shape, 0)
    chan = lax.broadcasted_iota(jnp.int32, shape, 1)
    group = ((row % 8) * 2 + row // 32 % 2) * 4 + row // 8 % 4
    perm[...] = jnp.where(chan == 5 * group + row // 64, 1.0, 0.0).astype(BF)
    lhs_t[...] = dot_nt(perm[...], cotx[2 * COLS : 10 * COLS, :]).astype(BF)
    mid_t[...] = dot_nt(perm[...], act[2 * COLS : 10 * COLS, :]).astype(BF)

    loads[2].wait()

    def conv_one(runs):
        def rows(i):
            parts = [a3[(first + i) * COLS : (first + count + i) * COLS, :] for first, count in runs]
            return parts[0] if len(parts) == 1 else jnp.concatenate(parts, axis=0)

        total = dot(rows(0), w1[0])
        total += dot(rows(1), w1[1])
        total += dot(rows(2), w1[2])
        at = 0
        for first, count in runs:
            acc[first * COLS : (first + count) * COLS, :] = total[at : at + count * COLS]
            at += count * COLS

        def finish(k, _):
            at = pl.ds(pl.multiple_of(k * COLS, COLS), COLS)
            hidden = acc[at, :].astype(BF).astype(F32)
            sig = jax.nn.sigmoid(hidden)
            slope[at, :] = sig * (1.0 + hidden * (1.0 - sig))
            h3[at, :] = jnp.concatenate(column_shifts(hidden * sig), axis=1)
            return 0

        for first, count in runs:
            lax.fori_loop(first, first + count, finish, 0)

    conv_one([(2, 6)])

    @pl.when(space == 0)
    def _():
        latx[0 : 2 * COLS, :] = jnp.zeros((2 * COLS, CH), BF)
        cotx[0 : 2 * COLS, :] = jnp.zeros((2 * COLS, CH), BF)

    @pl.when(space == 31)
    def _():
        latx[10 * COLS :, :] = jnp.zeros((2 * COLS, CH), BF)
        cotx[10 * COLS :, :] = jnp.zeros((2 * COLS, CH), BF)

    @pl.when(space < 31)
    def _():
        for to_up, _d in halos:
            to_up.wait_recv()

    @pl.when(space > 0)
    def _():
        for _u, to_down in halos:
            to_down.wait_recv()

    for first in (0, 10):
        widen(latx, a3, first, first + 2, False, True)
        widen(cotx, c3, first, first + 2, True, False)
    conv_one([(0, 2), (8, 2)])

    def clear_outside(ref):
        @pl.when(space == 0)
        def _():
            ref[0:COLS, :] = jnp.zeros((COLS, 3 * CH), BF)

        @pl.when(space == 31)
        def _():
            ref[9 * COLS :, :] = jnp.zeros((COLS, 3 * CH), BF)

    clear_outside(h3)

    other = (yy * 2 + 1 - core, space)

    def core_copy(n, r):
        return pltpu.make_async_remote_copy(
            src_ref=grid.at[n, pl.ds(8 * r, 8), pl.ds(4 * (1 - core), 4)],
            dst_ref=core_recv.at[n, pl.ds(8 * r, 8)],
            send_sem=core_send.at[n, r], recv_sem=core_rsem.at[n, r],
            device_id=other, device_id_type=MESH)

    def pack_terms(n):
        lane = lax.broadcasted_iota(jnp.int32, (64, LANES), 1)
        for r in range(5):
            for u in range(8):
                value = None
                for tap, col, size, put in unit_pieces(u):
                    base = min(col // 128 * 128, 1024 - LANES)
                    width = -(-max(col - base + size, LANES) // 128) * 128
                    shift = (put - (col - base)) % width
                    piece = terms[tap, 64 * r : 64 * r + 64, base : base + width]
                    if shift:
                        piece = pltpu.roll(piece, shift, 1)
                    piece = piece[:, :LANES]
                    value = piece if value is None else jnp.where(lane < put, value, piece)
                grid[n, 8 * r + u] = value.reshape(8, 8, LANES).astype(BF)
            core_copy(n, r).start()

    def core_sum(n):
        for r in range(5):
            core_copy(n, r).wait_recv()
        for k in range(4):
            part = grid[n, :, 4 * core + k].astype(F32) + core_recv[n, :, k].astype(F32)
            sums[n, k] = part.reshape(2, 4, 5, 8, LANES).astype(BF)

    def xcopy(n, part, way):
        step = 1 if way == 0 else 3
        target = (xx + (2 * step if part == 1 else step)) % 4
        lo = 2 * way if part < 3 else 2 - 2 * way
        return pltpu.make_async_remote_copy(
            src_ref=sums.at[n, pl.ds(lo, 2), :, target],
            dst_ref=xrecv.at[n, way, min(part, 2) - 1, pl.ds(lo, 2)],
            send_sem=xsend.at[n, way, part - 1], recv_sem=xrsem.at[n, way, part - 1],
            device_id=(dp, zz * 4 + (xx + step) % 4), device_id_type=MESH)

    def xstart(n):
        for part in (1, 3):
            for way in range(2):
                xcopy(n, part, way).start()

    def xstep(n):
        for way in range(2):
            xcopy(n, 1, way).wait_recv()
            lo = 2 * way
            ref = sums.at[n, pl.ds(lo, 2), :, (xx + (1 if way == 0 else 3)) % 4]
            ref[...] = (ref[...].astype(F32) + xrecv[n, way, 0, lo : lo + 2].astype(F32)).astype(BF)
            xcopy(n, 2, way).start()

    def z_direct(n, d):
        to = (zz + d) % 8
        return pltpu.make_async_remote_copy(
            src_ref=sums.at[n, to // 2, to % 2, xx], dst_ref=late.at[n, d - 1],
            send_sem=lsend.at[n, d - 1], recv_sem=lrsem.at[n, d - 1],
            device_id=(dp, to * 4 + xx), device_id_type=MESH)

    def y_direct(n, d):
        to = (yy + d) % 8
        return pltpu.make_async_remote_copy(
            src_ref=mids.at[n, to], dst_ref=midr.at[n, d - 1],
            send_sem=lsend.at[n, d - 1], recv_sem=lrsem.at[n, d - 1],
            device_id=(to * 2 + core, space), device_id_type=MESH)

    def xfinal(n):
        for way in range(2):
            for part in (2, 3):
                xcopy(n, part, way).wait_recv()

        @pl.when(core == 0)
        def _():
            ref = sums.at[n, :, :, xx]
            ref[...] = (ref[...].astype(F32) + xrecv[n, 0, 1].astype(F32) + xrecv[n, 1, 1].astype(F32)).astype(BF)
            for d in range(1, 8):
                z_direct(n, d).start()

        @pl.when(core == 1)
        def _():
            total = sums[n, :, :, xx].astype(F32) + xrecv[n, 0, 1].astype(F32) + xrecv[n, 1, 1].astype(F32)
            flat = total.reshape(40 * 8, LANES)
            for k in range(3):
                sc[k] = flat[:, 128 * k : 128 * k + 128]
            for to in range(8):
                for k in range(3):
                    mids[n, to, :, 128 * k : 128 * k + 128] = sc[k, pl.ds(to, 40, stride=8), :].astype(BF)
            for d in range(1, 8):
                y_direct(n, d).start()

    def last_copy(n, d, over_y):
        if over_y:
            to = (yy + d) % 8
            device = (to * 2 + core, space)
        else:
            to = (zz + d) % 8
            device = (dp, to * 4 + xx)
        return pltpu.make_async_remote_copy(
            src_ref=ys.at[n, to], dst_ref=yr.at[n, d - 1],
            send_sem=ysend.at[n, d - 1], recv_sem=yrsem.at[n, d - 1],
            device_id=device, device_id_type=MESH)

    def z_finish(n):
        total = sums[n, zz // 2, zz % 2, xx].astype(F32)
        for d in range(1, 8):
            z_direct(n, d).wait_recv()
            total += late[n, d - 1].astype(F32)
        flat = total.reshape(5 * 8, LANES)
        for k in range(3):
            sc[k, 0:40] = flat[:, 128 * k : 128 * k + 128]
        for to in range(8):
            for k in range(3):
                ys[n, to, 0:5, 128 * k : 128 * k + 128] = sc[k, pl.ds(to, 5, stride=8), :].astype(BF)
        for d in range(1, 8):
            last_copy(n, d, True).start()

    def y_finish(n):
        total = mids[n, yy].astype(F32)
        for d in range(1, 8):
            y_direct(n, d).wait_recv()
            total += midr[n, d - 1].astype(F32)
        for k in range(3):
            sc[k, 0:40] = total[:, 128 * k : 128 * k + 128]
        for to in range(8):
            for k in range(3):
                ys[n, to, 0:5, 128 * k : 128 * k + 128] = sc[k, 5 * to : 5 * to + 5, :].astype(BF)
        for d in range(1, 8):
            last_copy(n, d, False).start()

    def last(n, ref):
        def total_over(over_y):
            total = ys[n, yy if over_y else zz].astype(F32)
            for d in range(1, 8):
                last_copy(n, d, over_y).wait_recv()
                total += yr[n, d - 1].astype(F32)
            ref[...] = total

        @pl.when(core == 0)
        def _():
            total_over(True)

        @pl.when(core == 1)
        def _():
            total_over(False)

    def middle(n):
        @pl.when(core == 0)
        def _():
            z_finish(n)

        @pl.when(core == 1)
        def _():
            y_finish(n)

    ys[...] = jnp.zeros(ys.shape, BF)
    for i in range(3):
        terms[i, :, 3 * CH :] = jnp.zeros((CH, 64), F32)

    for i in range(3):
        terms[i, :, : 3 * CH] = dot(lhs_t[...], h3[i * COLS : i * COLS + OWN, :])
    pack_terms(1)

    loads[3].wait()
    def conv_back(runs):
        def rows(i):
            parts = [c3[(first + i) * COLS : (first + count + i) * COLS, :] for first, count in runs]
            return parts[0] if len(parts) == 1 else jnp.concatenate(parts, axis=0)

        total = dot(rows(2), w2[0])
        total += dot(rows(1), w2[1])
        total += dot(rows(0), w2[2])
        at = 0
        for first, count in runs:
            acc[first * COLS : (first + count) * COLS, :] = total[at : at + count * COLS]
            at += count * COLS

        def finish(k, _):
            at = pl.ds(pl.multiple_of(k * COLS, COLS), COLS)
            before, here, after = column_shifts(acc[at, :] * slope[at, :])
            hg3[at, :] = jnp.concatenate([after, here, before], axis=1)
            return 0

        for first, count in runs:
            lax.fori_loop(first, first + count, finish, 0)

    conv_back([(1, 8)])

    core_sum(1)
    xstart(1)

    for i in range(3):
        if i != 1:
            lhs_t[...] = dot_nt(perm[...], act[(i + 1) * COLS : (i + 1) * COLS + OWN, :]).astype(BF)
        left = mid_t if i == 1 else lhs_t
        terms[i, :, : 3 * CH] = dot(left[...], hg3[COLS : COLS + OWN, :])
    pack_terms(0)
    xstep(1)
    conv_back([(0, 1), (9, 1)])
    clear_outside(hg3)

    for i in range(3):
        w2t[i] = jnp.concatenate([w2[i, CH * j : CH * j + CH, :] for j in range(3)], axis=1)
        w1t[i] = jnp.concatenate([w1[i, CH * j : CH * j + CH, :] for j in range(3)], axis=1)
    core_sum(0)
    xstart(0)

    total = dot_nt(h3[0:OWN, :], w2t[0])
    total += dot_nt(h3[COLS : COLS + OWN, :], w2t[1])
    total += dot_nt(h3[2 * COLS : 2 * COLS + OWN, :], w2t[2])
    outv[...] = total.astype(BF)
    store_out = pltpu.make_async_copy(outv, out_hbm, store_sem.at[0])
    store_out.start()
    xfinal(1)
    xstep(0)

    total = dot_nt(hg3[2 * COLS : 2 * COLS + OWN, :], w1t[0])
    total += dot_nt(hg3[COLS : COLS + OWN, :], w1t[1])
    total += dot_nt(hg3[0:OWN, :], w1t[2])
    acc[0:OWN, :] = total

    def finish_latent(k, _):
        at = pl.ds(pl.multiple_of(k * COLS, COLS), COLS)
        value = latx[pl.ds(pl.multiple_of((k + 2) * COLS, COLS), COLS), :].astype(F32)
        sig = jax.nn.sigmoid(value)
        lgv[at, :] = (acc[at, :] * (sig * (1.0 + value * (1.0 - sig)))).astype(BF)
        return 0

    lax.fori_loop(0, 8, finish_latent, 0)
    store_lg = pltpu.make_async_copy(lgv, lg_hbm, store_sem.at[1])
    store_lg.start()
    middle(1)
    xfinal(0)

    @pl.when(space > 0)
    def _():
        for to_up, _d in halos:
            to_up.wait_send()

    @pl.when(space < 31)
    def _():
        for _u, to_down in halos:
            to_down.wait_send()

    for n in range(2):
        for r in range(5):
            core_copy(n, r).wait_send()
        for way in range(2):
            for part in (1, 2, 3):
                xcopy(n, part, way).wait_send()
    store_out.wait()
    store_lg.wait()
    middle(0)

    def sent(copy):
        for n in range(2):
            for d in range(1, 8):
                copy(n, d).wait_send()

    @pl.when(core == 0)
    def _():
        sent(z_direct)

    @pl.when(core == 1)
    def _():
        sent(y_direct)

    last(1, g2_ref)
    last(0, g1_ref)

    @pl.when(core == 0)
    def _():
        sent(lambda n, d: last_copy(n, d, True))

    @pl.when(core == 1)
    def _():
        sent(lambda n, d: last_copy(n, d, False))


def finish_kernel(out_hbm, lg_hbm, g1_hbm, g2_hbm, out_res, lg_res, f1_res, f2_res, buf, share, f1, f2, sem_in, sem_out):
    shares = [
        pltpu.make_async_copy(g1_hbm, share.at[0], sem_in.at[2, 0]),
        pltpu.make_async_copy(g2_hbm, share.at[1], sem_in.at[2, 1]),
    ]
    flats = [
        pltpu.make_async_copy(f1, f1_res, sem_out.at[2, 0]),
        pltpu.make_async_copy(f2, f2_res, sem_out.at[2, 1]),
    ]
    for copy in shares:
        copy.start()
    takes, puts = [], []
    for n, (src, dst) in enumerate(((out_hbm, out_res), (lg_hbm, lg_res))):
        for k in range(2):
            at = pl.ds(k * OWN // 2, OWN // 2)
            takes.append(pltpu.make_async_copy(src.at[at], buf.at[n, at], sem_in.at[n, k]))
            puts.append(pltpu.make_async_copy(buf.at[n, at], dst.at[at], sem_out.at[n, k]))
    for take in takes:
        take.start()
    for copy in shares:
        copy.wait()
    lane = lax.broadcasted_iota(jnp.int32, (1, 128), 1)
    for n, dst in enumerate((f1, f2)):
        src = share.at[n]
        for k in range(15):
            start, end = 128 * k, min(128 * k + 128, 5 * UNIT)
            size, value, at = end - start, None, start
            while at < end:
                row, col = divmod(at, UNIT)
                base = min(col // 128 * 128, LANES - 256)
                piece = src[row : row + 1, base : base + 256]
                shift = (at - start - (col - base)) % 256
                if shift:
                    piece = pltpu.roll(piece, shift, 1)
                piece = piece[:, :128]
                value = piece if value is None else jnp.where(lane < at - start, value, piece)
                at += min(UNIT - col, end - at)
            dst[pl.ds(start, size)] = value[0, :size]
        flats[n].start()
    for take, put in zip(takes, puts):
        take.wait()
        put.start()
    for copy in puts + flats:
        copy.wait()


def local(latent, first_weight, second_weight, cotangent):
    def taps(weight):
        return jnp.transpose(weight, (1, 2, 0, 3)).reshape(3, 3 * CH, CH)

    any_spec = pl.BlockSpec(memory_space=pl.ANY)
    vmem_spec = pl.BlockSpec(memory_space=pltpu.VMEM)
    dma = pltpu.SemaphoreType.DMA
    out, latent_grad, first, second = pl.pallas_call(
        kernel,
        out_shape=(
            jax.ShapeDtypeStruct((OWN, CH), BF),
            jax.ShapeDtypeStruct((OWN, CH), BF),
            jax.ShapeDtypeStruct((8, LANES), F32),
            jax.ShapeDtypeStruct((8, LANES), F32),
        ),
        in_specs=[any_spec] * 4,
        out_specs=(any_spec, any_spec, vmem_spec, vmem_spec),
        scratch_shapes=[
            pltpu.VMEM((EXT, CH), BF),
            pltpu.VMEM((EXT, CH), BF),
            pltpu.VMEM((EXT, CH), BF),
            pltpu.VMEM((EXT, 3 * CH), BF),
            pltpu.VMEM((EXT, 3 * CH), BF),
            pltpu.VMEM((3, 3 * CH, CH), BF),
            pltpu.VMEM((3, 3 * CH, CH), BF),
            pltpu.VMEM((3, CH, 3 * CH), BF),
            pltpu.VMEM((3, CH, 3 * CH), BF),
            pltpu.VMEM((MID, CH), F32),
            pltpu.VMEM((MID, CH), F32),
            pltpu.VMEM((MID, 3 * CH), BF),
            pltpu.VMEM((MID, 3 * CH), BF),
            pltpu.VMEM((3, CH, 1024), F32),
            pltpu.VMEM((CH, CH), BF),
            pltpu.VMEM((CH, OWN), BF),
            pltpu.VMEM((CH, OWN), BF),
            pltpu.VMEM((2, UNITS, 8, 8, LANES), BF),
            pltpu.VMEM((2, UNITS, 4, 8, LANES), BF),
            pltpu.VMEM((2, 4, 2, 4, 5, 8, LANES), BF),
            pltpu.VMEM((2, 2, 2, 4, 2, 5, 8, LANES), BF),
            pltpu.VMEM((2, 7, 5, 8, LANES), BF),
            pltpu.VMEM((2, 8, 40, LANES), BF),
            pltpu.VMEM((2, 7, 40, LANES), BF),
            pltpu.VMEM((3, 320, 128), F32),
            pltpu.VMEM((2, 8, 8, LANES), BF),
            pltpu.VMEM((2, 7, 8, LANES), BF),
            pltpu.VMEM((OWN, CH), BF),
            pltpu.VMEM((OWN, CH), BF),
            dma((4,)),
            dma((4,)),
            dma((4,)),
            dma((2, 5)),
            dma((2, 5)),
            dma((2, 2, 3)),
            dma((2, 2, 3)),
            dma((2, 7)),
            dma((2, 7)),
            dma((2, 7)),
            dma((2, 7)),
            dma((2,)),
        ],
        compiler_params=pltpu.CompilerParams(
            collective_id=0, has_side_effects=True, vmem_limit_bytes=60 * 1024 * 1024
        ),
        name="conv_pair",
    )(
        latent.reshape(OWN, CH), taps(first_weight), taps(second_weight), cotangent.reshape(OWN, CH)
    )
    out, latent_grad, first, second = pl.pallas_call(
        finish_kernel,
        out_shape=(
            jax.ShapeDtypeStruct((OWN, CH), BF),
            jax.ShapeDtypeStruct((OWN, CH), BF),
            jax.ShapeDtypeStruct((5 * UNIT,), F32),
            jax.ShapeDtypeStruct((5 * UNIT,), F32),
        ),
        in_specs=[any_spec] * 4,
        out_specs=(any_spec,) * 4,
        scratch_shapes=[
            pltpu.VMEM((2, OWN, CH), BF),
            pltpu.VMEM((2, 8, LANES), F32),
            pltpu.VMEM((5 * UNIT,), F32),
            pltpu.VMEM((5 * UNIT,), F32),
            dma((3, 2)),
            dma((3, 2)),
        ],
        name="finish",
    )(out, latent_grad, first, second)
    return (
        out.reshape(1, ROWS, COLS, CH),
        latent_grad.reshape(1, ROWS, COLS, CH),
        first,
        second,
    )


def solution(mesh):
    placed = (P("dp", "space", None, None), P(), P(), P("dp", "space", None, None))
    return jax.shard_map(
        local,
        mesh=mesh,
        in_specs=placed,
        out_specs=(
            P("dp", "space", None, None),
            P("dp", "space", None, None),
            P(("dp", "space")),
            P(("dp", "space")),
        ),
        check_vma=False,
    )
```

```python
import jax
import jax.numpy as jnp
from jax import lax
from jax.experimental import pallas as pl
from jax.experimental.pallas import tpu as pltpu
from jax.sharding import PartitionSpec as P

BF = jnp.bfloat16
F32 = jnp.float32
MESH = pl.DeviceIdType.MESH
COLS = 64
CH = 320
ROWS = 8
OWN = ROWS * COLS
EXT = (ROWS + 4) * COLS
MID = (ROWS + 2) * COLS
NT = (((1,), (1,)), ((), ()))
UNIT = 360
LANES = 384
UNITS = 40
FAR_FIRST = (4, 3, 5, 2, 6, 1, 7)


def dot(a, b):
    return jnp.dot(a, b, preferred_element_type=F32)


def dot_nt(a, b):
    return lax.dot_general(a, b, NT, preferred_element_type=F32)


def column_shifts(value):
    count = value.shape[0]
    col = lax.broadcasted_iota(jnp.int32, value.shape, 0) % COLS
    before = jnp.where(col == 0, 0.0, pltpu.roll(value, 1, 0))
    after = jnp.where(col == COLS - 1, 0.0, pltpu.roll(value, count - 1, 0))
    return before.astype(BF), value.astype(BF), after.astype(BF)


def unit_pieces(u):
    pieces = []
    start, left, lane = UNIT * u, UNIT, 0
    while left:
        tap, col = divmod(start, 3 * CH)
        size = min(left, 3 * CH - col)
        pieces.append((tap, col, size, lane))
        start, left, lane = start + size, left - size, lane + size
    return pieces


def kernel(
    lat_hbm, w1_hbm, w2_hbm, cot_hbm, out_hbm, lg_hbm, g1_ref, g2_ref,
    latx, cotx, act, a3, c3, w1, w2, w1t, w2t, acc, slope, h3, hg3, terms, perm, lhs_t, mid_t,
    grid, core_recv, sums, xrecv, late, mids, midr, sc, ys, yr, outv, lgv,
    load_sem, halo_send, halo_recv, core_send, core_rsem, xsend, xrsem, lsend, lrsem, ysend, yrsem, store_sem,
):
    dp, space = lax.axis_index("dp"), lax.axis_index("space")
    yy, core = dp // 2, dp % 2
    zz, xx = space // 4, space % 4
    up, down = (space + 31) % 32, (space + 1) % 32

    loads = [
        pltpu.make_async_copy(lat_hbm, latx.at[pl.ds(2 * COLS, OWN)], load_sem.at[0]),
        pltpu.make_async_copy(cot_hbm, cotx.at[pl.ds(2 * COLS, OWN)], load_sem.at[1]),
        pltpu.make_async_copy(w1_hbm, w1, load_sem.at[2]),
        pltpu.make_async_copy(w2_hbm, w2, load_sem.at[3]),
    ]
    for load in loads:
        load.start()

    peers = [(dp, up), (dp, down), (yy * 2 + 1 - core, space)]
    peers += [(dp, (zz + k) % 8 * 4 + xx) for k in range(1, 8)]
    peers += [(dp, zz * 4 + (xx + k) % 4) for k in (1, 2, 3)]
    peers += [((yy + k) % 8 * 2 + core, space) for k in range(1, 8)]
    barrier = pltpu.get_barrier_semaphore()
    for peer in peers:
        pl.semaphore_signal(barrier, inc=1, device_id=peer, device_id_type=MESH)

    def widen(src, dst, first, last, flip, activate):
        def group(k, _):
            at = pl.ds(pl.multiple_of(k * COLS, COLS), COLS)
            value = src[at, :].astype(F32)
            if activate:
                value = value * jax.nn.sigmoid(value)
                act[at, :] = value.astype(BF)
            one, two, three = column_shifts(value)
            dst[at, :] = jnp.concatenate([three, two, one] if flip else [one, two, three], axis=1)
            return 0
        lax.fori_loop(first, last, group, 0)

    loads[0].wait()
    widen(latx, a3, 2, 10, False, True)
    loads[1].wait()
    widen(cotx, c3, 2, 10, True, False)

    pl.semaphore_wait(barrier, len(peers))
    halos = []
    for n, (src, dst) in enumerate(((lat_hbm, latx), (cot_hbm, cotx))):
        to_up = pltpu.make_async_remote_copy(
            src_ref=src.at[pl.ds(0, 2 * COLS)], dst_ref=dst.at[pl.ds(10 * COLS, 2 * COLS)],
            send_sem=halo_send.at[2 * n], recv_sem=halo_recv.at[2 * n],
            device_id=(dp, up), device_id_type=MESH)
        to_down = pltpu.make_async_remote_copy(
            src_ref=src.at[pl.ds(6 * COLS, 2 * COLS)], dst_ref=dst.at[pl.ds(0, 2 * COLS)],
            send_sem=halo_send.at[2 * n + 1], recv_sem=halo_recv.at[2 * n + 1],
            device_id=(dp, down), device_id_type=MESH)
        halos.append((to_up, to_down))

    @pl.when(space > 0)
    def _():
        for to_up, _d in halos:
            to_up.start()

    @pl.when(space < 31)
    def _():
        for _u, to_down in halos:
            to_down.start()

    shape = (CH, CH)
    row = lax.broadcasted_iota(jnp.int32, shape, 0)
    chan = lax.broadcasted_iota(jnp.int32, shape, 1)
    group = ((row % 8) * 2 + row // 32 % 2) * 4 + row // 8 % 4
    perm[...] = jnp.where(chan == 5 * group + row // 64, 1.0, 0.0).astype(BF)
    lhs_t[...] = dot_nt(perm[...], cotx[2 * COLS : 10 * COLS, :]).astype(BF)
    mid_t[...] = dot_nt(perm[...], act[2 * COLS : 10 * COLS, :]).astype(BF)

    loads[2].wait()

    def conv_one(runs):
        def rows(i):
            parts = [a3[(first + i) * COLS : (first + count + i) * COLS, :] for first, count in runs]
            return parts[0] if len(parts) == 1 else jnp.concatenate(parts, axis=0)

        total = dot(rows(0), w1[0])
        total += dot(rows(1), w1[1])
        total += dot(rows(2), w1[2])
        at = 0
        for first, count in runs:
            acc[first * COLS : (first + count) * COLS, :] = total[at : at + count * COLS]
            at += count * COLS

        def finish(k, _):
            at = pl.ds(pl.multiple_of(k * COLS, COLS), COLS)
            hidden = acc[at, :].astype(BF).astype(F32)
            sig = jax.nn.sigmoid(hidden)
            slope[at, :] = sig * (1.0 + hidden * (1.0 - sig))
            h3[at, :] = jnp.concatenate(column_shifts(hidden * sig), axis=1)
            return 0

        for first, count in runs:
            lax.fori_loop(first, first + count, finish, 0)

    conv_one([(2, 6)])

    @pl.when(space == 0)
    def _():
        latx[0 : 2 * COLS, :] = jnp.zeros((2 * COLS, CH), BF)
        cotx[0 : 2 * COLS, :] = jnp.zeros((2 * COLS, CH), BF)

    @pl.when(space == 31)
    def _():
        latx[10 * COLS :, :] = jnp.zeros((2 * COLS, CH), BF)
        cotx[10 * COLS :, :] = jnp.zeros((2 * COLS, CH), BF)

    @pl.when(space < 31)
    def _():
        for to_up, _d in halos:
            to_up.wait_recv()

    @pl.when(space > 0)
    def _():
        for _u, to_down in halos:
            to_down.wait_recv()

    for first in (0, 10):
        widen(latx, a3, first, first + 2, False, True)
        widen(cotx, c3, first, first + 2, True, False)
    conv_one([(0, 2), (8, 2)])

    def clear_outside(ref):
        @pl.when(space == 0)
        def _():
            ref[0:COLS, :] = jnp.zeros((COLS, 3 * CH), BF)

        @pl.when(space == 31)
        def _():
            ref[9 * COLS :, :] = jnp.zeros((COLS, 3 * CH), BF)

    clear_outside(h3)

    other = (yy * 2 + 1 - core, space)

    def core_copy(n, r):
        return pltpu.make_async_remote_copy(
            src_ref=grid.at[n, pl.ds(8 * r, 8), pl.ds(4 * (1 - core), 4)],
            dst_ref=core_recv.at[n, pl.ds(8 * r, 8)],
            send_sem=core_send.at[n, r], recv_sem=core_rsem.at[n, r],
            device_id=other, device_id_type=MESH)

    def pack_terms(n):
        lane = lax.broadcasted_iota(jnp.int32, (64, LANES), 1)
        for r in range(5):
            for u in range(8):
                value = None
                for tap, col, size, put in unit_pieces(u):
                    base = min(col // 128 * 128, 1024 - LANES)
                    width = -(-max(col - base + size, LANES) // 128) * 128
                    shift = (put - (col - base)) % width
                    piece = terms[tap, 64 * r : 64 * r + 64, base : base + width]
                    if shift:
                        piece = pltpu.roll(piece, shift, 1)
                    piece = piece[:, :LANES]
                    value = piece if value is None else jnp.where(lane < put, value, piece)
                grid[n, 8 * r + u] = value.reshape(8, 8, LANES).astype(BF)
            core_copy(n, r).start()

    def core_sum(n):
        for r in range(5):
            core_copy(n, r).wait_recv()
        for k in range(4):
            part = grid[n, :, 4 * core + k].astype(F32) + core_recv[n, :, k].astype(F32)
            sums[n, k] = part.reshape(2, 4, 5, 8, LANES).astype(BF)

    def xcopy(n, part, way):
        step = 1 if way == 0 else 3
        target = (xx + (2 * step if part == 1 else step)) % 4
        lo = 2 * way if part < 3 else 2 - 2 * way
        return pltpu.make_async_remote_copy(
            src_ref=sums.at[n, pl.ds(lo, 2), :, target],
            dst_ref=xrecv.at[n, way, min(part, 2) - 1, pl.ds(lo, 2)],
            send_sem=xsend.at[n, way, part - 1], recv_sem=xrsem.at[n, way, part - 1],
            device_id=(dp, zz * 4 + (xx + step) % 4), device_id_type=MESH)

    def xstart(n):
        for part in (1, 3):
            for way in range(2):
                xcopy(n, part, way).start()

    def xstep(n):
        for way in range(2):
            xcopy(n, 1, way).wait_recv()
            lo = 2 * way
            ref = sums.at[n, pl.ds(lo, 2), :, (xx + (1 if way == 0 else 3)) % 4]
            ref[...] = (ref[...].astype(F32) + xrecv[n, way, 0, lo : lo + 2].astype(F32)).astype(BF)
            xcopy(n, 2, way).start()

    def z_direct(n, d):
        to = (zz + d) % 8
        return pltpu.make_async_remote_copy(
            src_ref=sums.at[n, to // 2, to % 2, xx], dst_ref=late.at[n, d - 1],
            send_sem=lsend.at[n, d - 1], recv_sem=lrsem.at[n, d - 1],
            device_id=(dp, to * 4 + xx), device_id_type=MESH)

    def y_direct(n, d):
        to = (yy + d) % 8
        return pltpu.make_async_remote_copy(
            src_ref=mids.at[n, to], dst_ref=midr.at[n, d - 1],
            send_sem=lsend.at[n, d - 1], recv_sem=lrsem.at[n, d - 1],
            device_id=(to * 2 + core, space), device_id_type=MESH)

    def xfinal(n):
        for way in range(2):
            for part in (2, 3):
                xcopy(n, part, way).wait_recv()

        @pl.when(core == 0)
        def _():
            ref = sums.at[n, :, :, xx]
            ref[...] = (ref[...].astype(F32) + xrecv[n, 0, 1].astype(F32) + xrecv[n, 1, 1].astype(F32)).astype(BF)
            for d in FAR_FIRST:
                z_direct(n, d).start()

        @pl.when(core == 1)
        def _():
            total = sums[n, :, :, xx].astype(F32) + xrecv[n, 0, 1].astype(F32) + xrecv[n, 1, 1].astype(F32)
            flat = total.reshape(40 * 8, LANES)
            for k in range(3):
                sc[k] = flat[:, 128 * k : 128 * k + 128]
            for to in range(8):
                for k in range(3):
                    mids[n, to, :, 128 * k : 128 * k + 128] = sc[k, pl.ds(to, 40, stride=8), :].astype(BF)
            for d in FAR_FIRST:
                y_direct(n, d).start()

    def last_copy(n, d, over_y):
        if over_y:
            to = (yy + d) % 8
            device = (to * 2 + core, space)
        else:
            to = (zz + d) % 8
            device = (dp, to * 4 + xx)
        return pltpu.make_async_remote_copy(
            src_ref=ys.at[n, to], dst_ref=yr.at[n, d - 1],
            send_sem=ysend.at[n, d - 1], recv_sem=yrsem.at[n, d - 1],
            device_id=device, device_id_type=MESH)

    def z_finish(n):
        total = sums[n, zz // 2, zz % 2, xx].astype(F32)
        for d in range(1, 8):
            z_direct(n, d).wait_recv()
            total += late[n, d - 1].astype(F32)
        flat = total.reshape(5 * 8, LANES)
        for k in range(3):
            sc[k, 0:40] = flat[:, 128 * k : 128 * k + 128]
        for to in range(8):
            for k in range(3):
                ys[n, to, 0:5, 128 * k : 128 * k + 128] = sc[k, pl.ds(to, 5, stride=8), :].astype(BF)
        for d in FAR_FIRST:
            last_copy(n, d, True).start()

    def y_finish(n):
        total = mids[n, yy].astype(F32)
        for d in range(1, 8):
            y_direct(n, d).wait_recv()
            total += midr[n, d - 1].astype(F32)
        for k in range(3):
            sc[k, 0:40] = total[:, 128 * k : 128 * k + 128]
        for to in range(8):
            for k in range(3):
                ys[n, to, 0:5, 128 * k : 128 * k + 128] = sc[k, 5 * to : 5 * to + 5, :].astype(BF)
        for d in FAR_FIRST:
            last_copy(n, d, False).start()

    def last(n, ref):
        def total_over(over_y):
            total = ys[n, yy if over_y else zz].astype(F32)
            for d in range(1, 8):
                last_copy(n, d, over_y).wait_recv()
                total += yr[n, d - 1].astype(F32)
            ref[...] = total

        @pl.when(core == 0)
        def _():
            total_over(True)

        @pl.when(core == 1)
        def _():
            total_over(False)

    def middle(n):
        @pl.when(core == 0)
        def _():
            z_finish(n)

        @pl.when(core == 1)
        def _():
            y_finish(n)

    ys[...] = jnp.zeros(ys.shape, BF)
    for i in range(3):
        terms[i, :, 3 * CH :] = jnp.zeros((CH, 64), F32)

    for i in range(3):
        terms[i, :, : 3 * CH] = dot(lhs_t[...], h3[i * COLS : i * COLS + OWN, :])
    pack_terms(1)

    loads[3].wait()
    def conv_back(runs):
        def rows(i):
            parts = [c3[(first + i) * COLS : (first + count + i) * COLS, :] for first, count in runs]
            return parts[0] if len(parts) == 1 else jnp.concatenate(parts, axis=0)

        total = dot(rows(2), w2[0])
        total += dot(rows(1), w2[1])
        total += dot(rows(0), w2[2])
        at = 0
        for first, count in runs:
            acc[first * COLS : (first + count) * COLS, :] = total[at : at + count * COLS]
            at += count * COLS

        def finish(k, _):
            at = pl.ds(pl.multiple_of(k * COLS, COLS), COLS)
            before, here, after = column_shifts(acc[at, :] * slope[at, :])
            hg3[at, :] = jnp.concatenate([after, here, before], axis=1)
            return 0

        for first, count in runs:
            lax.fori_loop(first, first + count, finish, 0)

    conv_back([(1, 8)])

    core_sum(1)
    xstart(1)

    for i in range(3):
        if i != 1:
            lhs_t[...] = dot_nt(perm[...], act[(i + 1) * COLS : (i + 1) * COLS + OWN, :]).astype(BF)
        left = mid_t if i == 1 else lhs_t
        terms[i, :, : 3 * CH] = dot(left[...], hg3[COLS : COLS + OWN, :])
    pack_terms(0)
    xstep(1)

    for i in range(3):
        w2t[i] = jnp.concatenate([w2[i, CH * j : CH * j + CH, :] for j in range(3)], axis=1)
        w1t[i] = jnp.concatenate([w1[i, CH * j : CH * j + CH, :] for j in range(3)], axis=1)
    core_sum(0)
    xstart(0)

    total = dot_nt(h3[0:OWN, :], w2t[0])
    total += dot_nt(h3[COLS : COLS + OWN, :], w2t[1])
    total += dot_nt(h3[2 * COLS : 2 * COLS + OWN, :], w2t[2])
    outv[...] = total.astype(BF)
    store_out = pltpu.make_async_copy(outv, out_hbm, store_sem.at[0])
    store_out.start()
    xfinal(1)
    xstep(0)
    conv_back([(0, 1), (9, 1)])
    clear_outside(hg3)

    total = dot_nt(hg3[2 * COLS : 2 * COLS + OWN, :], w1t[0])
    total += dot_nt(hg3[COLS : COLS + OWN, :], w1t[1])
    total += dot_nt(hg3[0:OWN, :], w1t[2])
    acc[0:OWN, :] = total

    def finish_latent(k, _):
        at = pl.ds(pl.multiple_of(k * COLS, COLS), COLS)
        value = latx[pl.ds(pl.multiple_of((k + 2) * COLS, COLS), COLS), :].astype(F32)
        sig = jax.nn.sigmoid(value)
        lgv[at, :] = (acc[at, :] * (sig * (1.0 + value * (1.0 - sig)))).astype(BF)
        return 0

    lax.fori_loop(0, 8, finish_latent, 0)
    store_lg = pltpu.make_async_copy(lgv, lg_hbm, store_sem.at[1])
    store_lg.start()
    middle(1)
    xfinal(0)

    @pl.when(space > 0)
    def _():
        for to_up, _d in halos:
            to_up.wait_send()

    @pl.when(space < 31)
    def _():
        for _u, to_down in halos:
            to_down.wait_send()

    for n in range(2):
        for r in range(5):
            core_copy(n, r).wait_send()
        for way in range(2):
            for part in (1, 2, 3):
                xcopy(n, part, way).wait_send()
    store_out.wait()
    store_lg.wait()
    middle(0)

    def sent(copy):
        for n in range(2):
            for d in range(1, 8):
                copy(n, d).wait_send()

    @pl.when(core == 0)
    def _():
        sent(z_direct)

    @pl.when(core == 1)
    def _():
        sent(y_direct)

    last(1, g2_ref)
    last(0, g1_ref)

    @pl.when(core == 0)
    def _():
        sent(lambda n, d: last_copy(n, d, True))

    @pl.when(core == 1)
    def _():
        sent(lambda n, d: last_copy(n, d, False))


def finish_kernel(out_hbm, lg_hbm, g1_hbm, g2_hbm, out_res, lg_res, f1_res, f2_res, buf, share, f1, f2, sem_in, sem_out):
    shares = [
        pltpu.make_async_copy(g1_hbm, share.at[0], sem_in.at[2, 0]),
        pltpu.make_async_copy(g2_hbm, share.at[1], sem_in.at[2, 1]),
    ]
    flats = [
        pltpu.make_async_copy(f1, f1_res, sem_out.at[2, 0]),
        pltpu.make_async_copy(f2, f2_res, sem_out.at[2, 1]),
    ]
    for copy in shares:
        copy.start()
    takes, puts = [], []
    for n, (src, dst) in enumerate(((out_hbm, out_res), (lg_hbm, lg_res))):
        for k in range(2):
            at = pl.ds(k * OWN // 2, OWN // 2)
            takes.append(pltpu.make_async_copy(src.at[at], buf.at[n, at], sem_in.at[n, k]))
            puts.append(pltpu.make_async_copy(buf.at[n, at], dst.at[at], sem_out.at[n, k]))
    for take in takes:
        take.start()
    for copy in shares:
        copy.wait()
    lane = lax.broadcasted_iota(jnp.int32, (1, 128), 1)
    for n, dst in enumerate((f1, f2)):
        src = share.at[n]
        for k in range(15):
            start, end = 128 * k, min(128 * k + 128, 5 * UNIT)
            size, value, at = end - start, None, start
            while at < end:
                row, col = divmod(at, UNIT)
                base = min(col // 128 * 128, LANES - 256)
                piece = src[row : row + 1, base : base + 256]
                shift = (at - start - (col - base)) % 256
                if shift:
                    piece = pltpu.roll(piece, shift, 1)
                piece = piece[:, :128]
                value = piece if value is None else jnp.where(lane < at - start, value, piece)
                at += min(UNIT - col, end - at)
            dst[pl.ds(start, size)] = value[0, :size]
        flats[n].start()
    for take, put in zip(takes, puts):
        take.wait()
        put.start()
    for copy in puts + flats:
        copy.wait()


def local(latent, first_weight, second_weight, cotangent):
    def taps(weight):
        return jnp.transpose(weight, (1, 2, 0, 3)).reshape(3, 3 * CH, CH)

    any_spec = pl.BlockSpec(memory_space=pl.ANY)
    vmem_spec = pl.BlockSpec(memory_space=pltpu.VMEM)
    dma = pltpu.SemaphoreType.DMA
    out, latent_grad, first, second = pl.pallas_call(
        kernel,
        out_shape=(
            jax.ShapeDtypeStruct((OWN, CH), BF),
            jax.ShapeDtypeStruct((OWN, CH), BF),
            jax.ShapeDtypeStruct((8, LANES), F32),
            jax.ShapeDtypeStruct((8, LANES), F32),
        ),
        in_specs=[any_spec] * 4,
        out_specs=(any_spec, any_spec, vmem_spec, vmem_spec),
        scratch_shapes=[
            pltpu.VMEM((EXT, CH), BF),
            pltpu.VMEM((EXT, CH), BF),
            pltpu.VMEM((EXT, CH), BF),
            pltpu.VMEM((EXT, 3 * CH), BF),
            pltpu.VMEM((EXT, 3 * CH), BF),
            pltpu.VMEM((3, 3 * CH, CH), BF),
            pltpu.VMEM((3, 3 * CH, CH), BF),
            pltpu.VMEM((3, CH, 3 * CH), BF),
            pltpu.VMEM((3, CH, 3 * CH), BF),
            pltpu.VMEM((MID, CH), F32),
            pltpu.VMEM((MID, CH), F32),
            pltpu.VMEM((MID, 3 * CH), BF),
            pltpu.VMEM((MID, 3 * CH), BF),
            pltpu.VMEM((3, CH, 1024), F32),
            pltpu.VMEM((CH, CH), BF),
            pltpu.VMEM((CH, OWN), BF),
            pltpu.VMEM((CH, OWN), BF),
            pltpu.VMEM((2, UNITS, 8, 8, LANES), BF),
            pltpu.VMEM((2, UNITS, 4, 8, LANES), BF),
            pltpu.VMEM((2, 4, 2, 4, 5, 8, LANES), BF),
            pltpu.VMEM((2, 2, 2, 4, 2, 5, 8, LANES), BF),
            pltpu.VMEM((2, 7, 5, 8, LANES), BF),
            pltpu.VMEM((2, 8, 40, LANES), BF),
            pltpu.VMEM((2, 7, 40, LANES), BF),
            pltpu.VMEM((3, 320, 128), F32),
            pltpu.VMEM((2, 8, 8, LANES), BF),
            pltpu.VMEM((2, 7, 8, LANES), BF),
            pltpu.VMEM((OWN, CH), BF),
            pltpu.VMEM((OWN, CH), BF),
            dma((4,)),
            dma((4,)),
            dma((4,)),
            dma((2, 5)),
            dma((2, 5)),
            dma((2, 2, 3)),
            dma((2, 2, 3)),
            dma((2, 7)),
            dma((2, 7)),
            dma((2, 7)),
            dma((2, 7)),
            dma((2,)),
        ],
        compiler_params=pltpu.CompilerParams(
            collective_id=0, has_side_effects=True, vmem_limit_bytes=60 * 1024 * 1024
        ),
        name="conv_pair",
    )(
        latent.reshape(OWN, CH), taps(first_weight), taps(second_weight), cotangent.reshape(OWN, CH)
    )
    out, latent_grad, first, second = pl.pallas_call(
        finish_kernel,
        out_shape=(
            jax.ShapeDtypeStruct((OWN, CH), BF),
            jax.ShapeDtypeStruct((OWN, CH), BF),
            jax.ShapeDtypeStruct((5 * UNIT,), F32),
            jax.ShapeDtypeStruct((5 * UNIT,), F32),
        ),
        in_specs=[any_spec] * 4,
        out_specs=(any_spec,) * 4,
        scratch_shapes=[
            pltpu.VMEM((2, OWN, CH), BF),
            pltpu.VMEM((2, 8, LANES), F32),
            pltpu.VMEM((5 * UNIT,), F32),
            pltpu.VMEM((5 * UNIT,), F32),
            dma((3, 2)),
            dma((3, 2)),
        ],
        name="finish",
    )(out, latent_grad, first, second)
    return (
        out.reshape(1, ROWS, COLS, CH),
        latent_grad.reshape(1, ROWS, COLS, CH),
        first,
        second,
    )


def solution(mesh):
    placed = (P("dp", "space", None, None), P(), P(), P("dp", "space", None, None))
    return jax.shard_map(
        local,
        mesh=mesh,
        in_specs=placed,
        out_specs=(
            P("dp", "space", None, None),
            P("dp", "space", None, None),
            P(("dp", "space")),
            P(("dp", "space")),
        ),
        check_vma=False,
    )
```

```python
import jax
import jax.numpy as jnp
from jax import lax
from jax.experimental import pallas as pl
from jax.experimental.pallas import tpu as pltpu
from jax.sharding import PartitionSpec as P

BF = jnp.bfloat16
F32 = jnp.float32
MESH = pl.DeviceIdType.MESH
COLS = 64
CH = 320
ROWS = 8
OWN = ROWS * COLS
EXT = (ROWS + 4) * COLS
MID = (ROWS + 2) * COLS
NT = (((1,), (1,)), ((), ()))
UNIT = 360
LANES = 384
UNITS = 40
FAR_FIRST = (4, 3, 5, 2, 6, 1, 7)


def dot(a, b):
    return jnp.dot(a, b, preferred_element_type=F32)


def dot_nt(a, b):
    return lax.dot_general(a, b, NT, preferred_element_type=F32)


def column_shifts(value):
    count = value.shape[0]
    col = lax.broadcasted_iota(jnp.int32, value.shape, 0) % COLS
    before = jnp.where(col == 0, 0.0, pltpu.roll(value, 1, 0))
    after = jnp.where(col == COLS - 1, 0.0, pltpu.roll(value, count - 1, 0))
    return before.astype(BF), value.astype(BF), after.astype(BF)


def unit_pieces(u):
    pieces = []
    start, left, lane = UNIT * u, UNIT, 0
    while left:
        tap, col = divmod(start, 3 * CH)
        size = min(left, 3 * CH - col)
        pieces.append((tap, col, size, lane))
        start, left, lane = start + size, left - size, lane + size
    return pieces


def kernel(
    lat_hbm, w1_hbm, w2_hbm, cot_hbm, out_hbm, lg_hbm, g1_ref, g2_ref,
    latx, cotx, act, a3, c3, w1, w2, w1t, w2t, acc, slope, h3, hg3, terms, perm, lhs_t, mid_t,
    grid, core_recv, sums, zrecv, xrecv, late, mids, midr, sc, ys, yr, outv, lgv,
    load_sem, halo_send, halo_recv, core_send, core_rsem, zsend, zrsem, xsend, xrsem, lsend, lrsem, ysend, yrsem, store_sem,
):
    dp, space = lax.axis_index("dp"), lax.axis_index("space")
    yy, core = dp // 2, dp % 2
    zz, xx = space // 4, space % 4
    up, down = (space + 31) % 32, (space + 1) % 32

    loads = [
        pltpu.make_async_copy(lat_hbm, latx.at[pl.ds(2 * COLS, OWN)], load_sem.at[0]),
        pltpu.make_async_copy(cot_hbm, cotx.at[pl.ds(2 * COLS, OWN)], load_sem.at[1]),
        pltpu.make_async_copy(w1_hbm, w1, load_sem.at[2]),
        pltpu.make_async_copy(w2_hbm, w2, load_sem.at[3]),
    ]
    for load in loads:
        load.start()

    peers = [(dp, up), (dp, down), (yy * 2 + 1 - core, space)]
    peers += [(dp, (zz + k) % 8 * 4 + xx) for k in range(1, 8)]
    peers += [(dp, zz * 4 + (xx + k) % 4) for k in (1, 2, 3)]
    peers += [((yy + k) % 8 * 2 + core, space) for k in range(1, 8)]
    barrier = pltpu.get_barrier_semaphore()
    for peer in peers:
        pl.semaphore_signal(barrier, inc=1, device_id=peer, device_id_type=MESH)

    def widen(src, dst, first, last, flip, activate):
        def group(k, _):
            at = pl.ds(pl.multiple_of(k * COLS, COLS), COLS)
            value = src[at, :].astype(F32)
            if activate:
                value = value * jax.nn.sigmoid(value)
                act[at, :] = value.astype(BF)
            one, two, three = column_shifts(value)
            dst[at, :] = jnp.concatenate([three, two, one] if flip else [one, two, three], axis=1)
            return 0
        lax.fori_loop(first, last, group, 0)

    loads[0].wait()
    widen(latx, a3, 2, 10, False, True)
    loads[1].wait()
    widen(cotx, c3, 2, 10, True, False)

    pl.semaphore_wait(barrier, len(peers))
    halos = []
    for n, (src, dst) in enumerate(((lat_hbm, latx), (cot_hbm, cotx))):
        to_up = pltpu.make_async_remote_copy(
            src_ref=src.at[pl.ds(0, 2 * COLS)], dst_ref=dst.at[pl.ds(10 * COLS, 2 * COLS)],
            send_sem=halo_send.at[2 * n], recv_sem=halo_recv.at[2 * n],
            device_id=(dp, up), device_id_type=MESH)
        to_down = pltpu.make_async_remote_copy(
            src_ref=src.at[pl.ds(6 * COLS, 2 * COLS)], dst_ref=dst.at[pl.ds(0, 2 * COLS)],
            send_sem=halo_send.at[2 * n + 1], recv_sem=halo_recv.at[2 * n + 1],
            device_id=(dp, down), device_id_type=MESH)
        halos.append((to_up, to_down))

    @pl.when(space > 0)
    def _():
        for to_up, _d in halos:
            to_up.start()

    @pl.when(space < 31)
    def _():
        for _u, to_down in halos:
            to_down.start()

    shape = (CH, CH)
    row = lax.broadcasted_iota(jnp.int32, shape, 0)
    chan = lax.broadcasted_iota(jnp.int32, shape, 1)
    group = ((row % 8) * 2 + row // 32 % 2) * 4 + row // 8 % 4
    perm[...] = jnp.where(chan == 5 * group + row // 64, 1.0, 0.0).astype(BF)
    lhs_t[...] = dot_nt(perm[...], cotx[2 * COLS : 10 * COLS, :]).astype(BF)
    mid_t[...] = dot_nt(perm[...], act[2 * COLS : 10 * COLS, :]).astype(BF)

    loads[2].wait()

    def conv_one(runs):
        def rows(i):
            parts = [a3[(first + i) * COLS : (first + count + i) * COLS, :] for first, count in runs]
            return parts[0] if len(parts) == 1 else jnp.concatenate(parts, axis=0)

        total = dot(rows(0), w1[0])
        total += dot(rows(1), w1[1])
        total += dot(rows(2), w1[2])
        at = 0
        for first, count in runs:
            acc[first * COLS : (first + count) * COLS, :] = total[at : at + count * COLS]
            at += count * COLS

        def finish(k, _):
            at = pl.ds(pl.multiple_of(k * COLS, COLS), COLS)
            hidden = acc[at, :].astype(BF).astype(F32)
            sig = jax.nn.sigmoid(hidden)
            slope[at, :] = sig * (1.0 + hidden * (1.0 - sig))
            h3[at, :] = jnp.concatenate(column_shifts(hidden * sig), axis=1)
            return 0

        for first, count in runs:
            lax.fori_loop(first, first + count, finish, 0)

    conv_one([(2, 6)])

    @pl.when(space == 0)
    def _():
        latx[0 : 2 * COLS, :] = jnp.zeros((2 * COLS, CH), BF)
        cotx[0 : 2 * COLS, :] = jnp.zeros((2 * COLS, CH), BF)

    @pl.when(space == 31)
    def _():
        latx[10 * COLS :, :] = jnp.zeros((2 * COLS, CH), BF)
        cotx[10 * COLS :, :] = jnp.zeros((2 * COLS, CH), BF)

    @pl.when(space < 31)
    def _():
        for to_up, _d in halos:
            to_up.wait_recv()

    @pl.when(space > 0)
    def _():
        for _u, to_down in halos:
            to_down.wait_recv()

    for first in (0, 10):
        widen(latx, a3, first, first + 2, False, True)
        widen(cotx, c3, first, first + 2, True, False)
    conv_one([(0, 2), (8, 2)])

    def clear_outside(ref):
        @pl.when(space == 0)
        def _():
            ref[0:COLS, :] = jnp.zeros((COLS, 3 * CH), BF)

        @pl.when(space == 31)
        def _():
            ref[9 * COLS :, :] = jnp.zeros((COLS, 3 * CH), BF)

    clear_outside(h3)

    other = (yy * 2 + 1 - core, space)

    def core_copy(n, r):
        return pltpu.make_async_remote_copy(
            src_ref=grid.at[n, pl.ds(8 * r, 8), pl.ds(4 * (1 - core), 4)],
            dst_ref=core_recv.at[n, pl.ds(8 * r, 8)],
            send_sem=core_send.at[n, r], recv_sem=core_rsem.at[n, r],
            device_id=other, device_id_type=MESH)

    def pack_terms(n):
        lane = lax.broadcasted_iota(jnp.int32, (64, LANES), 1)
        for r in range(5):
            for u in range(8):
                value = None
                for tap, col, size, put in unit_pieces(u):
                    base = min(col // 128 * 128, 1024 - LANES)
                    width = -(-max(col - base + size, LANES) // 128) * 128
                    shift = (put - (col - base)) % width
                    piece = terms[tap, 64 * r : 64 * r + 64, base : base + width]
                    if shift:
                        piece = pltpu.roll(piece, shift, 1)
                    piece = piece[:, :LANES]
                    value = piece if value is None else jnp.where(lane < put, value, piece)
                grid[n, 8 * r + u] = value.reshape(8, 8, LANES).astype(BF)
            core_copy(n, r).start()

    def core_sum(n):
        for r in range(5):
            core_copy(n, r).wait_recv()
        for k in range(4):
            part = grid[n, :, 4 * core + k].astype(F32) + core_recv[n, :, k].astype(F32)
            sums[n, k] = part.reshape(2, 4, 5, 8, LANES).astype(BF)

    def xcopy(n, part, way):
        step = 1 if way == 0 else 3
        target = (xx + (2 * step if part == 1 else step)) % 4
        lo = 2 * way if part < 3 else 2 - 2 * way
        return pltpu.make_async_remote_copy(
            src_ref=sums.at[n, pl.ds(lo, 2), :, target],
            dst_ref=xrecv.at[n, way, min(part, 2) - 1, pl.ds(lo, 2)],
            send_sem=xsend.at[n, way, part - 1], recv_sem=xrsem.at[n, way, part - 1],
            device_id=(dp, zz * 4 + (xx + step) % 4), device_id_type=MESH)

    def xstart(n):
        for part in (1, 3):
            for way in range(2):
                xcopy(n, part, way).start()

    def xstep(n):
        for way in range(2):
            xcopy(n, 1, way).wait_recv()
            lo = 2 * way
            ref = sums.at[n, pl.ds(lo, 2), :, (xx + (1 if way == 0 else 3)) % 4]
            ref[...] = (ref[...].astype(F32) + xrecv[n, way, 0, lo : lo + 2].astype(F32)).astype(BF)
            xcopy(n, 2, way).start()

    steps = (1, 7)

    def zblock(target, way, half):
        lo, size = (2 * way, 2) if half else (0, 4)
        return sums.at[1, target // 2, target % 2, pl.ds(lo, size)]

    def zcopy(step, way):
        target = (zz + steps[way] * (5 - step)) % 8
        lo, size = (2 * way, 2) if step == 1 else (0, 4)
        return pltpu.make_async_remote_copy(
            src_ref=zblock(target, way, step == 1), dst_ref=zrecv.at[way, step - 1, pl.ds(lo, size)],
            send_sem=zsend.at[way, step - 1], recv_sem=zrsem.at[way, step - 1],
            device_id=(dp, (zz + steps[way]) % 8 * 4 + xx), device_id_type=MESH)

    def zstep(step):
        for way in range(2):
            if step >= 2:
                zcopy(step - 1, way).wait_recv()
                ref = zblock((zz + steps[way] * (5 - step)) % 8, way, step == 2)
                lo, size = (2 * way, 2) if step == 2 else (0, 4)
                ref[...] = (ref[...].astype(F32) + zrecv[way, step - 2, lo : lo + size].astype(F32)).astype(BF)
            zcopy(step, way).start()

    def x_direct(d):
        to = (xx + d) % 4
        return pltpu.make_async_remote_copy(
            src_ref=sums.at[1, zz // 2, zz % 2, to], dst_ref=late.at[1, d - 1],
            send_sem=lsend.at[1, d - 1], recv_sem=lrsem.at[1, d - 1],
            device_id=(dp, zz * 4 + to), device_id_type=MESH)

    def zfinal():
        for way in range(2):
            zcopy(4, way).wait_recv()
        ref = sums.at[1, zz // 2, zz % 2]
        ref[...] = (ref[...].astype(F32) + zrecv[0, 3].astype(F32) + zrecv[1, 3].astype(F32)).astype(BF)
        for d in (2, 1, 3):
            x_direct(d).start()

    def z_direct(n, d):
        to = (zz + d) % 8
        return pltpu.make_async_remote_copy(
            src_ref=sums.at[n, to // 2, to % 2, xx], dst_ref=late.at[n, d - 1],
            send_sem=lsend.at[n, d - 1], recv_sem=lrsem.at[n, d - 1],
            device_id=(dp, to * 4 + xx), device_id_type=MESH)

    def y_direct(n, d):
        to = (yy + d) % 8
        return pltpu.make_async_remote_copy(
            src_ref=mids.at[n, to], dst_ref=midr.at[n, d - 1],
            send_sem=lsend.at[n, d - 1], recv_sem=lrsem.at[n, d - 1],
            device_id=(to * 2 + core, space), device_id_type=MESH)

    def xfinal(n):
        for way in range(2):
            for part in (2, 3):
                xcopy(n, part, way).wait_recv()

        @pl.when(core == 0)
        def _():
            ref = sums.at[n, :, :, xx]
            ref[...] = (ref[...].astype(F32) + xrecv[n, 0, 1].astype(F32) + xrecv[n, 1, 1].astype(F32)).astype(BF)
            for d in FAR_FIRST:
                z_direct(n, d).start()

        @pl.when(core == 1)
        def _():
            total = sums[n, :, :, xx].astype(F32) + xrecv[n, 0, 1].astype(F32) + xrecv[n, 1, 1].astype(F32)
            flat = total.reshape(40 * 8, LANES)
            for k in range(3):
                sc[k] = flat[:, 128 * k : 128 * k + 128]
            for to in range(8):
                for k in range(3):
                    mids[n, to, :, 128 * k : 128 * k + 128] = sc[k, pl.ds(to, 40, stride=8), :].astype(BF)
            for d in FAR_FIRST:
                y_direct(n, d).start()

    def last_copy(n, d, over_y):
        if over_y:
            to = (yy + d) % 8
            device = (to * 2 + core, space)
        else:
            to = (zz + d) % 8
            device = (dp, to * 4 + xx)
        return pltpu.make_async_remote_copy(
            src_ref=ys.at[n, to], dst_ref=yr.at[n, d - 1],
            send_sem=ysend.at[n, d - 1], recv_sem=yrsem.at[n, d - 1],
            device_id=device, device_id_type=MESH)

    def late_finish(n):
        total = sums[n, zz // 2, zz % 2, xx].astype(F32)
        for d in range(1, 4 if n else 8):
            (x_direct(d) if n else z_direct(n, d)).wait_recv()
            total += late[n, d - 1].astype(F32)
        flat = total.reshape(5 * 8, LANES)
        for k in range(3):
            sc[k, 0:40] = flat[:, 128 * k : 128 * k + 128]
        for to in range(8):
            for k in range(3):
                ys[n, to, 0:5, 128 * k : 128 * k + 128] = sc[k, pl.ds(to, 5, stride=8), :].astype(BF)
        for d in FAR_FIRST:
            last_copy(n, d, True).start()

    def y_finish(n):
        total = mids[n, yy].astype(F32)
        for d in range(1, 8):
            y_direct(n, d).wait_recv()
            total += midr[n, d - 1].astype(F32)
        for k in range(3):
            sc[k, 0:40] = total[:, 128 * k : 128 * k + 128]
        for to in range(8):
            for k in range(3):
                ys[n, to, 0:5, 128 * k : 128 * k + 128] = sc[k, 5 * to : 5 * to + 5, :].astype(BF)
        for d in FAR_FIRST:
            last_copy(n, d, False).start()

    def last(n, ref):
        def total_over(over_y):
            total = ys[n, yy if over_y else zz].astype(F32)
            for d in range(1, 8):
                last_copy(n, d, over_y).wait_recv()
                total += yr[n, d - 1].astype(F32)
            ref[...] = total

        @pl.when(core == 0)
        def _():
            total_over(True)

        @pl.when(core == 1)
        def _():
            total_over(False)

    def by_core(zero, one):
        pl.when(core == 0)(zero)
        pl.when(core == 1)(one)

    def middle(n):
        @pl.when(core == 0)
        def _():
            late_finish(n)

        @pl.when(core == 1)
        def _():
            y_finish(n)

    ys[...] = jnp.zeros(ys.shape, BF)
    for i in range(3):
        terms[i, :, 3 * CH :] = jnp.zeros((CH, 64), F32)

    for i in range(3):
        terms[i, :, : 3 * CH] = dot(lhs_t[...], h3[i * COLS : i * COLS + OWN, :])
    pack_terms(1)

    loads[3].wait()
    def conv_back(runs):
        def rows(i):
            parts = [c3[(first + i) * COLS : (first + count + i) * COLS, :] for first, count in runs]
            return parts[0] if len(parts) == 1 else jnp.concatenate(parts, axis=0)

        total = dot(rows(2), w2[0])
        total += dot(rows(1), w2[1])
        total += dot(rows(0), w2[2])
        at = 0
        for first, count in runs:
            acc[first * COLS : (first + count) * COLS, :] = total[at : at + count * COLS]
            at += count * COLS

        def finish(k, _):
            at = pl.ds(pl.multiple_of(k * COLS, COLS), COLS)
            before, here, after = column_shifts(acc[at, :] * slope[at, :])
            hg3[at, :] = jnp.concatenate([after, here, before], axis=1)
            return 0

        for first, count in runs:
            lax.fori_loop(first, first + count, finish, 0)

    conv_back([(1, 8)])

    core_sum(1)
    by_core(lambda: zstep(1), lambda: xstart(1))

    for i in range(3):
        if i != 1:
            lhs_t[...] = dot_nt(perm[...], act[(i + 1) * COLS : (i + 1) * COLS + OWN, :]).astype(BF)
        left = mid_t if i == 1 else lhs_t
        terms[i, :, : 3 * CH] = dot(left[...], hg3[COLS : COLS + OWN, :])
    pack_terms(0)
    by_core(lambda: zstep(2), lambda: xstep(1))

    for i in range(3):
        w2t[i] = jnp.concatenate([w2[i, CH * j : CH * j + CH, :] for j in range(3)], axis=1)
        w1t[i] = jnp.concatenate([w1[i, CH * j : CH * j + CH, :] for j in range(3)], axis=1)
    core_sum(0)
    xstart(0)

    total = dot_nt(h3[0:OWN, :], w2t[0])
    total += dot_nt(h3[COLS : COLS + OWN, :], w2t[1])
    total += dot_nt(h3[2 * COLS : 2 * COLS + OWN, :], w2t[2])
    outv[...] = total.astype(BF)
    store_out = pltpu.make_async_copy(outv, out_hbm, store_sem.at[0])
    store_out.start()
    by_core(lambda: zstep(3), lambda: xfinal(1))
    xstep(0)
    conv_back([(0, 1), (9, 1)])
    pl.when(core == 0)(lambda: zstep(4))
    clear_outside(hg3)

    total = dot_nt(hg3[2 * COLS : 2 * COLS + OWN, :], w1t[0])
    total += dot_nt(hg3[COLS : COLS + OWN, :], w1t[1])
    total += dot_nt(hg3[0:OWN, :], w1t[2])
    acc[0:OWN, :] = total

    def finish_latent(k, _):
        at = pl.ds(pl.multiple_of(k * COLS, COLS), COLS)
        value = latx[pl.ds(pl.multiple_of((k + 2) * COLS, COLS), COLS), :].astype(F32)
        sig = jax.nn.sigmoid(value)
        lgv[at, :] = (acc[at, :] * (sig * (1.0 + value * (1.0 - sig)))).astype(BF)
        return 0

    lax.fori_loop(0, 8, finish_latent, 0)
    store_lg = pltpu.make_async_copy(lgv, lg_hbm, store_sem.at[1])
    store_lg.start()
    by_core(zfinal, lambda: y_finish(1))
    xfinal(0)

    @pl.when(space > 0)
    def _():
        for to_up, _d in halos:
            to_up.wait_send()

    @pl.when(space < 31)
    def _():
        for _u, to_down in halos:
            to_down.wait_send()

    for n in range(2):
        for r in range(5):
            core_copy(n, r).wait_send()

    def sent_x(n):
        for way in range(2):
            for part in (1, 2, 3):
                xcopy(n, part, way).wait_send()

    def sent_z():
        for way in range(2):
            for step in range(1, 5):
                zcopy(step, way).wait_send()

    sent_x(0)
    by_core(sent_z, lambda: sent_x(1))
    store_out.wait()
    store_lg.wait()
    pl.when(core == 0)(lambda: late_finish(1))
    middle(0)

    def sent(copy):
        for n in range(2):
            for d in range(1, 8):
                copy(n, d).wait_send()

    @pl.when(core == 0)
    def _():
        for d in range(1, 8):
            z_direct(0, d).wait_send()
        for d in range(1, 4):
            x_direct(d).wait_send()

    @pl.when(core == 1)
    def _():
        sent(y_direct)

    last(1, g2_ref)
    last(0, g1_ref)

    @pl.when(core == 0)
    def _():
        sent(lambda n, d: last_copy(n, d, True))

    @pl.when(core == 1)
    def _():
        sent(lambda n, d: last_copy(n, d, False))


def finish_kernel(out_hbm, lg_hbm, g1_hbm, g2_hbm, out_res, lg_res, f1_res, f2_res, buf, share, f1, f2, sem_in, sem_out):
    shares = [
        pltpu.make_async_copy(g1_hbm, share.at[0], sem_in.at[2, 0]),
        pltpu.make_async_copy(g2_hbm, share.at[1], sem_in.at[2, 1]),
    ]
    flats = [
        pltpu.make_async_copy(f1, f1_res, sem_out.at[2, 0]),
        pltpu.make_async_copy(f2, f2_res, sem_out.at[2, 1]),
    ]
    for copy in shares:
        copy.start()
    takes, puts = [], []
    for n, (src, dst) in enumerate(((out_hbm, out_res), (lg_hbm, lg_res))):
        for k in range(2):
            at = pl.ds(k * OWN // 2, OWN // 2)
            takes.append(pltpu.make_async_copy(src.at[at], buf.at[n, at], sem_in.at[n, k]))
            puts.append(pltpu.make_async_copy(buf.at[n, at], dst.at[at], sem_out.at[n, k]))
    for take in takes:
        take.start()
    for copy in shares:
        copy.wait()
    lane = lax.broadcasted_iota(jnp.int32, (1, 128), 1)
    for n, dst in enumerate((f1, f2)):
        src = share.at[n]
        for k in range(15):
            start, end = 128 * k, min(128 * k + 128, 5 * UNIT)
            size, value, at = end - start, None, start
            while at < end:
                row, col = divmod(at, UNIT)
                base = min(col // 128 * 128, LANES - 256)
                piece = src[row : row + 1, base : base + 256]
                shift = (at - start - (col - base)) % 256
                if shift:
                    piece = pltpu.roll(piece, shift, 1)
                piece = piece[:, :128]
                value = piece if value is None else jnp.where(lane < at - start, value, piece)
                at += min(UNIT - col, end - at)
            dst[pl.ds(start, size)] = value[0, :size]
        flats[n].start()
    for take, put in zip(takes, puts):
        take.wait()
        put.start()
    for copy in puts + flats:
        copy.wait()


def local(latent, first_weight, second_weight, cotangent):
    def taps(weight):
        return jnp.transpose(weight, (1, 2, 0, 3)).reshape(3, 3 * CH, CH)

    any_spec = pl.BlockSpec(memory_space=pl.ANY)
    vmem_spec = pl.BlockSpec(memory_space=pltpu.VMEM)
    dma = pltpu.SemaphoreType.DMA
    out, latent_grad, first, second = pl.pallas_call(
        kernel,
        out_shape=(
            jax.ShapeDtypeStruct((OWN, CH), BF),
            jax.ShapeDtypeStruct((OWN, CH), BF),
            jax.ShapeDtypeStruct((8, LANES), F32),
            jax.ShapeDtypeStruct((8, LANES), F32),
        ),
        in_specs=[any_spec] * 4,
        out_specs=(any_spec, any_spec, vmem_spec, vmem_spec),
        scratch_shapes=[
            pltpu.VMEM((EXT, CH), BF),
            pltpu.VMEM((EXT, CH), BF),
            pltpu.VMEM((EXT, CH), BF),
            pltpu.VMEM((EXT, 3 * CH), BF),
            pltpu.VMEM((EXT, 3 * CH), BF),
            pltpu.VMEM((3, 3 * CH, CH), BF),
            pltpu.VMEM((3, 3 * CH, CH), BF),
            pltpu.VMEM((3, CH, 3 * CH), BF),
            pltpu.VMEM((3, CH, 3 * CH), BF),
            pltpu.VMEM((MID, CH), F32),
            pltpu.VMEM((MID, CH), F32),
            pltpu.VMEM((MID, 3 * CH), BF),
            pltpu.VMEM((MID, 3 * CH), BF),
            pltpu.VMEM((3, CH, 1024), F32),
            pltpu.VMEM((CH, CH), BF),
            pltpu.VMEM((CH, OWN), BF),
            pltpu.VMEM((CH, OWN), BF),
            pltpu.VMEM((2, UNITS, 8, 8, LANES), BF),
            pltpu.VMEM((2, UNITS, 4, 8, LANES), BF),
            pltpu.VMEM((2, 4, 2, 4, 5, 8, LANES), BF),
            pltpu.VMEM((2, 4, 4, 5, 8, LANES), BF),
            pltpu.VMEM((2, 2, 2, 4, 2, 5, 8, LANES), BF),
            pltpu.VMEM((2, 7, 5, 8, LANES), BF),
            pltpu.VMEM((2, 8, 40, LANES), BF),
            pltpu.VMEM((2, 7, 40, LANES), BF),
            pltpu.VMEM((3, 320, 128), F32),
            pltpu.VMEM((2, 8, 8, LANES), BF),
            pltpu.VMEM((2, 7, 8, LANES), BF),
            pltpu.VMEM((OWN, CH), BF),
            pltpu.VMEM((OWN, CH), BF),
            dma((4,)),
            dma((4,)),
            dma((4,)),
            dma((2, 5)),
            dma((2, 5)),
            dma((2, 4)),
            dma((2, 4)),
            dma((2, 2, 3)),
            dma((2, 2, 3)),
            dma((2, 7)),
            dma((2, 7)),
            dma((2, 7)),
            dma((2, 7)),
            dma((2,)),
        ],
        compiler_params=pltpu.CompilerParams(
            collective_id=0, has_side_effects=True, vmem_limit_bytes=60 * 1024 * 1024
        ),
        name="conv_pair",
    )(
        latent.reshape(OWN, CH), taps(first_weight), taps(second_weight), cotangent.reshape(OWN, CH)
    )
    out, latent_grad, first, second = pl.pallas_call(
        finish_kernel,
        out_shape=(
            jax.ShapeDtypeStruct((OWN, CH), BF),
            jax.ShapeDtypeStruct((OWN, CH), BF),
            jax.ShapeDtypeStruct((5 * UNIT,), F32),
            jax.ShapeDtypeStruct((5 * UNIT,), F32),
        ),
        in_specs=[any_spec] * 4,
        out_specs=(any_spec,) * 4,
        scratch_shapes=[
            pltpu.VMEM((2, OWN, CH), BF),
            pltpu.VMEM((2, 8, LANES), F32),
            pltpu.VMEM((5 * UNIT,), F32),
            pltpu.VMEM((5 * UNIT,), F32),
            dma((3, 2)),
            dma((3, 2)),
        ],
        name="finish",
    )(out, latent_grad, first, second)
    return (
        out.reshape(1, ROWS, COLS, CH),
        latent_grad.reshape(1, ROWS, COLS, CH),
        first,
        second,
    )


def solution(mesh):
    placed = (P("dp", "space", None, None), P(), P(), P("dp", "space", None, None))
    return jax.shard_map(
        local,
        mesh=mesh,
        in_specs=placed,
        out_specs=(
            P("dp", "space", None, None),
            P("dp", "space", None, None),
            P(("dp", "space")),
            P(("dp", "space")),
        ),
        check_vma=False,
    )
```

```python
import jax
import jax.numpy as jnp
from jax import lax
from jax.experimental import pallas as pl
from jax.experimental.pallas import tpu as pltpu
from jax.sharding import PartitionSpec as P

BF = jnp.bfloat16
F32 = jnp.float32
MESH = pl.DeviceIdType.MESH
COLS = 64
CH = 320
ROWS = 8
OWN = ROWS * COLS
EXT = (ROWS + 4) * COLS
MID = (ROWS + 2) * COLS
NT = (((1,), (1,)), ((), ()))
UNIT = 360
LANES = 384
UNITS = 40
FAR_FIRST = (4, 3, 5, 2, 6, 1, 7)


def dot(a, b):
    return jnp.dot(a, b, preferred_element_type=F32)


def dot_nt(a, b):
    return lax.dot_general(a, b, NT, preferred_element_type=F32)


def column_shifts(value):
    count = value.shape[0]
    col = lax.broadcasted_iota(jnp.int32, value.shape, 0) % COLS
    before = jnp.where(col == 0, 0.0, pltpu.roll(value, 1, 0))
    after = jnp.where(col == COLS - 1, 0.0, pltpu.roll(value, count - 1, 0))
    return before.astype(BF), value.astype(BF), after.astype(BF)


def unit_pieces(u):
    pieces = []
    start, left, lane = UNIT * u, UNIT, 0
    while left:
        tap, col = divmod(start, 3 * CH)
        size = min(left, 3 * CH - col)
        pieces.append((tap, col, size, lane))
        start, left, lane = start + size, left - size, lane + size
    return pieces


def kernel(
    lat_hbm, w1_hbm, w2_hbm, cot_hbm, out_hbm, lg_hbm, g1_ref, g2_ref,
    latx, cotx, act, a3, c3, w1, w2, w1t, w2t, acc, slope, h3, hg3, terms, perm, lhs_t, mid_t,
    grid, core_recv, sums, zrecv, xrecv, late, mids, midr, sc, ys, yr, outv, lgv,
    load_sem, halo_send, halo_recv, core_send, core_rsem, zsend, zrsem, xsend, xrsem, lsend, lrsem, ysend, yrsem, store_sem,
):
    dp, space = lax.axis_index("dp"), lax.axis_index("space")
    yy, core = dp // 2, dp % 2
    zz, xx = space // 4, space % 4
    up, down = (space + 31) % 32, (space + 1) % 32

    loads = [
        pltpu.make_async_copy(lat_hbm, latx.at[pl.ds(2 * COLS, OWN)], load_sem.at[0]),
        pltpu.make_async_copy(cot_hbm, cotx.at[pl.ds(2 * COLS, OWN)], load_sem.at[1]),
        pltpu.make_async_copy(w1_hbm, w1, load_sem.at[2]),
        pltpu.make_async_copy(w2_hbm, w2, load_sem.at[3]),
    ]
    for load in loads:
        load.start()

    peers = [(dp, up), (dp, down), (yy * 2 + 1 - core, space)]
    peers += [(dp, (zz + k) % 8 * 4 + xx) for k in range(1, 8)]
    peers += [(dp, zz * 4 + (xx + k) % 4) for k in (1, 2, 3)]
    peers += [((yy + k) % 8 * 2 + core, space) for k in range(1, 8)]
    barrier = pltpu.get_barrier_semaphore()
    for peer in peers:
        pl.semaphore_signal(barrier, inc=1, device_id=peer, device_id_type=MESH)

    def widen(src, dst, first, last, flip, activate):
        def group(k, _):
            at = pl.ds(pl.multiple_of(k * COLS, COLS), COLS)
            value = src[at, :].astype(F32)
            if activate:
                value = value * jax.nn.sigmoid(value)
                act[at, :] = value.astype(BF)
            one, two, three = column_shifts(value)
            dst[at, :] = jnp.concatenate([three, two, one] if flip else [one, two, three], axis=1)
            return 0
        lax.fori_loop(first, last, group, 0)

    loads[0].wait()
    widen(latx, a3, 2, 10, False, True)
    loads[1].wait()
    widen(cotx, c3, 2, 10, True, False)

    pl.semaphore_wait(barrier, len(peers))
    halos = []
    for n, (src, dst) in enumerate(((lat_hbm, latx), (cot_hbm, cotx))):
        to_up = pltpu.make_async_remote_copy(
            src_ref=src.at[pl.ds(0, 2 * COLS)], dst_ref=dst.at[pl.ds(10 * COLS, 2 * COLS)],
            send_sem=halo_send.at[2 * n], recv_sem=halo_recv.at[2 * n],
            device_id=(dp, up), device_id_type=MESH)
        to_down = pltpu.make_async_remote_copy(
            src_ref=src.at[pl.ds(6 * COLS, 2 * COLS)], dst_ref=dst.at[pl.ds(0, 2 * COLS)],
            send_sem=halo_send.at[2 * n + 1], recv_sem=halo_recv.at[2 * n + 1],
            device_id=(dp, down), device_id_type=MESH)
        halos.append((to_up, to_down))

    @pl.when(space > 0)
    def _():
        for to_up, _d in halos:
            to_up.start()

    @pl.when(space < 31)
    def _():
        for _u, to_down in halos:
            to_down.start()

    shape = (CH, CH)
    row = lax.broadcasted_iota(jnp.int32, shape, 0)
    chan = lax.broadcasted_iota(jnp.int32, shape, 1)
    group = ((row % 8) * 2 + row // 32 % 2) * 4 + row // 8 % 4
    perm[...] = jnp.where(chan == 5 * group + row // 64, 1.0, 0.0).astype(BF)
    lhs_t[...] = dot_nt(perm[...], cotx[2 * COLS : 10 * COLS, :]).astype(BF)
    mid_t[...] = dot_nt(perm[...], act[2 * COLS : 10 * COLS, :]).astype(BF)

    loads[2].wait()

    def conv_one(runs):
        def rows(i):
            parts = [a3[(first + i) * COLS : (first + count + i) * COLS, :] for first, count in runs]
            return parts[0] if len(parts) == 1 else jnp.concatenate(parts, axis=0)

        total = dot(rows(0), w1[0])
        total += dot(rows(1), w1[1])
        total += dot(rows(2), w1[2])
        at = 0
        for first, count in runs:
            acc[first * COLS : (first + count) * COLS, :] = total[at : at + count * COLS]
            at += count * COLS

        def finish(k, _):
            at = pl.ds(pl.multiple_of(k * COLS, COLS), COLS)
            hidden = acc[at, :].astype(BF).astype(F32)
            sig = jax.nn.sigmoid(hidden)
            slope[at, :] = sig * (1.0 + hidden * (1.0 - sig))
            h3[at, :] = jnp.concatenate(column_shifts(hidden * sig), axis=1)
            return 0

        for first, count in runs:
            lax.fori_loop(first, first + count, finish, 0)

    conv_one([(2, 6)])
    ys[...] = jnp.zeros(ys.shape, BF)
    for i in range(3):
        terms[i, :, 3 * CH :] = jnp.zeros((CH, 64), F32)

    @pl.when(space == 0)
    def _():
        latx[0 : 2 * COLS, :] = jnp.zeros((2 * COLS, CH), BF)
        cotx[0 : 2 * COLS, :] = jnp.zeros((2 * COLS, CH), BF)

    @pl.when(space == 31)
    def _():
        latx[10 * COLS :, :] = jnp.zeros((2 * COLS, CH), BF)
        cotx[10 * COLS :, :] = jnp.zeros((2 * COLS, CH), BF)

    @pl.when(space < 31)
    def _():
        for to_up, _d in halos:
            to_up.wait_recv()

    @pl.when(space > 0)
    def _():
        for _u, to_down in halos:
            to_down.wait_recv()

    for first in (0, 10):
        widen(latx, a3, first, first + 2, False, True)
        widen(cotx, c3, first, first + 2, True, False)
    conv_one([(0, 2), (8, 2)])

    def clear_outside(ref):
        @pl.when(space == 0)
        def _():
            ref[0:COLS, :] = jnp.zeros((COLS, 3 * CH), BF)

        @pl.when(space == 31)
        def _():
            ref[9 * COLS :, :] = jnp.zeros((COLS, 3 * CH), BF)

    clear_outside(h3)

    other = (yy * 2 + 1 - core, space)

    def core_copy(n, r):
        return pltpu.make_async_remote_copy(
            src_ref=grid.at[n, pl.ds(8 * r, 8), pl.ds(4 * (1 - core), 4)],
            dst_ref=core_recv.at[n, pl.ds(8 * r, 8)],
            send_sem=core_send.at[n, r], recv_sem=core_rsem.at[n, r],
            device_id=other, device_id_type=MESH)

    def pack_terms(n):
        lane = lax.broadcasted_iota(jnp.int32, (64, LANES), 1)
        for r in range(5):
            for u in range(8):
                value = None
                for tap, col, size, put in unit_pieces(u):
                    base = min(col // 128 * 128, 1024 - LANES)
                    width = -(-max(col - base + size, LANES) // 128) * 128
                    shift = (put - (col - base)) % width
                    piece = terms[tap, 64 * r : 64 * r + 64, base : base + width]
                    if shift:
                        piece = pltpu.roll(piece, shift, 1)
                    piece = piece[:, :LANES]
                    value = piece if value is None else jnp.where(lane < put, value, piece)
                grid[n, 8 * r + u] = value.reshape(8, 8, LANES).astype(BF)
            core_copy(n, r).start()

    def core_sum(n):
        for r in range(5):
            core_copy(n, r).wait_recv()
        for k in range(4):
            part = grid[n, :, 4 * core + k].astype(F32) + core_recv[n, :, k].astype(F32)
            sums[n, k] = part.reshape(2, 4, 5, 8, LANES).astype(BF)

    def xcopy(n, part, way):
        step = 1 if way == 0 else 3
        target = (xx + (2 * step if part == 1 else step)) % 4
        lo = 2 * way if part < 3 else 2 - 2 * way
        return pltpu.make_async_remote_copy(
            src_ref=sums.at[n, pl.ds(lo, 2), :, target],
            dst_ref=xrecv.at[n, way, min(part, 2) - 1, pl.ds(lo, 2)],
            send_sem=xsend.at[n, way, part - 1], recv_sem=xrsem.at[n, way, part - 1],
            device_id=(dp, zz * 4 + (xx + step) % 4), device_id_type=MESH)

    def xstart(n):
        for part in (1, 3):
            for way in range(2):
                xcopy(n, part, way).start()

    def xstep(n):
        for way in range(2):
            xcopy(n, 1, way).wait_recv()
            lo = 2 * way
            ref = sums.at[n, pl.ds(lo, 2), :, (xx + (1 if way == 0 else 3)) % 4]
            ref[...] = (ref[...].astype(F32) + xrecv[n, way, 0, lo : lo + 2].astype(F32)).astype(BF)
            xcopy(n, 2, way).start()

    steps = (1, 7)

    def zblock(target, way, half):
        lo, size = (2 * way, 2) if half else (0, 4)
        return sums.at[1, target // 2, target % 2, pl.ds(lo, size)]

    def zcopy(step, way):
        target = (zz + steps[way] * (5 - step)) % 8
        lo, size = (2 * way, 2) if step == 1 else (0, 4)
        return pltpu.make_async_remote_copy(
            src_ref=zblock(target, way, step == 1), dst_ref=zrecv.at[way, step - 1, pl.ds(lo, size)],
            send_sem=zsend.at[way, step - 1], recv_sem=zrsem.at[way, step - 1],
            device_id=(dp, (zz + steps[way]) % 8 * 4 + xx), device_id_type=MESH)

    def zstep(step):
        for way in range(2):
            if step >= 2:
                zcopy(step - 1, way).wait_recv()
                ref = zblock((zz + steps[way] * (5 - step)) % 8, way, step == 2)
                lo, size = (2 * way, 2) if step == 2 else (0, 4)
                ref[...] = (ref[...].astype(F32) + zrecv[way, step - 2, lo : lo + size].astype(F32)).astype(BF)
            zcopy(step, way).start()

    def x_direct(d):
        to = (xx + d) % 4
        return pltpu.make_async_remote_copy(
            src_ref=sums.at[1, zz // 2, zz % 2, to], dst_ref=late.at[1, d - 1],
            send_sem=lsend.at[1, d - 1], recv_sem=lrsem.at[1, d - 1],
            device_id=(dp, zz * 4 + to), device_id_type=MESH)

    def zfinal():
        for way in range(2):
            zcopy(4, way).wait_recv()
        ref = sums.at[1, zz // 2, zz % 2]
        ref[...] = (ref[...].astype(F32) + zrecv[0, 3].astype(F32) + zrecv[1, 3].astype(F32)).astype(BF)
        for d in (2, 1, 3):
            x_direct(d).start()

    def z_direct(n, d):
        to = (zz + d) % 8
        return pltpu.make_async_remote_copy(
            src_ref=sums.at[n, to // 2, to % 2, xx], dst_ref=late.at[n, d - 1],
            send_sem=lsend.at[n, d - 1], recv_sem=lrsem.at[n, d - 1],
            device_id=(dp, to * 4 + xx), device_id_type=MESH)

    def y_direct(n, d):
        to = (yy + d) % 8
        return pltpu.make_async_remote_copy(
            src_ref=mids.at[n, to], dst_ref=midr.at[n, d - 1],
            send_sem=lsend.at[n, d - 1], recv_sem=lrsem.at[n, d - 1],
            device_id=(to * 2 + core, space), device_id_type=MESH)

    def xfinal(n):
        for way in range(2):
            for part in (2, 3):
                xcopy(n, part, way).wait_recv()

        @pl.when(core == 0)
        def _():
            ref = sums.at[n, :, :, xx]
            ref[...] = (ref[...].astype(F32) + xrecv[n, 0, 1].astype(F32) + xrecv[n, 1, 1].astype(F32)).astype(BF)
            for d in FAR_FIRST:
                z_direct(n, d).start()

        @pl.when(core == 1)
        def _():
            total = sums[n, :, :, xx].astype(F32) + xrecv[n, 0, 1].astype(F32) + xrecv[n, 1, 1].astype(F32)
            flat = total.reshape(40 * 8, LANES)
            for k in range(3):
                sc[k] = flat[:, 128 * k : 128 * k + 128]
            for to in range(8):
                for k in range(3):
                    mids[n, to, :, 128 * k : 128 * k + 128] = sc[k, pl.ds(to, 40, stride=8), :].astype(BF)
            for d in FAR_FIRST:
                y_direct(n, d).start()

    def last_copy(n, d, over_y):
        if over_y:
            to = (yy + d) % 8
            device = (to * 2 + core, space)
        else:
            to = (zz + d) % 8
            device = (dp, to * 4 + xx)
        return pltpu.make_async_remote_copy(
            src_ref=ys.at[n, to], dst_ref=yr.at[n, d - 1],
            send_sem=ysend.at[n, d - 1], recv_sem=yrsem.at[n, d - 1],
            device_id=device, device_id_type=MESH)

    def late_finish(n):
        total = sums[n, zz // 2, zz % 2, xx].astype(F32)
        for d in range(1, 4 if n else 8):
            (x_direct(d) if n else z_direct(n, d)).wait_recv()
            total += late[n, d - 1].astype(F32)
        flat = total.reshape(5 * 8, LANES)
        for k in range(3):
            sc[k, 0:40] = flat[:, 128 * k : 128 * k + 128]
        for to in range(8):
            for k in range(3):
                ys[n, to, 0:5, 128 * k : 128 * k + 128] = sc[k, pl.ds(to, 5, stride=8), :].astype(BF)
        for d in FAR_FIRST:
            last_copy(n, d, True).start()

    def y_finish(n):
        total = mids[n, yy].astype(F32)
        for d in range(1, 8):
            y_direct(n, d).wait_recv()
            total += midr[n, d - 1].astype(F32)
        for k in range(3):
            sc[k, 0:40] = total[:, 128 * k : 128 * k + 128]
        for to in range(8):
            for k in range(3):
                ys[n, to, 0:5, 128 * k : 128 * k + 128] = sc[k, 5 * to : 5 * to + 5, :].astype(BF)
        for d in FAR_FIRST:
            last_copy(n, d, False).start()

    def last(n, ref):
        def total_over(over_y):
            total = ys[n, yy if over_y else zz].astype(F32)
            for d in range(1, 8):
                last_copy(n, d, over_y).wait_recv()
                total += yr[n, d - 1].astype(F32)
            ref[...] = total

        @pl.when(core == 0)
        def _():
            total_over(True)

        @pl.when(core == 1)
        def _():
            total_over(False)

    def by_core(zero, one):
        pl.when(core == 0)(zero)
        pl.when(core == 1)(one)

    def middle(n):
        @pl.when(core == 0)
        def _():
            late_finish(n)

        @pl.when(core == 1)
        def _():
            y_finish(n)

    for i in range(3):
        terms[i, :, : 3 * CH] = dot(lhs_t[...], h3[i * COLS : i * COLS + OWN, :])
    pack_terms(1)

    loads[3].wait()
    def conv_back(runs):
        def rows(i):
            parts = [c3[(first + i) * COLS : (first + count + i) * COLS, :] for first, count in runs]
            return parts[0] if len(parts) == 1 else jnp.concatenate(parts, axis=0)

        total = dot(rows(2), w2[0])
        total += dot(rows(1), w2[1])
        total += dot(rows(0), w2[2])
        at = 0
        for first, count in runs:
            acc[first * COLS : (first + count) * COLS, :] = total[at : at + count * COLS]
            at += count * COLS

        def finish(k, _):
            at = pl.ds(pl.multiple_of(k * COLS, COLS), COLS)
            before, here, after = column_shifts(acc[at, :] * slope[at, :])
            hg3[at, :] = jnp.concatenate([after, here, before], axis=1)
            return 0

        for first, count in runs:
            lax.fori_loop(first, first + count, finish, 0)

    conv_back([(1, 8)])

    core_sum(1)
    by_core(lambda: zstep(1), lambda: xstart(1))

    for i in range(3):
        if i != 1:
            lhs_t[...] = dot_nt(perm[...], act[(i + 1) * COLS : (i + 1) * COLS + OWN, :]).astype(BF)
        left = mid_t if i == 1 else lhs_t
        terms[i, :, : 3 * CH] = dot(left[...], hg3[COLS : COLS + OWN, :])
    pack_terms(0)
    by_core(lambda: zstep(2), lambda: xstep(1))

    core_sum(0)
    xstart(0)

    for i in range(3):
        w2t[i] = jnp.concatenate([w2[i, CH * j : CH * j + CH, :] for j in range(3)], axis=1)
        w1t[i] = jnp.concatenate([w1[i, CH * j : CH * j + CH, :] for j in range(3)], axis=1)

    total = dot_nt(h3[0:OWN, :], w2t[0])
    total += dot_nt(h3[COLS : COLS + OWN, :], w2t[1])
    total += dot_nt(h3[2 * COLS : 2 * COLS + OWN, :], w2t[2])
    outv[...] = total.astype(BF)
    store_out = pltpu.make_async_copy(outv, out_hbm, store_sem.at[0])
    store_out.start()
    by_core(lambda: zstep(3), lambda: xfinal(1))
    xstep(0)
    conv_back([(0, 1), (9, 1)])
    pl.when(core == 0)(lambda: zstep(4))
    clear_outside(hg3)

    total = dot_nt(hg3[2 * COLS : 2 * COLS + OWN, :], w1t[0])
    total += dot_nt(hg3[COLS : COLS + OWN, :], w1t[1])
    total += dot_nt(hg3[0:OWN, :], w1t[2])
    acc[0:OWN, :] = total

    def finish_latent(k, _):
        at = pl.ds(pl.multiple_of(k * COLS, COLS), COLS)
        value = latx[pl.ds(pl.multiple_of((k + 2) * COLS, COLS), COLS), :].astype(F32)
        sig = jax.nn.sigmoid(value)
        lgv[at, :] = (acc[at, :] * (sig * (1.0 + value * (1.0 - sig)))).astype(BF)
        return 0

    lax.fori_loop(0, 8, finish_latent, 0)
    store_lg = pltpu.make_async_copy(lgv, lg_hbm, store_sem.at[1])
    store_lg.start()
    by_core(zfinal, lambda: y_finish(1))
    xfinal(0)

    @pl.when(space > 0)
    def _():
        for to_up, _d in halos:
            to_up.wait_send()

    @pl.when(space < 31)
    def _():
        for _u, to_down in halos:
            to_down.wait_send()

    for n in range(2):
        for r in range(5):
            core_copy(n, r).wait_send()

    def sent_x(n):
        for way in range(2):
            for part in (1, 2, 3):
                xcopy(n, part, way).wait_send()

    def sent_z():
        for way in range(2):
            for step in range(1, 5):
                zcopy(step, way).wait_send()

    sent_x(0)
    by_core(sent_z, lambda: sent_x(1))
    store_out.wait()
    store_lg.wait()
    pl.when(core == 0)(lambda: late_finish(1))
    middle(0)

    def sent(copy):
        for n in range(2):
            for d in range(1, 8):
                copy(n, d).wait_send()

    @pl.when(core == 0)
    def _():
        for d in range(1, 8):
            z_direct(0, d).wait_send()
        for d in range(1, 4):
            x_direct(d).wait_send()

    @pl.when(core == 1)
    def _():
        sent(y_direct)

    last(1, g2_ref)
    last(0, g1_ref)

    @pl.when(core == 0)
    def _():
        sent(lambda n, d: last_copy(n, d, True))

    @pl.when(core == 1)
    def _():
        sent(lambda n, d: last_copy(n, d, False))


def finish_kernel(out_hbm, lg_hbm, g1_hbm, g2_hbm, out_res, lg_res, f1_res, f2_res, buf, share, f1, f2, sem_in, sem_out):
    shares = [
        pltpu.make_async_copy(g1_hbm, share.at[0], sem_in.at[2, 0]),
        pltpu.make_async_copy(g2_hbm, share.at[1], sem_in.at[2, 1]),
    ]
    flats = [
        pltpu.make_async_copy(f1, f1_res, sem_out.at[2, 0]),
        pltpu.make_async_copy(f2, f2_res, sem_out.at[2, 1]),
    ]
    for copy in shares:
        copy.start()
    takes, puts = [], []
    for n, (src, dst) in enumerate(((out_hbm, out_res), (lg_hbm, lg_res))):
        for k in range(2):
            at = pl.ds(k * OWN // 2, OWN // 2)
            takes.append(pltpu.make_async_copy(src.at[at], buf.at[n, at], sem_in.at[n, k]))
            puts.append(pltpu.make_async_copy(buf.at[n, at], dst.at[at], sem_out.at[n, k]))
    for take in takes:
        take.start()
    for copy in shares:
        copy.wait()
    lane = lax.broadcasted_iota(jnp.int32, (1, 128), 1)
    for n, dst in enumerate((f1, f2)):
        src = share.at[n]
        for k in range(15):
            start, end = 128 * k, min(128 * k + 128, 5 * UNIT)
            size, value, at = end - start, None, start
            while at < end:
                row, col = divmod(at, UNIT)
                base = min(col // 128 * 128, LANES - 256)
                piece = src[row : row + 1, base : base + 256]
                shift = (at - start - (col - base)) % 256
                if shift:
                    piece = pltpu.roll(piece, shift, 1)
                piece = piece[:, :128]
                value = piece if value is None else jnp.where(lane < at - start, value, piece)
                at += min(UNIT - col, end - at)
            dst[pl.ds(start, size)] = value[0, :size]
        flats[n].start()
    for take, put in zip(takes, puts):
        take.wait()
        put.start()
    for copy in puts + flats:
        copy.wait()


def local(latent, first_weight, second_weight, cotangent):
    def taps(weight):
        return jnp.transpose(weight, (1, 2, 0, 3)).reshape(3, 3 * CH, CH)

    any_spec = pl.BlockSpec(memory_space=pl.ANY)
    vmem_spec = pl.BlockSpec(memory_space=pltpu.VMEM)
    dma = pltpu.SemaphoreType.DMA
    out, latent_grad, first, second = pl.pallas_call(
        kernel,
        out_shape=(
            jax.ShapeDtypeStruct((OWN, CH), BF),
            jax.ShapeDtypeStruct((OWN, CH), BF),
            jax.ShapeDtypeStruct((8, LANES), F32),
            jax.ShapeDtypeStruct((8, LANES), F32),
        ),
        in_specs=[any_spec] * 4,
        out_specs=(any_spec, any_spec, vmem_spec, vmem_spec),
        scratch_shapes=[
            pltpu.VMEM((EXT, CH), BF),
            pltpu.VMEM((EXT, CH), BF),
            pltpu.VMEM((EXT, CH), BF),
            pltpu.VMEM((EXT, 3 * CH), BF),
            pltpu.VMEM((EXT, 3 * CH), BF),
            pltpu.VMEM((3, 3 * CH, CH), BF),
            pltpu.VMEM((3, 3 * CH, CH), BF),
            pltpu.VMEM((3, CH, 3 * CH), BF),
            pltpu.VMEM((3, CH, 3 * CH), BF),
            pltpu.VMEM((MID, CH), F32),
            pltpu.VMEM((MID, CH), F32),
            pltpu.VMEM((MID, 3 * CH), BF),
            pltpu.VMEM((MID, 3 * CH), BF),
            pltpu.VMEM((3, CH, 1024), F32),
            pltpu.VMEM((CH, CH), BF),
            pltpu.VMEM((CH, OWN), BF),
            pltpu.VMEM((CH, OWN), BF),
            pltpu.VMEM((2, UNITS, 8, 8, LANES), BF),
            pltpu.VMEM((2, UNITS, 4, 8, LANES), BF),
            pltpu.VMEM((2, 4, 2, 4, 5, 8, LANES), BF),
            pltpu.VMEM((2, 4, 4, 5, 8, LANES), BF),
            pltpu.VMEM((2, 2, 2, 4, 2, 5, 8, LANES), BF),
            pltpu.VMEM((2, 7, 5, 8, LANES), BF),
            pltpu.VMEM((2, 8, 40, LANES), BF),
            pltpu.VMEM((2, 7, 40, LANES), BF),
            pltpu.VMEM((3, 320, 128), F32),
            pltpu.VMEM((2, 8, 8, LANES), BF),
            pltpu.VMEM((2, 7, 8, LANES), BF),
            pltpu.VMEM((OWN, CH), BF),
            pltpu.VMEM((OWN, CH), BF),
            dma((4,)),
            dma((4,)),
            dma((4,)),
            dma((2, 5)),
            dma((2, 5)),
            dma((2, 4)),
            dma((2, 4)),
            dma((2, 2, 3)),
            dma((2, 2, 3)),
            dma((2, 7)),
            dma((2, 7)),
            dma((2, 7)),
            dma((2, 7)),
            dma((2,)),
        ],
        compiler_params=pltpu.CompilerParams(
            collective_id=0, has_side_effects=True, vmem_limit_bytes=60 * 1024 * 1024
        ),
        name="conv_pair",
    )(
        latent.reshape(OWN, CH), taps(first_weight), taps(second_weight), cotangent.reshape(OWN, CH)
    )
    out, latent_grad, first, second = pl.pallas_call(
        finish_kernel,
        out_shape=(
            jax.ShapeDtypeStruct((OWN, CH), BF),
            jax.ShapeDtypeStruct((OWN, CH), BF),
            jax.ShapeDtypeStruct((5 * UNIT,), F32),
            jax.ShapeDtypeStruct((5 * UNIT,), F32),
        ),
        in_specs=[any_spec] * 4,
        out_specs=(any_spec,) * 4,
        scratch_shapes=[
            pltpu.VMEM((2, OWN, CH), BF),
            pltpu.VMEM((2, 8, LANES), F32),
            pltpu.VMEM((5 * UNIT,), F32),
            pltpu.VMEM((5 * UNIT,), F32),
            dma((3, 2)),
            dma((3, 2)),
        ],
        name="finish",
    )(out, latent_grad, first, second)
    return (
        out.reshape(1, ROWS, COLS, CH),
        latent_grad.reshape(1, ROWS, COLS, CH),
        first,
        second,
    )


def solution(mesh):
    placed = (P("dp", "space", None, None), P(), P(), P("dp", "space", None, None))
    return jax.shard_map(
        local,
        mesh=mesh,
        in_specs=placed,
        out_specs=(
            P("dp", "space", None, None),
            P("dp", "space", None, None),
            P(("dp", "space")),
            P(("dp", "space")),
        ),
        check_vma=False,
    )
```

```python
import jax
import jax.numpy as jnp
from jax import lax
from jax.experimental import pallas as pl
from jax.experimental.pallas import tpu as pltpu
from jax.sharding import PartitionSpec as P

BF = jnp.bfloat16
F32 = jnp.float32
MESH = pl.DeviceIdType.MESH
COLS = 64
CH = 320
ROWS = 8
OWN = ROWS * COLS
EXT = (ROWS + 4) * COLS
MID = (ROWS + 2) * COLS
NT = (((1,), (1,)), ((), ()))
UNIT = 360
LANES = 384
UNITS = 40
FAR_FIRST = (4, 3, 5, 2, 6, 1, 7)


def dot(a, b):
    return jnp.dot(a, b, preferred_element_type=F32)


def dot_nt(a, b):
    return lax.dot_general(a, b, NT, preferred_element_type=F32)


def column_shifts(value):
    count = value.shape[0]
    col = lax.broadcasted_iota(jnp.int32, value.shape, 0) % COLS
    before = jnp.where(col == 0, 0.0, pltpu.roll(value, 1, 0))
    after = jnp.where(col == COLS - 1, 0.0, pltpu.roll(value, count - 1, 0))
    return before.astype(BF), value.astype(BF), after.astype(BF)


def unit_pieces(u):
    pieces = []
    start, left, lane = UNIT * u, UNIT, 0
    while left:
        tap, col = divmod(start, 3 * CH)
        size = min(left, 3 * CH - col)
        pieces.append((tap, col, size, lane))
        start, left, lane = start + size, left - size, lane + size
    return pieces


def kernel(
    lat_hbm, w1_hbm, w2_hbm, cot_hbm, out_hbm, lg_hbm, g1_ref, g2_ref,
    latx, cotx, act, a3, c3, w1, w2, w1t, w2t, acc, slope, h3, hg3, terms, perm, lhs_t, mid_t,
    grid, core_recv, sums, zrecv, xrecv, late, mids, midr, sc, ys, yr, outv, lgv,
    load_sem, halo_send, halo_recv, core_send, core_rsem, zsend, zrsem, xsend, xrsem, lsend, lrsem, ysend, yrsem, store_sem,
):
    dp, space = lax.axis_index("dp"), lax.axis_index("space")
    yy, core = dp // 2, dp % 2
    zz, xx = space // 4, space % 4
    up, down = (space + 31) % 32, (space + 1) % 32

    loads = [
        pltpu.make_async_copy(lat_hbm, latx.at[pl.ds(2 * COLS, OWN)], load_sem.at[0]),
        pltpu.make_async_copy(cot_hbm, cotx.at[pl.ds(2 * COLS, OWN)], load_sem.at[1]),
        pltpu.make_async_copy(w1_hbm, w1, load_sem.at[2]),
        pltpu.make_async_copy(w2_hbm, w2, load_sem.at[3]),
    ]
    for load in loads:
        load.start()

    peers = [(dp, up), (dp, down), (yy * 2 + 1 - core, space)]
    peers += [(dp, (zz + k) % 8 * 4 + xx) for k in range(1, 8)]
    peers += [(dp, zz * 4 + (xx + k) % 4) for k in (1, 2, 3)]
    peers += [((yy + k) % 8 * 2 + core, space) for k in range(1, 8)]
    barrier = pltpu.get_barrier_semaphore()
    for peer in peers:
        pl.semaphore_signal(barrier, inc=1, device_id=peer, device_id_type=MESH)

    def widen(src, dst, first, last, flip, activate):
        def group(k, _):
            at = pl.ds(pl.multiple_of(k * COLS, COLS), COLS)
            value = src[at, :].astype(F32)
            if activate:
                value = value * jax.nn.sigmoid(value)
                act[at, :] = value.astype(BF)
            one, two, three = column_shifts(value)
            dst[at, :] = jnp.concatenate([three, two, one] if flip else [one, two, three], axis=1)
            return 0
        lax.fori_loop(first, last, group, 0)

    loads[0].wait()
    widen(latx, a3, 2, 10, False, True)
    loads[1].wait()
    widen(cotx, c3, 2, 10, True, False)

    pl.semaphore_wait(barrier, len(peers))
    halos = []
    for n, (src, dst) in enumerate(((lat_hbm, latx), (cot_hbm, cotx))):
        to_up = pltpu.make_async_remote_copy(
            src_ref=src.at[pl.ds(0, 2 * COLS)], dst_ref=dst.at[pl.ds(10 * COLS, 2 * COLS)],
            send_sem=halo_send.at[2 * n], recv_sem=halo_recv.at[2 * n],
            device_id=(dp, up), device_id_type=MESH)
        to_down = pltpu.make_async_remote_copy(
            src_ref=src.at[pl.ds(6 * COLS, 2 * COLS)], dst_ref=dst.at[pl.ds(0, 2 * COLS)],
            send_sem=halo_send.at[2 * n + 1], recv_sem=halo_recv.at[2 * n + 1],
            device_id=(dp, down), device_id_type=MESH)
        halos.append((to_up, to_down))

    @pl.when(space > 0)
    def _():
        for to_up, _d in halos:
            to_up.start()

    @pl.when(space < 31)
    def _():
        for _u, to_down in halos:
            to_down.start()

    shape = (CH, CH)
    row = lax.broadcasted_iota(jnp.int32, shape, 0)
    chan = lax.broadcasted_iota(jnp.int32, shape, 1)
    group = ((row % 8) * 2 + row // 32 % 2) * 4 + row // 8 % 4
    perm[...] = jnp.where(chan == 5 * group + row // 64, 1.0, 0.0).astype(BF)
    lhs_t[...] = dot_nt(perm[...], cotx[2 * COLS : 10 * COLS, :]).astype(BF)
    mid_t[...] = dot_nt(perm[...], act[2 * COLS : 10 * COLS, :]).astype(BF)

    loads[2].wait()

    def conv_one(runs):
        def rows(i):
            parts = [a3[(first + i) * COLS : (first + count + i) * COLS, :] for first, count in runs]
            return parts[0] if len(parts) == 1 else jnp.concatenate(parts, axis=0)

        total = dot(rows(0), w1[0])
        total += dot(rows(1), w1[1])
        total += dot(rows(2), w1[2])
        at = 0
        for first, count in runs:
            acc[first * COLS : (first + count) * COLS, :] = total[at : at + count * COLS]
            at += count * COLS

        def finish(k, _):
            at = pl.ds(pl.multiple_of(k * COLS, COLS), COLS)
            hidden = acc[at, :].astype(BF).astype(F32)
            sig = jax.nn.sigmoid(hidden)
            slope[at, :] = sig * (1.0 + hidden * (1.0 - sig))
            h3[at, :] = jnp.concatenate(column_shifts(hidden * sig), axis=1)
            return 0

        for first, count in runs:
            lax.fori_loop(first, first + count, finish, 0)

    conv_one([(2, 6)])

    @pl.when(space == 0)
    def _():
        latx[0 : 2 * COLS, :] = jnp.zeros((2 * COLS, CH), BF)
        cotx[0 : 2 * COLS, :] = jnp.zeros((2 * COLS, CH), BF)

    @pl.when(space == 31)
    def _():
        latx[10 * COLS :, :] = jnp.zeros((2 * COLS, CH), BF)
        cotx[10 * COLS :, :] = jnp.zeros((2 * COLS, CH), BF)

    @pl.when(space < 31)
    def _():
        for to_up, _d in halos:
            to_up.wait_recv()

    @pl.when(space > 0)
    def _():
        for _u, to_down in halos:
            to_down.wait_recv()

    for first in (0, 10):
        widen(latx, a3, first, first + 2, False, True)
        widen(cotx, c3, first, first + 2, True, False)
    conv_one([(0, 2), (8, 2)])

    def clear_outside(ref):
        @pl.when(space == 0)
        def _():
            ref[0:COLS, :] = jnp.zeros((COLS, 3 * CH), BF)

        @pl.when(space == 31)
        def _():
            ref[9 * COLS :, :] = jnp.zeros((COLS, 3 * CH), BF)

    clear_outside(h3)

    other = (yy * 2 + 1 - core, space)

    def core_copy(n, r):
        return pltpu.make_async_remote_copy(
            src_ref=grid.at[n, pl.ds(8 * r, 8), pl.ds(4 * (1 - core), 4)],
            dst_ref=core_recv.at[n, pl.ds(8 * r, 8)],
            send_sem=core_send.at[n, r], recv_sem=core_rsem.at[n, r],
            device_id=other, device_id_type=MESH)

    def pack_terms(n):
        lane = lax.broadcasted_iota(jnp.int32, (64, LANES), 1)
        for r in range(5):
            for u in range(8):
                value = None
                for tap, col, size, put in unit_pieces(u):
                    base = min(col // 128 * 128, 1024 - LANES)
                    width = -(-max(col - base + size, LANES) // 128) * 128
                    shift = (put - (col - base)) % width
                    piece = terms[tap, 64 * r : 64 * r + 64, base : base + width]
                    if shift:
                        piece = pltpu.roll(piece, shift, 1)
                    piece = piece[:, :LANES]
                    value = piece if value is None else jnp.where(lane < put, value, piece)
                grid[n, 8 * r + u] = value.reshape(8, 8, LANES).astype(BF)
            core_copy(n, r).start()

    def core_sum(n):
        for r in range(5):
            core_copy(n, r).wait_recv()
        for k in range(4):
            part = grid[n, :, 4 * core + k].astype(F32) + core_recv[n, :, k].astype(F32)
            sums[n, k] = part.reshape(2, 4, 5, 8, LANES).astype(BF)

    def xcopy(n, part, way):
        step = 1 if way == 0 else 3
        target = (xx + (2 * step if part == 1 else step)) % 4
        lo = 2 * way if part < 3 else 2 - 2 * way
        return pltpu.make_async_remote_copy(
            src_ref=sums.at[n, pl.ds(lo, 2), :, target],
            dst_ref=xrecv.at[n, way, min(part, 2) - 1, pl.ds(lo, 2)],
            send_sem=xsend.at[n, way, part - 1], recv_sem=xrsem.at[n, way, part - 1],
            device_id=(dp, zz * 4 + (xx + step) % 4), device_id_type=MESH)

    def xstart(n):
        for part in (1, 3):
            for way in range(2):
                xcopy(n, part, way).start()

    def xstep(n):
        for way in range(2):
            xcopy(n, 1, way).wait_recv()
            lo = 2 * way
            ref = sums.at[n, pl.ds(lo, 2), :, (xx + (1 if way == 0 else 3)) % 4]
            ref[...] = (ref[...].astype(F32) + xrecv[n, way, 0, lo : lo + 2].astype(F32)).astype(BF)
            xcopy(n, 2, way).start()

    steps = (1, 7)

    def zblock(target, way, half):
        lo, size = (2 * way, 2) if half else (0, 4)
        return sums.at[1, target // 2, target % 2, pl.ds(lo, size)]

    def zcopy(step, way):
        target = (zz + steps[way] * (5 - step)) % 8
        lo, size = (2 * way, 2) if step == 1 else (0, 4)
        return pltpu.make_async_remote_copy(
            src_ref=zblock(target, way, step == 1), dst_ref=zrecv.at[way, step - 1, pl.ds(lo, size)],
            send_sem=zsend.at[way, step - 1], recv_sem=zrsem.at[way, step - 1],
            device_id=(dp, (zz + steps[way]) % 8 * 4 + xx), device_id_type=MESH)

    def zstep(step):
        for way in range(2):
            if step >= 2:
                zcopy(step - 1, way).wait_recv()
                ref = zblock((zz + steps[way] * (5 - step)) % 8, way, step == 2)
                lo, size = (2 * way, 2) if step == 2 else (0, 4)
                ref[...] = (ref[...].astype(F32) + zrecv[way, step - 2, lo : lo + size].astype(F32)).astype(BF)
            zcopy(step, way).start()

    def x_direct(d):
        to = (xx + d) % 4
        return pltpu.make_async_remote_copy(
            src_ref=sums.at[1, zz // 2, zz % 2, to], dst_ref=late.at[1, d - 1],
            send_sem=lsend.at[1, d - 1], recv_sem=lrsem.at[1, d - 1],
            device_id=(dp, zz * 4 + to), device_id_type=MESH)

    def zfinal():
        for way in range(2):
            zcopy(4, way).wait_recv()
        ref = sums.at[1, zz // 2, zz % 2]
        ref[...] = (ref[...].astype(F32) + zrecv[0, 3].astype(F32) + zrecv[1, 3].astype(F32)).astype(BF)
        for d in (2, 1, 3):
            x_direct(d).start()

    def z_direct(n, d):
        to = (zz + d) % 8
        return pltpu.make_async_remote_copy(
            src_ref=sums.at[n, to // 2, to % 2, xx], dst_ref=late.at[n, d - 1],
            send_sem=lsend.at[n, d - 1], recv_sem=lrsem.at[n, d - 1],
            device_id=(dp, to * 4 + xx), device_id_type=MESH)

    def y_direct(n, d):
        to = (yy + d) % 8
        return pltpu.make_async_remote_copy(
            src_ref=mids.at[n, to], dst_ref=midr.at[n, d - 1],
            send_sem=lsend.at[n, d - 1], recv_sem=lrsem.at[n, d - 1],
            device_id=(to * 2 + core, space), device_id_type=MESH)

    def xfinal(n):
        for way in range(2):
            for part in (2, 3):
                xcopy(n, part, way).wait_recv()

        @pl.when(core == 0)
        def _():
            ref = sums.at[n, :, :, xx]
            ref[...] = (ref[...].astype(F32) + xrecv[n, 0, 1].astype(F32) + xrecv[n, 1, 1].astype(F32)).astype(BF)
            for d in FAR_FIRST:
                z_direct(n, d).start()

        @pl.when(core == 1)
        def _():
            total = sums[n, :, :, xx].astype(F32) + xrecv[n, 0, 1].astype(F32) + xrecv[n, 1, 1].astype(F32)
            flat = total.reshape(40 * 8, LANES)
            for k in range(3):
                sc[k] = flat[:, 128 * k : 128 * k + 128]
            for to in range(8):
                for k in range(3):
                    mids[n, to, :, 128 * k : 128 * k + 128] = sc[k, pl.ds(to, 40, stride=8), :].astype(BF)
            for d in FAR_FIRST:
                y_direct(n, d).start()

    def last_copy(n, d, over_y):
        if over_y:
            to = (yy + d) % 8
            device = (to * 2 + core, space)
        else:
            to = (zz + d) % 8
            device = (dp, to * 4 + xx)
        return pltpu.make_async_remote_copy(
            src_ref=ys.at[n, to], dst_ref=yr.at[n, d - 1],
            send_sem=ysend.at[n, d - 1], recv_sem=yrsem.at[n, d - 1],
            device_id=device, device_id_type=MESH)

    def late_finish(n):
        total = sums[n, zz // 2, zz % 2, xx].astype(F32)
        for d in range(1, 4 if n else 8):
            (x_direct(d) if n else z_direct(n, d)).wait_recv()
            total += late[n, d - 1].astype(F32)
        flat = total.reshape(5 * 8, LANES)
        for k in range(3):
            sc[k, 0:40] = flat[:, 128 * k : 128 * k + 128]
        for to in range(8):
            for k in range(3):
                ys[n, to, 0:5, 128 * k : 128 * k + 128] = sc[k, pl.ds(to, 5, stride=8), :].astype(BF)
        for d in FAR_FIRST:
            last_copy(n, d, True).start()

    def y_finish(n):
        total = mids[n, yy].astype(F32)
        for d in range(1, 8):
            y_direct(n, d).wait_recv()
            total += midr[n, d - 1].astype(F32)
        for k in range(3):
            sc[k, 0:40] = total[:, 128 * k : 128 * k + 128]
        for to in range(8):
            for k in range(3):
                ys[n, to, 0:5, 128 * k : 128 * k + 128] = sc[k, 5 * to : 5 * to + 5, :].astype(BF)
        for d in FAR_FIRST:
            last_copy(n, d, False).start()

    def last(n, ref):
        def total_over(over_y):
            total = ys[n, yy if over_y else zz].astype(F32)
            for d in range(1, 8):
                last_copy(n, d, over_y).wait_recv()
                total += yr[n, d - 1].astype(F32)
            ref[...] = total

        @pl.when(core == 0)
        def _():
            total_over(True)

        @pl.when(core == 1)
        def _():
            total_over(False)

    def by_core(zero, one):
        pl.when(core == 0)(zero)
        pl.when(core == 1)(one)

    def middle(n):
        @pl.when(core == 0)
        def _():
            late_finish(n)

        @pl.when(core == 1)
        def _():
            y_finish(n)

    ys[...] = jnp.zeros(ys.shape, BF)
    for i in range(3):
        terms[i, :, 3 * CH :] = jnp.zeros((CH, 64), F32)

    for i in range(3):
        terms[i, :, : 3 * CH] = dot(lhs_t[...], h3[i * COLS : i * COLS + OWN, :])
    pack_terms(1)

    loads[3].wait()
    def conv_back(runs):
        def rows(i):
            parts = [c3[(first + i) * COLS : (first + count + i) * COLS, :] for first, count in runs]
            return parts[0] if len(parts) == 1 else jnp.concatenate(parts, axis=0)

        total = dot(rows(2), w2[0])
        total += dot(rows(1), w2[1])
        total += dot(rows(0), w2[2])
        at = 0
        for first, count in runs:
            acc[first * COLS : (first + count) * COLS, :] = total[at : at + count * COLS]
            at += count * COLS

        def finish(k, _):
            at = pl.ds(pl.multiple_of(k * COLS, COLS), COLS)
            before, here, after = column_shifts(acc[at, :] * slope[at, :])
            hg3[at, :] = jnp.concatenate([after, here, before], axis=1)
            return 0

        for first, count in runs:
            lax.fori_loop(first, first + count, finish, 0)

    conv_back([(1, 8)])

    core_sum(1)
    by_core(lambda: zstep(1), lambda: xstart(1))

    for i in range(3):
        if i != 1:
            lhs_t[...] = dot_nt(perm[...], act[(i + 1) * COLS : (i + 1) * COLS + OWN, :]).astype(BF)
        left = mid_t if i == 1 else lhs_t
        terms[i, :, : 3 * CH] = dot(left[...], hg3[COLS : COLS + OWN, :])
    pack_terms(0)
    by_core(lambda: zstep(2), lambda: xstep(1))

    for i in range(3):
        w2t[i] = jnp.concatenate([w2[i, CH * j : CH * j + CH, :] for j in range(3)], axis=1)
        w1t[i] = jnp.concatenate([w1[i, CH * j : CH * j + CH, :] for j in range(3)], axis=1)
    core_sum(0)
    xstart(0)

    total = dot_nt(h3[0:OWN, :], w2t[0])
    total += dot_nt(h3[COLS : COLS + OWN, :], w2t[1])
    total += dot_nt(h3[2 * COLS : 2 * COLS + OWN, :], w2t[2])
    outv[...] = total.astype(BF)
    store_out = pltpu.make_async_copy(outv, out_hbm, store_sem.at[0])
    store_out.start()
    by_core(lambda: zstep(3), lambda: xfinal(1))
    xstep(0)
    conv_back([(0, 1), (9, 1)])
    pl.when(core == 0)(lambda: zstep(4))
    clear_outside(hg3)

    total = dot_nt(hg3[2 * COLS : 2 * COLS + OWN, :], w1t[0])
    total += dot_nt(hg3[COLS : COLS + OWN, :], w1t[1])
    total += dot_nt(hg3[0:OWN, :], w1t[2])
    acc[0:OWN, :] = total

    def finish_latent(k, _):
        at = pl.ds(pl.multiple_of(k * COLS, COLS), COLS)
        value = latx[pl.ds(pl.multiple_of((k + 2) * COLS, COLS), COLS), :].astype(F32)
        sig = jax.nn.sigmoid(value)
        lgv[at, :] = (acc[at, :] * (sig * (1.0 + value * (1.0 - sig)))).astype(BF)
        return 0

    lax.fori_loop(0, 8, finish_latent, 0)
    store_lg = pltpu.make_async_copy(lgv, lg_hbm, store_sem.at[1])
    store_lg.start()
    xfinal(0)
    by_core(zfinal, lambda: y_finish(1))

    @pl.when(space > 0)
    def _():
        for to_up, _d in halos:
            to_up.wait_send()

    @pl.when(space < 31)
    def _():
        for _u, to_down in halos:
            to_down.wait_send()

    for n in range(2):
        for r in range(5):
            core_copy(n, r).wait_send()

    def sent_x(n):
        for way in range(2):
            for part in (1, 2, 3):
                xcopy(n, part, way).wait_send()

    def sent_z():
        for way in range(2):
            for step in range(1, 5):
                zcopy(step, way).wait_send()

    sent_x(0)
    by_core(sent_z, lambda: sent_x(1))
    store_out.wait()
    store_lg.wait()
    pl.when(core == 0)(lambda: late_finish(1))
    middle(0)

    def sent(copy):
        for n in range(2):
            for d in range(1, 8):
                copy(n, d).wait_send()

    @pl.when(core == 0)
    def _():
        for d in range(1, 8):
            z_direct(0, d).wait_send()
        for d in range(1, 4):
            x_direct(d).wait_send()

    @pl.when(core == 1)
    def _():
        sent(y_direct)

    last(1, g2_ref)
    last(0, g1_ref)

    @pl.when(core == 0)
    def _():
        sent(lambda n, d: last_copy(n, d, True))

    @pl.when(core == 1)
    def _():
        sent(lambda n, d: last_copy(n, d, False))


def finish_kernel(out_hbm, lg_hbm, g1_hbm, g2_hbm, out_res, lg_res, f1_res, f2_res, buf, share, f1, f2, sem_in, sem_out):
    shares = [
        pltpu.make_async_copy(g1_hbm, share.at[0], sem_in.at[2, 0]),
        pltpu.make_async_copy(g2_hbm, share.at[1], sem_in.at[2, 1]),
    ]
    flats = [
        pltpu.make_async_copy(f1, f1_res, sem_out.at[2, 0]),
        pltpu.make_async_copy(f2, f2_res, sem_out.at[2, 1]),
    ]
    for copy in shares:
        copy.start()
    takes, puts = [], []
    for n, (src, dst) in enumerate(((out_hbm, out_res), (lg_hbm, lg_res))):
        for k in range(2):
            at = pl.ds(k * OWN // 2, OWN // 2)
            takes.append(pltpu.make_async_copy(src.at[at], buf.at[n, at], sem_in.at[n, k]))
            puts.append(pltpu.make_async_copy(buf.at[n, at], dst.at[at], sem_out.at[n, k]))
    for take in takes:
        take.start()
    for copy in shares:
        copy.wait()
    lane = lax.broadcasted_iota(jnp.int32, (1, 128), 1)
    for n, dst in enumerate((f1, f2)):
        src = share.at[n]
        for k in range(15):
            start, end = 128 * k, min(128 * k + 128, 5 * UNIT)
            size, value, at = end - start, None, start
            while at < end:
                row, col = divmod(at, UNIT)
                base = min(col // 128 * 128, LANES - 256)
                piece = src[row : row + 1, base : base + 256]
                shift = (at - start - (col - base)) % 256
                if shift:
                    piece = pltpu.roll(piece, shift, 1)
                piece = piece[:, :128]
                value = piece if value is None else jnp.where(lane < at - start, value, piece)
                at += min(UNIT - col, end - at)
            dst[pl.ds(start, size)] = value[0, :size]
        flats[n].start()
    for take, put in zip(takes, puts):
        take.wait()
        put.start()
    for copy in puts + flats:
        copy.wait()


def local(latent, first_weight, second_weight, cotangent):
    def taps(weight):
        return jnp.transpose(weight, (1, 2, 0, 3)).reshape(3, 3 * CH, CH)

    any_spec = pl.BlockSpec(memory_space=pl.ANY)
    vmem_spec = pl.BlockSpec(memory_space=pltpu.VMEM)
    dma = pltpu.SemaphoreType.DMA
    out, latent_grad, first, second = pl.pallas_call(
        kernel,
        out_shape=(
            jax.ShapeDtypeStruct((OWN, CH), BF),
            jax.ShapeDtypeStruct((OWN, CH), BF),
            jax.ShapeDtypeStruct((8, LANES), F32),
            jax.ShapeDtypeStruct((8, LANES), F32),
        ),
        in_specs=[any_spec] * 4,
        out_specs=(any_spec, any_spec, vmem_spec, vmem_spec),
        scratch_shapes=[
            pltpu.VMEM((EXT, CH), BF),
            pltpu.VMEM((EXT, CH), BF),
            pltpu.VMEM((EXT, CH), BF),
            pltpu.VMEM((EXT, 3 * CH), BF),
            pltpu.VMEM((EXT, 3 * CH), BF),
            pltpu.VMEM((3, 3 * CH, CH), BF),
            pltpu.VMEM((3, 3 * CH, CH), BF),
            pltpu.VMEM((3, CH, 3 * CH), BF),
            pltpu.VMEM((3, CH, 3 * CH), BF),
            pltpu.VMEM((MID, CH), F32),
            pltpu.VMEM((MID, CH), F32),
            pltpu.VMEM((MID, 3 * CH), BF),
            pltpu.VMEM((MID, 3 * CH), BF),
            pltpu.VMEM((3, CH, 1024), F32),
            pltpu.VMEM((CH, CH), BF),
            pltpu.VMEM((CH, OWN), BF),
            pltpu.VMEM((CH, OWN), BF),
            pltpu.VMEM((2, UNITS, 8, 8, LANES), BF),
            pltpu.VMEM((2, UNITS, 4, 8, LANES), BF),
            pltpu.VMEM((2, 4, 2, 4, 5, 8, LANES), BF),
            pltpu.VMEM((2, 4, 4, 5, 8, LANES), BF),
            pltpu.VMEM((2, 2, 2, 4, 2, 5, 8, LANES), BF),
            pltpu.VMEM((2, 7, 5, 8, LANES), BF),
            pltpu.VMEM((2, 8, 40, LANES), BF),
            pltpu.VMEM((2, 7, 40, LANES), BF),
            pltpu.VMEM((3, 320, 128), F32),
            pltpu.VMEM((2, 8, 8, LANES), BF),
            pltpu.VMEM((2, 7, 8, LANES), BF),
            pltpu.VMEM((OWN, CH), BF),
            pltpu.VMEM((OWN, CH), BF),
            dma((4,)),
            dma((4,)),
            dma((4,)),
            dma((2, 5)),
            dma((2, 5)),
            dma((2, 4)),
            dma((2, 4)),
            dma((2, 2, 3)),
            dma((2, 2, 3)),
            dma((2, 7)),
            dma((2, 7)),
            dma((2, 7)),
            dma((2, 7)),
            dma((2,)),
        ],
        compiler_params=pltpu.CompilerParams(
            collective_id=0, has_side_effects=True, vmem_limit_bytes=60 * 1024 * 1024
        ),
        name="conv_pair",
    )(
        latent.reshape(OWN, CH), taps(first_weight), taps(second_weight), cotangent.reshape(OWN, CH)
    )
    out, latent_grad, first, second = pl.pallas_call(
        finish_kernel,
        out_shape=(
            jax.ShapeDtypeStruct((OWN, CH), BF),
            jax.ShapeDtypeStruct((OWN, CH), BF),
            jax.ShapeDtypeStruct((5 * UNIT,), F32),
            jax.ShapeDtypeStruct((5 * UNIT,), F32),
        ),
        in_specs=[any_spec] * 4,
        out_specs=(any_spec,) * 4,
        scratch_shapes=[
            pltpu.VMEM((2, OWN, CH), BF),
            pltpu.VMEM((2, 8, LANES), F32),
            pltpu.VMEM((5 * UNIT,), F32),
            pltpu.VMEM((5 * UNIT,), F32),
            dma((3, 2)),
            dma((3, 2)),
        ],
        name="finish",
    )(out, latent_grad, first, second)
    return (
        out.reshape(1, ROWS, COLS, CH),
        latent_grad.reshape(1, ROWS, COLS, CH),
        first,
        second,
    )


def solution(mesh):
    placed = (P("dp", "space", None, None), P(), P(), P("dp", "space", None, None))
    return jax.shard_map(
        local,
        mesh=mesh,
        in_specs=placed,
        out_specs=(
            P("dp", "space", None, None),
            P("dp", "space", None, None),
            P(("dp", "space")),
            P(("dp", "space")),
        ),
        check_vma=False,
    )
```
